32 devices in a mesh: ffn: 16 (over z, y, core), tok: 2 (over x).
Axes of the slice: x: 2, y: 2, z: 4, core: 2. Of those that a mesh axis runs over, the one named last changes fastest.
Arguments:
- tokens: bfloat16 [16384, 768], P(('ffn', 'tok')), may hold values from -6 to 6
- joint_proj: bfloat16 [768, 2304], replicated, may hold values from -0.21875 to 0.21875
- query_bias: bfloat16 [768], replicated, may hold values from -1.5 to 1.5
- value_bias: bfloat16 [768], replicated, may hold values from -1.5 to 1.5
- out_proj: bfloat16 [768, 768], replicated, may hold values from -1.75 to 1.75
- out_bias: bfloat16 [768], replicated, may hold values from -1.5 to 1.5
- first_gain: float32 [768], replicated, may hold values from 0.5 to 1.5
- first_shift: float32 [768], replicated, may hold values from -1.5 to 1.5
- inner_proj: bfloat16 [768, 3072], P(None, 'ffn'), may hold values from -0.21875 to 0.21875
- inner_bias: bfloat16 [3072], P('ffn'), may hold values from -1.5 to 1.5
- outer_proj: bfloat16 [3072, 768], P('ffn'), may hold values from -0.15625 to 0.15625
- outer_bias: bfloat16 [768], replicated, may hold values from -1.5 to 1.5
- second_gain: float32 [768], replicated, may hold values from 0.5 to 1.5
- second_shift: float32 [768], replicated, may hold values from -1.5 to 1.5
- segment_ids: int32 [16384], P(('ffn', 'tok')), may hold values from 0 to 3, as said below
- cls_positions: int32 [32, 4], P(('ffn', 'tok')), may hold values from 0 to 480, as said below
- widths: int32 [2, 2], replicated, may hold values from 3 to 3072, as said below
- out_grad: bfloat16 [16384, 768], P(('ffn', 'tok')), may hold values from -6 to 6
Outputs:
- output: bfloat16 [16384, 768], P(('ffn', 'tok'))
- cls_states: float32 [32, 4, 768], P(('ffn', 'tok'))
- input_grad: float32 [16384, 768], P(('ffn', 'tok'))
- joint_proj_grad: float32 [768, 2304], replicated
- query_bias_grad: float32 [768], replicated
- value_bias_grad: float32 [768], replicated
- out_proj_grad: float32 [768, 768], replicated
- out_bias_grad: float32 [768], replicated
- first_gain_grad: float32 [768], replicated
- first_shift_grad: float32 [768], replicated
- inner_proj_grad: float32 [768, 3072], P(None, 'ffn')
- inner_bias_grad: float32 [3072], P('ffn')
- outer_proj_grad: float32 [3072, 768], P('ffn')
- outer_bias_grad: float32 [768], replicated
- second_gain_grad: float32 [768], replicated
- second_shift_grad: float32 [768], replicated
The draws below stay inside these ranges and needn't reach their ends.
Inputs may be any that keep to these rules, and one draw needn't show every extreme that they name: `segment_ids`: each row of 512 tokens holds exactly 4 examples numbered 0 to 3 in order, each of one token or more. `cls_positions`: the first position of each example of a row, counted from the row's start, in the order of the examples; the first is 0; the last example's start reaches the most in some row. `widths`: row m: neurons kept (a multiple of 768, at least 768) and heads kept (a multiple of 3, at least 3) of micro-batch m; one micro-batch keeps all 3072 neurons and all 12 heads.
All inputs are finite; a program needn't handle non-finite values.
Results may differ from the reference program's by a relative error of at most 0.014.
The reference program's roundings to bfloat16 on the way count: a program that leaves them out, or rounds other values in their place, can miss the bound.
Values may be sent and summed in bfloat16 or wider, within the bound.
A program may use at most 256 MiB of HBM per device.

```python
import math
import jax
import jax.numpy as jnp
from jax import lax

D = 768
HEADS = 12
DH = 64
FF = 3072
LENGTH = 512
SEGS = 4
MB = 2
TOKENS = 16384
ROWS = 32


def segment_starts(key):
    half_len = LENGTH // SEGS
    half_reach = half_len * 3 // 4
    swings = jax.random.randint(jax.random.fold_in(key, 5), (ROWS, SEGS // 2), -half_reach, half_reach + 1)
    swings = swings.at[0, SEGS // 2 - 1].set(half_reach)
    lengths = jnp.stack([half_len + swings, half_len - swings], axis=-1).reshape(ROWS, SEGS)
    return (jnp.cumsum(lengths, axis=1) - lengths).astype(jnp.int32)


def draw_segment_ids(key, part):
    starts = segment_starts(key)
    positions = jnp.arange(LENGTH, dtype=jnp.int32)
    marks = (positions[None, :, None] >= starts[:, None, 1:]).astype(jnp.int32)
    return jnp.sum(marks, axis=-1).reshape(TOKENS).astype(jnp.int32)


def draw_cls_positions(key, part):
    return segment_starts(key)


def draw_widths(key, part):
    full_batch = jax.random.randint(jax.random.fold_in(key, 21), (), 0, MB)
    quarters = jax.random.randint(jax.random.fold_in(key, 22), (MB, 2), 1, 4)
    batches = jnp.arange(MB, dtype=jnp.int32)
    quarters = jnp.where(batches[:, None] == full_batch, 4, quarters)
    return jnp.stack([quarters[:, 0] * (FF // 4), quarters[:, 1] * (HEADS // 4)], axis=-1).astype(jnp.int32)


def block_levels(stream_key, extent, split, smallest, top_value):
    level, own = 1.0, jax.random.fold_in(stream_key, 6)
    for position, blocks in split:
        steps = jnp.exp(jax.random.uniform(jax.random.fold_in(own, position), (blocks,), jnp.float32, smallest / len(split), top_value / len(split)))
        level = level * jnp.repeat(steps, extent[position] // blocks).reshape([-1 if axis == position else 1 for axis in range(len(extent))])
    return level


def noise(key, dims, deviation, reach, split=(), kind=jnp.bfloat16):
    level = block_levels(key, dims, split, -0.22, 0.18) if split else 1.0
    values = jax.random.normal(key, dims, jnp.float32) * deviation * level
    return jnp.minimum(jnp.maximum(values, -reach), reach).astype(kind)


def setup_inputs(seed: int = 0) -> dict:
    keys = jax.random.split(jax.random.key(seed), 19)
    tokens = noise(keys[0], (TOKENS, D), 1.0, 6.0, ((0, 32),))
    joint_proj = noise(keys[1], (D, 3 * D), D ** -0.5, 0.21875)
    query_bias = noise(keys[2], (D,), 0.3, 1.5)
    value_bias = noise(keys[3], (D,), 0.3, 1.5)
    out_proj = noise(keys[4], (D, D), (D // 64) ** -0.5, 1.75)
    out_bias = noise(keys[5], (D,), 0.3, 1.5)
    first_gain = jnp.clip(1.0 + 0.1 * jax.random.normal(keys[6], (D,), jnp.float32), 0.5, 1.5)
    first_shift = noise(keys[7], (D,), 0.3, 1.5, (), jnp.float32)
    inner_proj = noise(keys[8], (D, FF), D ** -0.5, 0.21875, ((1, 16),))
    inner_bias = noise(keys[9], (FF,), 0.3, 1.5, ((0, 16),))
    outer_proj = noise(keys[10], (FF, D), (FF // 2) ** -0.5, 0.15625, ((0, 16),))
    outer_bias = noise(keys[11], (D,), 0.3, 1.5)
    second_gain = jnp.clip(1.0 + 0.1 * jax.random.normal(keys[12], (D,), jnp.float32), 0.5, 1.5)
    second_shift = noise(keys[13], (D,), 0.3, 1.5, (), jnp.float32)
    segment_ids = draw_segment_ids(jax.random.fold_in(keys[18], 71), 0)
    cls_positions = draw_cls_positions(jax.random.fold_in(keys[18], 71), 0)
    widths = draw_widths(jax.random.fold_in(keys[18], 71), 0)
    out_grad = noise(keys[17], (TOKENS, D), 1.0, 6.0, ((0, 32),))
    return dict(tokens=tokens, joint_proj=joint_proj, query_bias=query_bias, value_bias=value_bias, out_proj=out_proj, out_bias=out_bias, first_gain=first_gain, first_shift=first_shift, inner_proj=inner_proj, inner_bias=inner_bias, outer_proj=outer_proj, outer_bias=outer_bias, second_gain=second_gain, second_shift=second_shift, segment_ids=segment_ids, cls_positions=cls_positions, widths=widths, out_grad=out_grad)


@jax.custom_vjp
def low(v):
    return lax.optimization_barrier(v.astype(jnp.bfloat16)).astype(jnp.float32)

@jax.custom_vjp
def low_back(v):
    return v

def low_keep(v):
    return (low(v), None)

def low_pass(kept, grad):
    return (grad,)

def back_keep(v):
    return (v, None)

def back_low(kept, grad):
    return (low(grad),)
low.defvjp(low_keep, low_pass)
low_back.defvjp(back_keep, back_low)

def layer_norm(inputs, gain_vec, shift_vec):
    row_mean = lax.optimization_barrier(jnp.mean(inputs, axis=-1, keepdims=True))
    centred = inputs - row_mean
    row_scale = lax.rsqrt(lax.optimization_barrier(jnp.mean(centred * centred, axis=-1, keepdims=True)) + 1e-12)
    return centred * row_scale * gain_vec + shift_vec

def layer_block(params, row_block, segments, heads_mask, neurons_mask):
    joint_proj, query_bias, value_bias, out_proj, out_bias, first_gain, first_shift, inner_proj, inner_bias, outer_proj, outer_bias, second_gain, second_shift = params
    highest = lax.Precision.HIGHEST
    seq_rows, seq_len, model_width = row_block.shape
    flat_rows = row_block.reshape(seq_rows * seq_len, model_width)
    zero_bias = jnp.zeros((model_width,), jnp.float32)
    joint_bias = jnp.concatenate([query_bias, zero_bias, value_bias])
    joint_low = low_back(low(jnp.dot(flat_rows, joint_proj, precision=highest) + joint_bias))
    joint_low = joint_low.reshape(seq_rows, seq_len, 3, HEADS, DH)
    queries = joint_low[:, :, 0]
    key_heads = joint_low[:, :, 1]
    value_heads = joint_low[:, :, 2]
    same_doc = (segments[:, :, None] == segments[:, None, :])[:, None]
    raw_scores = jnp.einsum('rqhd,rkhd->rhqk', queries, key_heads, precision=highest) * (1.0 / math.sqrt(DH))
    scores = low_back(jnp.where(same_doc, raw_scores, -1e+30))
    probs = low(jax.nn.softmax(scores, axis=-1))
    context = jnp.einsum('rhqk,rkhd->rqhd', probs, value_heads, precision=highest) * heads_mask[:, None, :, None]
    context = low_back(low(context)).reshape(seq_rows * seq_len, model_width)
    attn_out = low_back(jnp.dot(context, out_proj, precision=highest) + out_bias)
    first_out = layer_norm(flat_rows + attn_out, first_gain, first_shift)
    pre_act = low_back(jnp.dot(low(first_out), inner_proj, precision=highest) + inner_bias)
    gelu_out = jax.nn.gelu(pre_act, approximate=False).reshape(seq_rows, seq_len, -1) * neurons_mask[:, None, :]
    act_low = low(gelu_out.reshape(seq_rows * seq_len, -1))
    ffn_out = low_back(jnp.dot(act_low, outer_proj, precision=highest) + outer_bias)
    second_out = layer_norm(first_out + ffn_out, second_gain, second_shift)
    return second_out.reshape(seq_rows, seq_len, model_width)

def reference(tokens, joint_proj, query_bias, value_bias, out_proj, out_bias, first_gain, first_shift, inner_proj, inner_bias, outer_proj, outer_bias, second_gain, second_shift, segment_ids, cls_positions, widths, out_grad):
    row_group = jnp.arange(ROWS, dtype=jnp.int32) // (ROWS // MB)
    picked = (row_group[:, None] == jnp.arange(MB, dtype=jnp.int32)[None, :]).astype(jnp.int32)
    neurons_kept = lax.optimization_barrier(jnp.sum(picked * widths[None, :, 0], axis=1))
    heads_kept = lax.optimization_barrier(jnp.sum(picked * widths[None, :, 1], axis=1))
    head_on = (jnp.arange(HEADS, dtype=jnp.int32)[None, :] < heads_kept[:, None]).astype(jnp.float32)
    neuron_on = (jnp.arange(FF, dtype=jnp.int32)[None, :] < neurons_kept[:, None]).astype(jnp.float32)
    block_rows = min(ROWS, max(1, 4096 // LENGTH))
    blocks = ROWS // block_rows
    params = tuple((member.astype(jnp.float32) for member in (joint_proj, query_bias, value_bias, out_proj, out_bias, first_gain, first_shift, inner_proj, inner_bias, outer_proj, outer_bias, second_gain, second_shift)))
    saved_layer = jax.checkpoint(layer_block)
    block_items = (segment_ids.reshape(blocks, block_rows, LENGTH), head_on.reshape(blocks, block_rows, HEADS), neuron_on.reshape(blocks, block_rows, FF))

    def forward(weights, source):

        def scan_step(carry_in, block_item):
            row_block, segments, heads_mask, neurons_mask = block_item
            return (carry_in, saved_layer(weights, row_block, segments, heads_mask, neurons_mask))
        unused, result = lax.scan(scan_step, jnp.zeros((), jnp.float32), (source.reshape(blocks, block_rows, LENGTH, D),) + block_items)
        return result.reshape(TOKENS, D)
    result, pullback = jax.vjp(forward, params, tokens.astype(jnp.float32))
    param_grads, input_grad = pullback(out_grad.astype(jnp.float32))
    cls_states = jnp.take_along_axis(result.reshape(ROWS, LENGTH, D), cls_positions[:, :, None], axis=1)
    return (result.astype(jnp.bfloat16), cls_states, input_grad, param_grads[0], param_grads[1], param_grads[2], param_grads[3], param_grads[4], param_grads[5], param_grads[6], param_grads[7], param_grads[8], param_grads[9], param_grads[10], param_grads[11], param_grads[12])
```

```python
import math

import jax
import jax.numpy as jnp
from jax import lax
from jax.sharding import PartitionSpec as P

HEADS = 12
DH = 64
MB = 2


def normalize(inputs, gain_vec, shift_vec):
    row_mean = jnp.mean(inputs, axis=-1, keepdims=True)
    centred = inputs - row_mean
    row_scale = lax.rsqrt(jnp.mean(centred * centred, axis=-1, keepdims=True) + 1e-12)
    normed = centred * row_scale
    return (normed * gain_vec + shift_vec, normed, row_scale)


def normalize_back(incoming, normed, row_scale, gain_vec):
    gain_grad = jnp.sum(incoming * normed, axis=0)
    shift_grad = jnp.sum(incoming, axis=0)
    scaled_grad = incoming * gain_vec
    inputs_grad = row_scale * (
        scaled_grad
        - jnp.mean(scaled_grad, axis=-1, keepdims=True)
        - normed * jnp.mean(scaled_grad * normed, axis=-1, keepdims=True)
    )
    return (inputs_grad, gain_grad, shift_grad)


def gelu_slope(inputs):
    return (
        0.5 * (1.0 + lax.erf(inputs * 0.7071067811865476))
        + inputs * jnp.exp(-0.5 * inputs * inputs) * 0.3989422804014327
    )


def contract_rows(left_side, right_side):
    return lax.dot_general(
        left_side, right_side, (((0,), (0,)), ((), ())), preferred_element_type=jnp.float32
    )


def contract_cols(left_side, right_side):
    return lax.dot_general(
        left_side, right_side, (((1,), (1,)), ((), ())), preferred_element_type=jnp.float32
    )


def on_device(
    tokens,
    joint_proj,
    query_bias,
    value_bias,
    out_proj,
    out_bias,
    first_gain,
    first_shift,
    inner_proj,
    inner_bias,
    outer_proj,
    outer_bias,
    second_gain,
    second_shift,
    segment_ids,
    cls_positions,
    widths,
    out_grad,
):
    tok_rows, model_width = tokens.shape
    seq_rows = cls_positions.shape[0]
    seq_len = tok_rows // seq_rows
    unit_share = inner_proj.shape[1]
    ffn_count = lax.axis_size("ffn")
    tok_count = lax.axis_size("tok")
    ffn_place = lax.axis_index("ffn")
    tok_place = lax.axis_index("tok")
    per_group = seq_rows * ffn_count * tok_count // MB
    batches = jnp.arange(MB, dtype=jnp.int32)
    own_group = (ffn_place * tok_count + tok_place) * seq_rows // per_group
    own_pick = (batches == own_group).astype(jnp.int32)
    heads_kept = jnp.sum(own_pick * widths[:, 1])
    head_on = (jnp.arange(HEADS, dtype=jnp.int32) < heads_kept).astype(jnp.float32)
    factor = 1.0 / math.sqrt(DH)
    zero_bias = jnp.zeros((model_width,), jnp.bfloat16)
    joint_bias = jnp.concatenate([query_bias, zero_bias, value_bias])
    joint_low = (
        jnp.dot(tokens, joint_proj, preferred_element_type=jnp.float32) + joint_bias
    ).astype(jnp.bfloat16)
    joint_low = joint_low.reshape(seq_rows, seq_len, 3, HEADS, DH)
    queries = joint_low[:, :, 0]
    key_heads = joint_low[:, :, 1]
    value_heads = joint_low[:, :, 2]
    segments = segment_ids.reshape(seq_rows, seq_len)
    same_doc = (segments[:, :, None] == segments[:, None, :])[:, None]

    def scores_of(query_rows, key_rows):
        raw_scores = (
            jnp.einsum("rqhd,rkhd->rhqk", query_rows, key_rows, preferred_element_type=jnp.float32)
            * factor
        )
        return jnp.where(same_doc, raw_scores, -1e30)

    scores = scores_of(queries, key_heads)
    row_peak = jnp.max(scores, axis=-1, keepdims=True)
    log_total = row_peak + jnp.log(jnp.sum(jnp.exp(scores - row_peak), axis=-1, keepdims=True))
    probs_low = jnp.exp(scores - log_total).astype(jnp.bfloat16)
    context = (
        jnp.einsum("rhqk,rkhd->rqhd", probs_low, value_heads, preferred_element_type=jnp.float32)
        * head_on[:, None]
    )
    context_low = context.astype(jnp.bfloat16).reshape(tok_rows, model_width)
    attn_out = jnp.dot(context_low, out_proj, preferred_element_type=jnp.float32) + out_bias
    first_out, first_normed, first_scale = normalize(
        tokens.astype(jnp.float32) + attn_out, first_gain, first_shift
    )
    first_low = first_out.astype(jnp.bfloat16)
    unit_total = unit_share * ffn_count
    stacked = lax.all_gather(
        jnp.stack([inner_proj.T, outer_proj]), "ffn", axis=1, tiled=True
    )
    inner_rows, outer_rows = stacked[0], stacked[1]
    inner_bias_all = lax.all_gather(inner_bias, "ffn", axis=0, tiled=True)
    own_kept = jnp.sum(own_pick * widths[:, 0])
    neuron_on = (jnp.arange(unit_total, dtype=jnp.int32) < own_kept).astype(jnp.float32)
    pre_act = contract_cols(first_low, inner_rows) + inner_bias_all
    act_low = (jax.nn.gelu(pre_act, approximate=False) * neuron_on).astype(jnp.bfloat16)
    ffn_out = jnp.dot(act_low, outer_rows, preferred_element_type=jnp.float32) + outer_bias
    second_out, second_normed, second_scale = normalize(
        first_out + ffn_out, second_gain, second_shift
    )
    output = second_out.astype(jnp.bfloat16)
    cls_states = jnp.take_along_axis(
        second_out.reshape(seq_rows, seq_len, model_width), cls_positions[:, :, None], axis=1
    )
    sum_grad, second_gain_grad, second_shift_grad = normalize_back(
        out_grad.astype(jnp.float32), second_normed, second_scale, second_gain
    )
    ffn_grad = sum_grad.astype(jnp.bfloat16)
    outer_bias_grad = jnp.sum(ffn_grad.astype(jnp.float32), axis=0)
    outer_proj_grad = contract_rows(act_low, ffn_grad)
    act_grad = contract_cols(ffn_grad, outer_rows)
    pre_grad = (act_grad * (gelu_slope(pre_act) * neuron_on)).astype(jnp.bfloat16)
    inner_bias_sum = jnp.sum(pre_grad.astype(jnp.float32), axis=0)
    inner_rows_grad = contract_rows(pre_grad, first_low)
    first_back = jnp.dot(pre_grad, inner_rows, preferred_element_type=jnp.float32)
    unit_grads = jnp.stack(
        [inner_rows_grad.astype(jnp.bfloat16), outer_proj_grad.astype(jnp.bfloat16)]
    )
    unit_grads = lax.psum_scatter(unit_grads, "ffn", scatter_dimension=1, tiled=True)
    unit_grads = lax.psum(unit_grads, "tok").astype(jnp.float32)
    inner_proj_grad, outer_proj_grad = unit_grads[0].T, unit_grads[1]
    first_grad = sum_grad + first_back
    attn_sum_grad, first_gain_grad, first_shift_grad = normalize_back(
        first_grad, first_normed, first_scale, first_gain
    )
    attn_grad = attn_sum_grad.astype(jnp.bfloat16)
    out_bias_grad = jnp.sum(attn_grad.astype(jnp.float32), axis=0)
    out_proj_grad = contract_rows(context_low, attn_grad)
    context_grad = (
        contract_cols(attn_grad, out_proj)
        .astype(jnp.bfloat16)
        .reshape(seq_rows, seq_len, HEADS, DH)
    )
    context_grad = context_grad * head_on.astype(jnp.bfloat16)[:, None]
    scores = scores_of(queries, key_heads)
    probs = jnp.exp(scores - log_total)
    probs_again = probs.astype(jnp.bfloat16)
    value_part = jnp.einsum(
        "rhqk,rqhd->rkhd", probs_again, context_grad, preferred_element_type=jnp.float32
    )
    prob_grad = jnp.einsum(
        "rqhd,rkhd->rhqk", context_grad, value_heads, preferred_element_type=jnp.float32
    )
    score_grad = (probs * (prob_grad - jnp.sum(probs * prob_grad, axis=-1, keepdims=True))).astype(
        jnp.bfloat16
    )
    query_part = (
        jnp.einsum("rhqk,rkhd->rqhd", score_grad, key_heads, preferred_element_type=jnp.float32)
        * factor
    )
    key_part = (
        jnp.einsum("rhqk,rqhd->rkhd", score_grad, queries, preferred_element_type=jnp.float32)
        * factor
    )
    joint_grad = (
        jnp.stack([query_part, key_part, value_part], axis=2)
        .astype(jnp.bfloat16)
        .reshape(tok_rows, 3 * model_width)
    )
    joint_bias_grad = jnp.sum(joint_grad.astype(jnp.float32), axis=0)
    query_bias_grad = joint_bias_grad[:model_width]
    value_bias_grad = joint_bias_grad[2 * model_width :]
    joint_proj_grad = contract_rows(tokens, joint_grad)
    input_grad = attn_sum_grad + contract_cols(joint_grad, joint_proj)
    joint_proj_grad, out_proj_grad = lax.psum(
        (joint_proj_grad.astype(jnp.bfloat16), out_proj_grad.astype(jnp.bfloat16)),
        ("ffn", "tok"),
    )
    joint_proj_grad = joint_proj_grad.astype(jnp.float32)
    out_proj_grad = out_proj_grad.astype(jnp.float32)
    small = [
        query_bias_grad,
        value_bias_grad,
        out_bias_grad,
        first_gain_grad,
        first_shift_grad,
        outer_bias_grad,
        second_gain_grad,
        second_shift_grad,
        inner_bias_sum,
    ]
    small = lax.psum(jnp.concatenate(small), ("ffn", "tok"))
    (
        query_bias_grad,
        value_bias_grad,
        out_bias_grad,
        first_gain_grad,
        first_shift_grad,
        outer_bias_grad,
        second_gain_grad,
        second_shift_grad,
    ) = [small[i * model_width : (i + 1) * model_width] for i in range(8)]
    inner_bias_grad = lax.dynamic_slice(
        small, (8 * model_width + ffn_place * unit_share,), (unit_share,)
    )
    return (
        output,
        cls_states,
        input_grad,
        joint_proj_grad,
        query_bias_grad,
        value_bias_grad,
        out_proj_grad,
        out_bias_grad,
        first_gain_grad,
        first_shift_grad,
        inner_proj_grad,
        inner_bias_grad,
        outer_proj_grad,
        outer_bias_grad,
        second_gain_grad,
        second_shift_grad,
    )


def solution(mesh):
    return jax.shard_map(
        on_device,
        mesh=mesh,
        in_specs=(
            P(("ffn", "tok"), None),
            P(),
            P(),
            P(),
            P(),
            P(),
            P(),
            P(),
            P(None, "ffn"),
            P("ffn"),
            P("ffn", None),
            P(),
            P(),
            P(),
            P(("ffn", "tok")),
            P(("ffn", "tok"), None),
            P(),
            P(("ffn", "tok"), None),
        ),
        out_specs=(
            P(("ffn", "tok"), None),
            P(("ffn", "tok"), None, None),
            P(("ffn", "tok"), None),
            P(),
            P(),
            P(),
            P(),
            P(),
            P(),
            P(),
            P(None, "ffn"),
            P("ffn"),
            P("ffn", None),
            P(),
            P(),
            P(),
        ),
        check_vma=False,
    )
```

```python
import math

import jax
import jax.numpy as jnp
from jax import lax
from jax.experimental import pallas as pl
from jax.experimental.pallas import tpu as pltpu
from jax.sharding import PartitionSpec as P

MESH = pl.DeviceIdType.MESH
HEADS = 12
DH = 64
MB = 2
SEGS = 4


def normalize(inputs, gain_vec, shift_vec):
    row_mean = jnp.mean(inputs, axis=-1, keepdims=True)
    centred = inputs - row_mean
    row_scale = lax.rsqrt(jnp.mean(centred * centred, axis=-1, keepdims=True) + 1e-12)
    normed = centred * row_scale
    return (normed * gain_vec + shift_vec, normed, row_scale)


def normalize_back(incoming, normed, row_scale, gain_vec):
    gain_grad = jnp.sum(incoming * normed, axis=0)
    shift_grad = jnp.sum(incoming, axis=0)
    scaled_grad = incoming * gain_vec
    inputs_grad = row_scale * (
        scaled_grad
        - jnp.mean(scaled_grad, axis=-1, keepdims=True)
        - normed * jnp.mean(scaled_grad * normed, axis=-1, keepdims=True)
    )
    return (inputs_grad, gain_grad, shift_grad)


def gelu_slope(inputs):
    return (
        0.5 * (1.0 + lax.erf(inputs * 0.7071067811865476))
        + inputs * jnp.exp(-0.5 * inputs * inputs) * 0.3989422804014327
    )


def contract_rows(left_side, right_side):
    return lax.dot_general(
        left_side, right_side, (((0,), (0,)), ((), ())), preferred_element_type=jnp.float32
    )


def contract_cols(left_side, right_side):
    return lax.dot_general(
        left_side, right_side, (((1,), (1,)), ((), ())), preferred_element_type=jnp.float32
    )


def on_device(
    tokens,
    joint_proj,
    query_bias,
    value_bias,
    out_proj,
    out_bias,
    first_gain,
    first_shift,
    inner_proj,
    inner_bias,
    outer_proj,
    outer_bias,
    second_gain,
    second_shift,
    segment_ids,
    cls_positions,
    widths,
    out_grad,
):
    tok_rows, model_width = tokens.shape
    seq_rows = cls_positions.shape[0]
    seq_len = tok_rows // seq_rows
    unit_share = inner_proj.shape[1]
    ffn_count = lax.axis_size("ffn")
    tok_count = lax.axis_size("tok")
    ffn_place = lax.axis_index("ffn")
    tok_place = lax.axis_index("tok")
    per_group = seq_rows * ffn_count * tok_count // MB
    batches = jnp.arange(MB, dtype=jnp.int32)
    own_group = (ffn_place * tok_count + tok_place) * seq_rows // per_group
    own_pick = (batches == own_group).astype(jnp.int32)
    heads_kept = jnp.sum(own_pick * widths[:, 1])
    head_on = (jnp.arange(HEADS, dtype=jnp.int32) < heads_kept).astype(jnp.float32)
    factor = 1.0 / math.sqrt(DH)
    zero_bias = jnp.zeros((model_width,), jnp.bfloat16)
    joint_bias = jnp.concatenate([query_bias, zero_bias, value_bias])
    joint_low = (
        jnp.dot(tokens, joint_proj, preferred_element_type=jnp.float32) + joint_bias
    ).astype(jnp.bfloat16)
    joint_low = joint_low.reshape(seq_rows, seq_len, 3, HEADS, DH)
    queries = joint_low[:, :, 0]
    key_heads = joint_low[:, :, 1]
    value_heads = joint_low[:, :, 2]
    segments = segment_ids.reshape(seq_rows, seq_len)
    same_doc = (segments[:, :, None] == segments[:, None, :])[:, None]

    def scores_of(query_rows, key_rows):
        raw_scores = (
            jnp.einsum("rqhd,rkhd->rhqk", query_rows, key_rows, preferred_element_type=jnp.float32)
            * factor
        )
        return jnp.where(same_doc, raw_scores, -1e30)

    scores = scores_of(queries, key_heads)
    row_peak = jnp.max(scores, axis=-1, keepdims=True)
    log_total = row_peak + jnp.log(jnp.sum(jnp.exp(scores - row_peak), axis=-1, keepdims=True))
    probs_low = jnp.exp(scores - log_total).astype(jnp.bfloat16)
    context = (
        jnp.einsum("rhqk,rkhd->rqhd", probs_low, value_heads, preferred_element_type=jnp.float32)
        * head_on[:, None]
    )
    context_low = context.astype(jnp.bfloat16).reshape(tok_rows, model_width)
    attn_out = jnp.dot(context_low, out_proj, preferred_element_type=jnp.float32) + out_bias
    first_out, first_normed, first_scale = normalize(
        tokens.astype(jnp.float32) + attn_out, first_gain, first_shift
    )
    first_low = first_out.astype(jnp.bfloat16)
    unit_total = unit_share * ffn_count
    stacked = lax.all_gather(
        jnp.stack([inner_proj.T, outer_proj]), "ffn", axis=1, tiled=True
    )
    inner_rows, outer_rows = stacked[0], stacked[1]
    inner_bias_all = lax.all_gather(inner_bias, "ffn", axis=0, tiled=True)
    own_kept = jnp.sum(own_pick * widths[:, 0])
    neuron_on = (jnp.arange(unit_total, dtype=jnp.int32) < own_kept).astype(jnp.float32)
    pre_act = contract_cols(first_low, inner_rows) + inner_bias_all
    act_low = (jax.nn.gelu(pre_act, approximate=False) * neuron_on).astype(jnp.bfloat16)
    ffn_out = jnp.dot(act_low, outer_rows, preferred_element_type=jnp.float32) + outer_bias
    second_out, second_normed, second_scale = normalize(
        first_out + ffn_out, second_gain, second_shift
    )
    output = second_out.astype(jnp.bfloat16)
    cls_states = jnp.take_along_axis(
        second_out.reshape(seq_rows, seq_len, model_width), cls_positions[:, :, None], axis=1
    )
    sum_grad, second_gain_grad, second_shift_grad = normalize_back(
        out_grad.astype(jnp.float32), second_normed, second_scale, second_gain
    )
    ffn_grad = sum_grad.astype(jnp.bfloat16)
    outer_bias_grad = jnp.sum(ffn_grad.astype(jnp.float32), axis=0)
    outer_proj_grad = contract_rows(act_low, ffn_grad)
    act_grad = contract_cols(ffn_grad, outer_rows)
    pre_grad = (act_grad * (gelu_slope(pre_act) * neuron_on)).astype(jnp.bfloat16)
    inner_bias_sum = jnp.sum(pre_grad.astype(jnp.float32), axis=0)
    inner_rows_grad = contract_rows(pre_grad, first_low)
    first_back = jnp.dot(pre_grad, inner_rows, preferred_element_type=jnp.float32)
    unit_grads = jnp.stack(
        [inner_rows_grad.astype(jnp.bfloat16), outer_proj_grad.astype(jnp.bfloat16)]
    )
    unit_grads = lax.psum_scatter(unit_grads, "ffn", scatter_dimension=1, tiled=True)
    unit_grads = lax.psum(unit_grads, "tok").astype(jnp.float32)
    inner_proj_grad, outer_proj_grad = unit_grads[0].T, unit_grads[1]
    first_grad = sum_grad + first_back
    attn_sum_grad, first_gain_grad, first_shift_grad = normalize_back(
        first_grad, first_normed, first_scale, first_gain
    )
    attn_grad = attn_sum_grad.astype(jnp.bfloat16)
    out_bias_grad = jnp.sum(attn_grad.astype(jnp.float32), axis=0)
    out_proj_grad = contract_rows(context_low, attn_grad)
    context_grad = (
        contract_cols(attn_grad, out_proj)
        .astype(jnp.bfloat16)
        .reshape(seq_rows, seq_len, HEADS, DH)
    )
    context_grad = context_grad * head_on.astype(jnp.bfloat16)[:, None]
    scores = scores_of(queries, key_heads)
    probs = jnp.exp(scores - log_total)
    probs_again = probs.astype(jnp.bfloat16)
    value_part = jnp.einsum(
        "rhqk,rqhd->rkhd", probs_again, context_grad, preferred_element_type=jnp.float32
    )
    prob_grad = jnp.einsum(
        "rqhd,rkhd->rhqk", context_grad, value_heads, preferred_element_type=jnp.float32
    )
    score_grad = (probs * (prob_grad - jnp.sum(probs * prob_grad, axis=-1, keepdims=True))).astype(
        jnp.bfloat16
    )
    query_part = (
        jnp.einsum("rhqk,rkhd->rqhd", score_grad, key_heads, preferred_element_type=jnp.float32)
        * factor
    )
    key_part = (
        jnp.einsum("rhqk,rqhd->rkhd", score_grad, queries, preferred_element_type=jnp.float32)
        * factor
    )
    joint_grad = (
        jnp.stack([query_part, key_part, value_part], axis=2)
        .astype(jnp.bfloat16)
        .reshape(tok_rows, 3 * model_width)
    )
    joint_bias_grad = jnp.sum(joint_grad.astype(jnp.float32), axis=0)
    query_bias_grad = joint_bias_grad[:model_width]
    value_bias_grad = joint_bias_grad[2 * model_width :]
    joint_proj_grad = contract_rows(tokens, joint_grad)
    input_grad = attn_sum_grad + contract_cols(joint_grad, joint_proj)
    joint_proj_grad, out_proj_grad = lax.psum(
        (joint_proj_grad.astype(jnp.bfloat16), out_proj_grad.astype(jnp.bfloat16)),
        ("ffn", "tok"),
    )
    joint_proj_grad = joint_proj_grad.astype(jnp.float32)
    out_proj_grad = out_proj_grad.astype(jnp.float32)
    small = [
        query_bias_grad,
        value_bias_grad,
        out_bias_grad,
        first_gain_grad,
        first_shift_grad,
        outer_bias_grad,
        second_gain_grad,
        second_shift_grad,
        inner_bias_sum,
    ]
    small = lax.psum(jnp.concatenate(small), ("ffn", "tok"))
    (
        query_bias_grad,
        value_bias_grad,
        out_bias_grad,
        first_gain_grad,
        first_shift_grad,
        outer_bias_grad,
        second_gain_grad,
        second_shift_grad,
    ) = [small[i * model_width : (i + 1) * model_width] for i in range(8)]
    inner_bias_grad = lax.dynamic_slice(
        small, (8 * model_width + ffn_place * unit_share,), (unit_share,)
    )
    return (
        output,
        cls_states,
        input_grad,
        joint_proj_grad,
        query_bias_grad,
        value_bias_grad,
        out_proj_grad,
        out_bias_grad,
        first_gain_grad,
        first_shift_grad,
        inner_proj_grad,
        inner_bias_grad,
        outer_proj_grad,
        outer_bias_grad,
        second_gain_grad,
        second_shift_grad,
    )


def x_or1(v):
    return v + 1 - 2 * (v % 2)


def x_or2(v):
    return v + 2 - 4 * ((v // 2) % 2)


def z_peer(place, turn):
    deep = place // 4
    if turn & 1:
        deep = x_or1(deep)
    if turn & 2:
        deep = x_or2(deep)
    return deep * 4 + place % 4


def y_peer(place):
    return (place // 4) * 4 + ((place // 2 + 1) % 2) * 2 + place % 2


def c_peer(place):
    return x_or1(place)


def nt_dot(left_side, right_side):
    return lax.dot_general(
        left_side, right_side, (((1,), (1,)), ((), ())), preferred_element_type=jnp.float32
    )


def tn_dot(left_side, right_side):
    return lax.dot_general(
        left_side, right_side, (((0,), (0,)), ((), ())), preferred_element_type=jnp.float32
    )


def nn_dot(left_side, right_side):
    return lax.dot_general(
        left_side, right_side, (((1,), (0,)), ((), ())), preferred_element_type=jnp.float32
    )


def greet(place, side):
    barrier = pltpu.get_barrier_semaphore()
    peers = [
        (z_peer(place, 1), side),
        (z_peer(place, 2), side),
        (z_peer(place, 3), side),
        (y_peer(place), side),
        (c_peer(place), side),
        (place, 1 - side),
    ]
    for peer in peers:
        pl.semaphore_signal(barrier, inc=1, device_id=peer, device_id_type=MESH)
    pl.semaphore_wait(barrier, 6)


def remote(source, target, send_sem, recv_sem, device):
    return pltpu.make_async_remote_copy(
        src_ref=source,
        dst_ref=target,
        send_sem=send_sem,
        recv_sem=recv_sem,
        device_id=device,
        device_id_type=MESH,
    )


class Spread:
    def __init__(self, own, whole, place, side, rows, sems):
        self.own, self.whole, self.place, self.side, self.rows = own, whole, place, side, rows
        self.up_s, self.up_r, self.dn_s, self.dn_r, self.y_s, self.y_r = sems[:6]
        self.x_s, self.x_r, self.c_s, self.c_r, self.d_s, self.d_r = sems[6:]
        self.third = rows // 3
        self.deep = place // 4

    def span(self, source, offset, count):
        start = pl.multiple_of(source * self.rows + offset, 16)
        return self.whole.at[pl.ds(start, count)]

    def slab(self, source):
        return self.span(source, self.side * self.third, 2 * self.third)

    def edge(self, source, mine=True):
        side = self.side if mine else 1 - self.side
        return self.span(source, side * 2 * self.third, self.third)

    def own_slab(self):
        start = pl.multiple_of(self.side * self.third, 16)
        return self.own.at[pl.ds(start, 2 * self.third)]

    def source_of(self, step, up, cross=False):
        base = y_peer(self.place) if cross else self.place
        if step is None:
            return base
        return base - 4 * (step + 1) if up else base + 4 * (step + 1)

    def has(self, step, up):
        if step is None:
            return None
        return self.deep >= step + 1 if up else self.deep + step + 1 <= 3

    def hop(self, step, up, first=False):
        source = self.place if step == 0 else self.source_of(step - 1, up)
        piece = self.own_slab() if step == 0 else self.slab(source)
        send, recv = (self.up_s, self.up_r) if up else (self.dn_s, self.dn_r)
        device = (self.place + 4 if up else self.place - 4, self.side)
        return remote(piece, self.slab(source), send.at[step], recv.at[step], device)

    def hop_in(self, step, up):
        source = self.source_of(step, up)
        send, recv = (self.up_s, self.up_r) if up else (self.dn_s, self.dn_r)
        return remote(
            self.slab(source), self.slab(source), send.at[step], recv.at[step], (self.place, 1 - self.side)
        )

    def over_y(self, source, own=False):
        index = source // 4
        piece = self.own_slab() if own else self.slab(source)
        return remote(
            piece, self.slab(source), self.y_s.at[index], self.y_r.at[index], (y_peer(self.place), self.side)
        )

    def over_x(self, source, mine=True):
        index = source // 2
        piece = self.edge(source, mine)
        return remote(
            piece, piece, self.x_s.at[index], self.x_r.at[index], (self.place, 1 - self.side)
        )

    def over_c(self, source):
        index = source // 2
        return remote(
            self.slab(source),
            self.slab(source),
            self.c_s.at[index],
            self.c_r.at[index],
            (c_peer(self.place), self.side),
        )

    def over_d(self, source):
        index = source // 2
        piece = self.edge(source, False)
        return remote(piece, piece, self.d_s.at[index], self.d_r.at[index], (c_peer(self.place), self.side))

    def over_own(self):
        index = self.place // 2
        return remote(
            self.own,
            self.span(self.place, 0, self.rows),
            self.c_s.at[index],
            self.c_r.at[index],
            (c_peer(self.place), self.side),
        )

    def start(self):
        @pl.when(self.deep < 3)
        def _():
            self.hop(0, True).start()

        @pl.when(self.deep > 0)
        def _():
            self.hop(0, False).start()

        self.over_y(self.place, own=True).start()
        self.over_own().start()

    def z_event(self, step):
        for up in (True, False):

            @pl.when(self.has(step, up))
            def _(up=up):
                source = self.source_of(step, up)
                self.hop_in(step, up).wait_recv()
                if step < 2:

                    @pl.when(self.deep < 3 if up else self.deep > 0)
                    def _():
                        self.hop(step + 1, up).start()

                self.over_y(source).start()
                self.over_x(source).start()
                self.over_c(source).start()

    def each(self, step, work):
        if step is None:
            work(True)
            return
        for up in (True, False):

            @pl.when(self.has(step, up))
            def _(up=up):
                work(up)

    def y_event(self, step):
        def work(up):
            source = self.source_of(step, up, cross=True)
            self.over_y(source).wait_recv()
            self.over_x(source).start()
            self.over_c(source).start()

        self.each(step, work)

    def x_event(self, step, cross):
        def work(up):
            source = self.source_of(step, up, cross=cross)
            self.over_x(source, False).wait_recv()
            self.over_d(source).start()

        self.each(step, work)

    def finish(self):
        other = c_peer(self.place) % 2
        own = c_peer(self.place)
        for index in range(8):
            source = 2 * index + other

            @pl.when(source != own)
            def _(source=source):
                self.over_c(source).wait_recv()
                self.over_d(source).wait_recv()

            @pl.when(source == own)
            def _(source=source):
                remote(
                    self.own,
                    self.span(source, 0, self.rows),
                    self.c_s.at[index],
                    self.c_r.at[index],
                    (c_peer(self.place), self.side),
                ).wait_recv()

    def drain(self):
        for up in (True, False):
            for step in range(3):
                limit = self.deep < 3 if up else self.deep > 0
                if step > 0:
                    limit = jnp.logical_and(limit, self.has(step - 1, up))

                @pl.when(limit)
                def _(step=step, up=up):
                    self.hop(step, up).wait_send()

        for index in range(4):
            source = 4 * index + self.place % 4
            self.over_y(source).wait_send()
        mine = self.place % 2
        for index in range(8):
            source = 2 * index + mine

            @pl.when(source != self.place)
            def _(source=source):
                self.over_x(source).wait_send()
                self.over_c(source).wait_send()
                self.over_d(source).wait_send()

            @pl.when(source == self.place)
            def _():
                self.over_own().wait_send()


def forward_kernel(
    tokens,
    joint_proj,
    joint_bias,
    out_proj,
    out_bias,
    first_gain,
    first_shift,
    inner_own,
    outer_own,
    inner_bias,
    outer_bias,
    second_gain,
    second_shift,
    seg_down,
    seg_over,
    head_mask,
    unit_mask,
    cls_at,
    out_grad,
    output,
    cls_out,
    inner_out,
    outer_out,
    probs_out,
    joint_out,
    context_out,
    normed_out,
    scale_out,
    act_out,
    slope_out,
    sum_grad_out,
    small_out,
    inner_all,
    outer_all,
    probs,
    joint,
    context,
    mask_bias,
    act,
    slope,
    first_low,
    wide,
    save_sem,
    *sems,
):
    place, side = lax.axis_index("ffn"), lax.axis_index("tok")
    rows_total = tokens.shape[0]
    units = inner_all.shape[0]
    share = inner_own.shape[0]
    width = tokens.shape[1]
    half = rows_total // 2
    greet(place, side)
    inner = Spread(inner_own, inner_all, place, side, share, sems[:12])
    outer = Spread(outer_own, outer_all, place, side, share, sems[12:])
    inner.start()
    outer.start()
    own_rows = pl.ds(pl.multiple_of(place * share, 16), share)
    inner_all[own_rows, :] = inner_own[...]
    outer_all[own_rows, :] = outer_own[...]
    saves = []

    def save(source, target, index):
        pltpu.make_async_copy(source, target, save_sem.at[index]).start()
        saves.append((source, target, index))

    mask_bias[...] = jnp.where(seg_down[...] == seg_over[...], 0.0, -1e30)

    def joint_step(j, carry):
        cols = pl.ds(pl.multiple_of(j * 256, 256), 256)
        joint[:, cols] = (nn_dot(tokens[...], joint_proj[:, cols]) + joint_bias[:, cols]).astype(
            jnp.bfloat16
        )
        return carry

    lax.fori_loop(0, 3 * width // 256, joint_step, 0)
    save(joint, joint_out, 0)
    events = [
        lambda: inner.z_event(0),
        lambda: outer.z_event(0),
        lambda: inner.y_event(None),
        lambda: inner.z_event(1),
        lambda: outer.y_event(None),
        lambda: inner.y_event(0),
        lambda: outer.z_event(1),
        lambda: inner.x_event(0, False),
        lambda: inner.x_event(None, True),
        lambda: outer.y_event(0),
        lambda: inner.z_event(2),
        lambda: outer.x_event(0, False),
        lambda: outer.x_event(None, True),
        lambda: inner.y_event(1),
        lambda: outer.z_event(2),
        lambda: inner.x_event(1, False),
        lambda: inner.x_event(0, True),
        lambda: outer.y_event(1),
        lambda: inner.y_event(2),
        lambda: outer.x_event(1, False),
        lambda: outer.x_event(0, True),
        lambda: inner.x_event(2, False),
        lambda: inner.x_event(1, True),
        lambda: outer.y_event(2),
        lambda: inner.x_event(2, True),
        lambda: outer.x_event(2, False),
        lambda: outer.x_event(1, True),
        lambda: outer.x_event(2, True),
    ]
    events[0]()
    slots = {0: events[1:4], 1: events[4:6], 2: events[6:10], 3: events[10:14], 4: events[14:18], 5: events[18:22]}
    first_half = (lax.broadcasted_iota(jnp.int32, (1, 128), 1) < DH).astype(jnp.bfloat16)
    halves = (first_half, 1 - first_half)
    factor = 1.4426950408889634 / math.sqrt(DH)
    pairs = HEADS // 2

    def pair_step(p, carry):
        cols = [pl.ds(pl.multiple_of(s * width + p * 128, 128), 128) for s in range(3)]
        out_cols = pl.ds(pl.multiple_of(p * 128, 128), 128)
        keys, values = joint[:, cols[1]], joint[:, cols[2]]
        for b in range(2):
            lanes = slice(b * half, (b + 1) * half)
            queries = joint[lanes, cols[0]]
            total = None
            for a in range(2):
                scores = nt_dot(keys * halves[a], queries) * factor + mask_bias[:, lanes]
                weights = jnp.exp2(scores - jnp.max(scores, axis=0, keepdims=True))
                weights = weights * (1.0 / jnp.sum(weights, axis=0, keepdims=True))
                low = weights.astype(jnp.bfloat16)
                probs[2 * p + a, :, lanes] = low
                part = tn_dot(low, values * halves[a])
                total = part if total is None else total + part
            context[lanes, out_cols] = (total * head_mask[:, out_cols]).astype(jnp.bfloat16)
        pltpu.make_async_copy(
            probs.at[pl.ds(2 * p, 2)], probs_out.at[pl.ds(2 * p, 2)], save_sem.at[6 + p]
        ).start()
        for slot, todo in slots.items():

            @pl.when(p == slot)
            def _(todo=todo):
                for event in todo:
                    event()

        return carry

    lax.fori_loop(0, pairs, pair_step, 0)
    save(context, context_out, 1)
    for j in range(width // 256):
        cols = slice(j * 256, (j + 1) * 256)
        wide[:, cols] = nn_dot(context[...], out_proj[:, cols])

    def first_norm(i, carry):
        rows = pl.ds(pl.multiple_of(i * 128, 128), 128)
        total = tokens[rows, :].astype(jnp.float32) + (wide[rows, :] + out_bias[...])
        centred = total - jnp.mean(total, axis=-1, keepdims=True)
        scale = lax.rsqrt(jnp.mean(centred * centred, axis=-1, keepdims=True) + 1e-12)
        normed = centred * scale
        normed_out[rows, :] = normed
        scale_out[rows, :] = scale
        first_low[rows, :] = (normed * first_gain[...] + first_shift[...]).astype(jnp.bfloat16)
        return carry

    lax.fori_loop(0, rows_total // 128, first_norm, 0)
    for event in events[22:25]:
        event()
    inner.finish()
    save(inner_all, inner_out, 2)
    unit_slots = {0: events[25:26], 3: events[26:27], 6: events[27:]}

    def unit_step(j, carry):
        cols = pl.ds(pl.multiple_of(j * 256, 256), 256)
        for b in range(2):
            rows = slice(b * half, (b + 1) * half)
            pre = nt_dot(first_low[rows, :], inner_all[cols, :]) + inner_bias[:, cols]
            gate = 0.5 + 0.5 * lax.erf(pre * 0.7071067811865476)
            on = unit_mask[:, cols]
            act[rows, cols] = (pre * gate * on).astype(jnp.bfloat16)
            slope[rows, cols] = (
                (gate + pre * jnp.exp(-0.5 * pre * pre) * 0.3989422804014327) * on
            ).astype(jnp.bfloat16)
        for slot, todo in unit_slots.items():

            @pl.when(j == slot)
            def _(todo=todo):
                for event in todo:
                    event()

        return carry

    lax.fori_loop(0, units // 256, unit_step, 0)
    save(act, act_out, 3)
    save(slope, slope_out, 4)
    outer.finish()
    save(outer_all, outer_out, 5)
    for j in range(width // 256):
        cols = slice(j * 256, (j + 1) * 256)
        wide[:, cols] = nn_dot(act[...], outer_all[:, cols])
    small_out[...] = jnp.zeros_like(small_out)

    def second_norm(i, carry):
        rows = pl.ds(pl.multiple_of(i * 128, 128), 128)
        first = normed_out[rows, :] * first_gain[...] + first_shift[...]
        total = first + (wide[rows, :] + outer_bias[...])
        centred = total - jnp.mean(total, axis=-1, keepdims=True)
        scale = lax.rsqrt(jnp.mean(centred * centred, axis=-1, keepdims=True) + 1e-12)
        normed = centred * scale
        second = normed * second_gain[...] + second_shift[...]
        wide[rows, :] = second
        output[rows, :] = second.astype(jnp.bfloat16)
        grad = out_grad[rows, :].astype(jnp.float32)
        scaled = grad * second_gain[...]
        back = scale * (
            scaled
            - jnp.mean(scaled, axis=-1, keepdims=True)
            - normed * jnp.mean(scaled * normed, axis=-1, keepdims=True)
        )
        sum_grad_out[rows, :] = back
        low = back.astype(jnp.bfloat16).astype(jnp.float32)
        small_out[0:1, :] += jnp.sum(grad * normed, axis=0, keepdims=True)
        small_out[1:2, :] += jnp.sum(grad, axis=0, keepdims=True)
        small_out[2:3, :] += jnp.sum(low, axis=0, keepdims=True)
        return carry

    lax.fori_loop(0, rows_total // 128, second_norm, 0)
    for j in range(SEGS):
        cls_out[j : j + 1, :] = wide[pl.ds(cls_at[0, j], 1), :]
    inner.drain()
    outer.drain()
    for source, target, index in saves:
        pltpu.make_async_copy(source, target, save_sem.at[index]).wait()
    for p in range(pairs):
        pltpu.make_async_copy(
            probs.at[pl.ds(2 * p, 2)], probs_out.at[pl.ds(2 * p, 2)], save_sem.at[6 + p]
        ).wait()


def run_forward(args, share, units, rows_total, width):
    sems = []
    for unused in range(2):
        for count in (3, 3, 3, 3, 4, 4, 8, 8, 8, 8, 8, 8):
            sems.append(pltpu.SemaphoreType.DMA((count,)))
    bf, fp = jnp.bfloat16, jnp.float32
    shape = jax.ShapeDtypeStruct
    vmem = pl.BlockSpec(memory_space=pltpu.VMEM)
    anywhere = pl.BlockSpec(memory_space=pl.ANY)
    in_specs = [vmem] * 17 + [pl.BlockSpec(memory_space=pltpu.SMEM), vmem]
    return pl.pallas_call(
        forward_kernel,
        out_shape=(
            shape((rows_total, width), bf),
            shape((SEGS, width), fp),
            shape((units, width), bf),
            shape((units, width), bf),
            shape((HEADS, rows_total, rows_total), bf),
            shape((rows_total, 3 * width), bf),
            shape((rows_total, width), bf),
            shape((rows_total, width), fp),
            shape((rows_total, 1), fp),
            shape((rows_total, units), bf),
            shape((rows_total, units), bf),
            shape((rows_total, width), fp),
            shape((16, width), fp),
        ),
        in_specs=in_specs,
        out_specs=(
            vmem, vmem, anywhere, anywhere, anywhere, anywhere, anywhere, vmem, vmem, anywhere, anywhere, vmem, vmem,
        ),
        scratch_shapes=[
            pltpu.VMEM((units, width), bf),
            pltpu.VMEM((units, width), bf),
            pltpu.VMEM((HEADS, rows_total, rows_total), bf),
            pltpu.VMEM((rows_total, 3 * width), bf),
            pltpu.VMEM((rows_total, width), bf),
            pltpu.VMEM((rows_total, rows_total), fp),
            pltpu.VMEM((rows_total, units), bf),
            pltpu.VMEM((rows_total, units), bf),
            pltpu.VMEM((rows_total, width), bf),
            pltpu.VMEM((rows_total, width), fp),
            pltpu.SemaphoreType.DMA((6 + HEADS // 2,)),
        ]
        + sems,
        compiler_params=pltpu.CompilerParams(
            collective_id=0, has_side_effects=True, vmem_limit_bytes=64 * 1024 * 1024 - 65536
        ),
        name="forward",
    )(*args)


def on_device_fast(
    tokens,
    joint_proj,
    query_bias,
    value_bias,
    out_proj,
    out_bias,
    first_gain,
    first_shift,
    inner_proj,
    inner_bias,
    outer_proj,
    outer_bias,
    second_gain,
    second_shift,
    segment_ids,
    cls_positions,
    widths,
    out_grad,
):
    tok_rows, model_width = tokens.shape
    seq_rows = cls_positions.shape[0]
    seq_len = tok_rows // seq_rows
    unit_share = inner_proj.shape[1]
    ffn_count = lax.axis_size("ffn")
    tok_count = lax.axis_size("tok")
    ffn_place = lax.axis_index("ffn")
    tok_place = lax.axis_index("tok")
    per_group = seq_rows * ffn_count * tok_count // MB
    batches = jnp.arange(MB, dtype=jnp.int32)
    own_group = (ffn_place * tok_count + tok_place) * seq_rows // per_group
    own_pick = (batches == own_group).astype(jnp.int32)
    heads_kept = jnp.sum(own_pick * widths[:, 1])
    head_on = (jnp.arange(HEADS, dtype=jnp.int32) < heads_kept).astype(jnp.float32)
    factor = 1.0 / math.sqrt(DH)
    unit_total = unit_share * ffn_count
    own_kept = jnp.sum(own_pick * widths[:, 0])
    neuron_on = (jnp.arange(unit_total, dtype=jnp.int32) < own_kept).astype(jnp.float32)
    zero_bias = jnp.zeros((model_width,), jnp.bfloat16)
    joint_bias = jnp.concatenate([query_bias, zero_bias, value_bias]).astype(jnp.float32)
    inner_bias_all = lax.all_gather(inner_bias, "ffn", axis=0, tiled=True).astype(jnp.float32)
    head_mask = jnp.repeat(head_on, DH)
    (
        output, cls_states, inner_rows, outer_rows, probs_again, joint_flat, context_low,
        first_normed, first_scale, act_low, slope_low, sum_grad, small_a,
    ) = run_forward(
        (
            tokens, joint_proj, joint_bias[None], out_proj, out_bias.astype(jnp.float32)[None],
            first_gain[None], first_shift[None], inner_proj.T, outer_proj, inner_bias_all[None],
            outer_bias.astype(jnp.float32)[None], second_gain[None], second_shift[None],
            segment_ids[:, None], segment_ids[None], head_mask[None], neuron_on[None],
            cls_positions, out_grad,
        ),
        unit_share, unit_total, tok_rows, model_width,
    )
    cls_states = cls_states[None]
    first_low = (first_normed * first_gain + first_shift).astype(jnp.bfloat16)
    ffn_grad = sum_grad.astype(jnp.bfloat16)
    second_gain_grad, second_shift_grad, outer_bias_grad = small_a[0], small_a[1], small_a[2]
    joint_low = joint_flat.reshape(seq_rows, seq_len, 3, HEADS, DH)
    queries, key_heads, value_heads = joint_low[:, :, 0], joint_low[:, :, 1], joint_low[:, :, 2]
    probs_again = probs_again[None]
    outer_proj_grad = contract_rows(act_low, ffn_grad)
    act_grad = contract_cols(ffn_grad, outer_rows)
    pre_grad = (act_grad * slope_low.astype(jnp.float32)).astype(jnp.bfloat16)
    inner_bias_sum = jnp.sum(pre_grad.astype(jnp.float32), axis=0)
    inner_rows_grad = contract_rows(pre_grad, first_low)
    first_back = jnp.dot(pre_grad, inner_rows, preferred_element_type=jnp.float32)
    unit_grads = jnp.stack(
        [inner_rows_grad.astype(jnp.bfloat16), outer_proj_grad.astype(jnp.bfloat16)]
    )
    unit_grads = lax.psum_scatter(unit_grads, "ffn", scatter_dimension=1, tiled=True)
    unit_grads = lax.psum(unit_grads, "tok").astype(jnp.float32)
    inner_proj_grad, outer_proj_grad = unit_grads[0].T, unit_grads[1]
    first_grad = sum_grad + first_back
    attn_sum_grad, first_gain_grad, first_shift_grad = normalize_back(
        first_grad, first_normed, first_scale, first_gain
    )
    attn_grad = attn_sum_grad.astype(jnp.bfloat16)
    out_bias_grad = jnp.sum(attn_grad.astype(jnp.float32), axis=0)
    out_proj_grad = contract_rows(context_low, attn_grad)
    context_grad = (
        contract_cols(attn_grad, out_proj)
        .astype(jnp.bfloat16)
        .reshape(seq_rows, seq_len, HEADS, DH)
    )
    context_grad = context_grad * head_on.astype(jnp.bfloat16)[:, None]
    probs = probs_again.astype(jnp.float32)
    value_part = jnp.einsum(
        "rhkq,rqhd->rkhd", probs_again, context_grad, preferred_element_type=jnp.float32
    )
    prob_grad = jnp.einsum(
        "rqhd,rkhd->rhkq", context_grad, value_heads, preferred_element_type=jnp.float32
    )
    score_grad = (probs * (prob_grad - jnp.sum(probs * prob_grad, axis=-2, keepdims=True))).astype(
        jnp.bfloat16
    )
    query_part = (
        jnp.einsum("rhkq,rkhd->rqhd", score_grad, key_heads, preferred_element_type=jnp.float32)
        * factor
    )
    key_part = (
        jnp.einsum("rhkq,rqhd->rkhd", score_grad, queries, preferred_element_type=jnp.float32)
        * factor
    )
    joint_grad = (
        jnp.stack([query_part, key_part, value_part], axis=2)
        .astype(jnp.bfloat16)
        .reshape(tok_rows, 3 * model_width)
    )
    joint_bias_grad = jnp.sum(joint_grad.astype(jnp.float32), axis=0)
    query_bias_grad = joint_bias_grad[:model_width]
    value_bias_grad = joint_bias_grad[2 * model_width :]
    joint_proj_grad = contract_rows(tokens, joint_grad)
    input_grad = attn_sum_grad + contract_cols(joint_grad, joint_proj)
    joint_proj_grad, out_proj_grad = lax.psum(
        (joint_proj_grad.astype(jnp.bfloat16), out_proj_grad.astype(jnp.bfloat16)),
        ("ffn", "tok"),
    )
    joint_proj_grad = joint_proj_grad.astype(jnp.float32)
    out_proj_grad = out_proj_grad.astype(jnp.float32)
    small = [
        query_bias_grad,
        value_bias_grad,
        out_bias_grad,
        first_gain_grad,
        first_shift_grad,
        outer_bias_grad,
        second_gain_grad,
        second_shift_grad,
        inner_bias_sum,
    ]
    small = lax.psum(jnp.concatenate(small), ("ffn", "tok"))
    (
        query_bias_grad,
        value_bias_grad,
        out_bias_grad,
        first_gain_grad,
        first_shift_grad,
        outer_bias_grad,
        second_gain_grad,
        second_shift_grad,
    ) = [small[i * model_width : (i + 1) * model_width] for i in range(8)]
    inner_bias_grad = lax.dynamic_slice(
        small, (8 * model_width + ffn_place * unit_share,), (unit_share,)
    )
    return (
        output,
        cls_states,
        input_grad,
        joint_proj_grad,
        query_bias_grad,
        value_bias_grad,
        out_proj_grad,
        out_bias_grad,
        first_gain_grad,
        first_shift_grad,
        inner_proj_grad,
        inner_bias_grad,
        outer_proj_grad,
        outer_bias_grad,
        second_gain_grad,
        second_shift_grad,
    )


def solution(mesh):
    return jax.shard_map(
        on_device_fast if mesh.shape["ffn"] == 16 and mesh.shape["tok"] == 2 else on_device,
        mesh=mesh,
        in_specs=(
            P(("ffn", "tok"), None),
            P(),
            P(),
            P(),
            P(),
            P(),
            P(),
            P(),
            P(None, "ffn"),
            P("ffn"),
            P("ffn", None),
            P(),
            P(),
            P(),
            P(("ffn", "tok")),
            P(("ffn", "tok"), None),
            P(),
            P(("ffn", "tok"), None),
        ),
        out_specs=(
            P(("ffn", "tok"), None),
            P(("ffn", "tok"), None, None),
            P(("ffn", "tok"), None),
            P(),
            P(),
            P(),
            P(),
            P(),
            P(),
            P(),
            P(None, "ffn"),
            P("ffn"),
            P("ffn", None),
            P(),
            P(),
            P(),
        ),
        check_vma=False,
    )
```

```python
import math

import jax
import jax.numpy as jnp
from jax import lax
from jax.experimental import pallas as pl
from jax.experimental.pallas import tpu as pltpu
from jax.sharding import PartitionSpec as P

MESH = pl.DeviceIdType.MESH
HEADS = 12
DH = 64
MB = 2
SEGS = 4


def normalize(inputs, gain_vec, shift_vec):
    row_mean = jnp.mean(inputs, axis=-1, keepdims=True)
    centred = inputs - row_mean
    row_scale = lax.rsqrt(jnp.mean(centred * centred, axis=-1, keepdims=True) + 1e-12)
    normed = centred * row_scale
    return (normed * gain_vec + shift_vec, normed, row_scale)


def normalize_back(incoming, normed, row_scale, gain_vec):
    gain_grad = jnp.sum(incoming * normed, axis=0)
    shift_grad = jnp.sum(incoming, axis=0)
    scaled_grad = incoming * gain_vec
    inputs_grad = row_scale * (
        scaled_grad
        - jnp.mean(scaled_grad, axis=-1, keepdims=True)
        - normed * jnp.mean(scaled_grad * normed, axis=-1, keepdims=True)
    )
    return (inputs_grad, gain_grad, shift_grad)


def gelu_slope(inputs):
    return (
        0.5 * (1.0 + lax.erf(inputs * 0.7071067811865476))
        + inputs * jnp.exp(-0.5 * inputs * inputs) * 0.3989422804014327
    )


def contract_rows(left_side, right_side):
    return lax.dot_general(
        left_side, right_side, (((0,), (0,)), ((), ())), preferred_element_type=jnp.float32
    )


def contract_cols(left_side, right_side):
    return lax.dot_general(
        left_side, right_side, (((1,), (1,)), ((), ())), preferred_element_type=jnp.float32
    )


def on_device(
    tokens,
    joint_proj,
    query_bias,
    value_bias,
    out_proj,
    out_bias,
    first_gain,
    first_shift,
    inner_proj,
    inner_bias,
    outer_proj,
    outer_bias,
    second_gain,
    second_shift,
    segment_ids,
    cls_positions,
    widths,
    out_grad,
):
    tok_rows, model_width = tokens.shape
    seq_rows = cls_positions.shape[0]
    seq_len = tok_rows // seq_rows
    unit_share = inner_proj.shape[1]
    ffn_count = lax.axis_size("ffn")
    tok_count = lax.axis_size("tok")
    ffn_place = lax.axis_index("ffn")
    tok_place = lax.axis_index("tok")
    per_group = seq_rows * ffn_count * tok_count // MB
    batches = jnp.arange(MB, dtype=jnp.int32)
    own_group = (ffn_place * tok_count + tok_place) * seq_rows // per_group
    own_pick = (batches == own_group).astype(jnp.int32)
    heads_kept = jnp.sum(own_pick * widths[:, 1])
    head_on = (jnp.arange(HEADS, dtype=jnp.int32) < heads_kept).astype(jnp.float32)
    factor = 1.0 / math.sqrt(DH)
    zero_bias = jnp.zeros((model_width,), jnp.bfloat16)
    joint_bias = jnp.concatenate([query_bias, zero_bias, value_bias])
    joint_low = (
        jnp.dot(tokens, joint_proj, preferred_element_type=jnp.float32) + joint_bias
    ).astype(jnp.bfloat16)
    joint_low = joint_low.reshape(seq_rows, seq_len, 3, HEADS, DH)
    queries = joint_low[:, :, 0]
    key_heads = joint_low[:, :, 1]
    value_heads = joint_low[:, :, 2]
    segments = segment_ids.reshape(seq_rows, seq_len)
    same_doc = (segments[:, :, None] == segments[:, None, :])[:, None]

    def scores_of(query_rows, key_rows):
        raw_scores = (
            jnp.einsum("rqhd,rkhd->rhqk", query_rows, key_rows, preferred_element_type=jnp.float32)
            * factor
        )
        return jnp.where(same_doc, raw_scores, -1e30)

    scores = scores_of(queries, key_heads)
    row_peak = jnp.max(scores, axis=-1, keepdims=True)
    log_total = row_peak + jnp.log(jnp.sum(jnp.exp(scores - row_peak), axis=-1, keepdims=True))
    probs_low = jnp.exp(scores - log_total).astype(jnp.bfloat16)
    context = (
        jnp.einsum("rhqk,rkhd->rqhd", probs_low, value_heads, preferred_element_type=jnp.float32)
        * head_on[:, None]
    )
    context_low = context.astype(jnp.bfloat16).reshape(tok_rows, model_width)
    attn_out = jnp.dot(context_low, out_proj, preferred_element_type=jnp.float32) + out_bias
    first_out, first_normed, first_scale = normalize(
        tokens.astype(jnp.float32) + attn_out, first_gain, first_shift
    )
    first_low = first_out.astype(jnp.bfloat16)
    unit_total = unit_share * ffn_count
    stacked = lax.all_gather(
        jnp.stack([inner_proj.T, outer_proj]), "ffn", axis=1, tiled=True
    )
    inner_rows, outer_rows = stacked[0], stacked[1]
    inner_bias_all = lax.all_gather(inner_bias, "ffn", axis=0, tiled=True)
    own_kept = jnp.sum(own_pick * widths[:, 0])
    neuron_on = (jnp.arange(unit_total, dtype=jnp.int32) < own_kept).astype(jnp.float32)
    pre_act = contract_cols(first_low, inner_rows) + inner_bias_all
    act_low = (jax.nn.gelu(pre_act, approximate=False) * neuron_on).astype(jnp.bfloat16)
    ffn_out = jnp.dot(act_low, outer_rows, preferred_element_type=jnp.float32) + outer_bias
    second_out, second_normed, second_scale = normalize(
        first_out + ffn_out, second_gain, second_shift
    )
    output = second_out.astype(jnp.bfloat16)
    cls_states = jnp.take_along_axis(
        second_out.reshape(seq_rows, seq_len, model_width), cls_positions[:, :, None], axis=1
    )
    sum_grad, second_gain_grad, second_shift_grad = normalize_back(
        out_grad.astype(jnp.float32), second_normed, second_scale, second_gain
    )
    ffn_grad = sum_grad.astype(jnp.bfloat16)
    outer_bias_grad = jnp.sum(ffn_grad.astype(jnp.float32), axis=0)
    outer_proj_grad = contract_rows(act_low, ffn_grad)
    act_grad = contract_cols(ffn_grad, outer_rows)
    pre_grad = (act_grad * (gelu_slope(pre_act) * neuron_on)).astype(jnp.bfloat16)
    inner_bias_sum = jnp.sum(pre_grad.astype(jnp.float32), axis=0)
    inner_rows_grad = contract_rows(pre_grad, first_low)
    first_back = jnp.dot(pre_grad, inner_rows, preferred_element_type=jnp.float32)
    unit_grads = jnp.stack(
        [inner_rows_grad.astype(jnp.bfloat16), outer_proj_grad.astype(jnp.bfloat16)]
    )
    unit_grads = lax.psum_scatter(unit_grads, "ffn", scatter_dimension=1, tiled=True)
    unit_grads = lax.psum(unit_grads, "tok").astype(jnp.float32)
    inner_proj_grad, outer_proj_grad = unit_grads[0].T, unit_grads[1]
    first_grad = sum_grad + first_back
    attn_sum_grad, first_gain_grad, first_shift_grad = normalize_back(
        first_grad, first_normed, first_scale, first_gain
    )
    attn_grad = attn_sum_grad.astype(jnp.bfloat16)
    out_bias_grad = jnp.sum(attn_grad.astype(jnp.float32), axis=0)
    out_proj_grad = contract_rows(context_low, attn_grad)
    context_grad = (
        contract_cols(attn_grad, out_proj)
        .astype(jnp.bfloat16)
        .reshape(seq_rows, seq_len, HEADS, DH)
    )
    context_grad = context_grad * head_on.astype(jnp.bfloat16)[:, None]
    scores = scores_of(queries, key_heads)
    probs = jnp.exp(scores - log_total)
    probs_again = probs.astype(jnp.bfloat16)
    value_part = jnp.einsum(
        "rhqk,rqhd->rkhd", probs_again, context_grad, preferred_element_type=jnp.float32
    )
    prob_grad = jnp.einsum(
        "rqhd,rkhd->rhqk", context_grad, value_heads, preferred_element_type=jnp.float32
    )
    score_grad = (probs * (prob_grad - jnp.sum(probs * prob_grad, axis=-1, keepdims=True))).astype(
        jnp.bfloat16
    )
    query_part = (
        jnp.einsum("rhqk,rkhd->rqhd", score_grad, key_heads, preferred_element_type=jnp.float32)
        * factor
    )
    key_part = (
        jnp.einsum("rhqk,rqhd->rkhd", score_grad, queries, preferred_element_type=jnp.float32)
        * factor
    )
    joint_grad = (
        jnp.stack([query_part, key_part, value_part], axis=2)
        .astype(jnp.bfloat16)
        .reshape(tok_rows, 3 * model_width)
    )
    joint_bias_grad = jnp.sum(joint_grad.astype(jnp.float32), axis=0)
    query_bias_grad = joint_bias_grad[:model_width]
    value_bias_grad = joint_bias_grad[2 * model_width :]
    joint_proj_grad = contract_rows(tokens, joint_grad)
    input_grad = attn_sum_grad + contract_cols(joint_grad, joint_proj)
    joint_proj_grad, out_proj_grad = lax.psum(
        (joint_proj_grad.astype(jnp.bfloat16), out_proj_grad.astype(jnp.bfloat16)),
        ("ffn", "tok"),
    )
    joint_proj_grad = joint_proj_grad.astype(jnp.float32)
    out_proj_grad = out_proj_grad.astype(jnp.float32)
    small = [
        query_bias_grad,
        value_bias_grad,
        out_bias_grad,
        first_gain_grad,
        first_shift_grad,
        outer_bias_grad,
        second_gain_grad,
        second_shift_grad,
        inner_bias_sum,
    ]
    small = lax.psum(jnp.concatenate(small), ("ffn", "tok"))
    (
        query_bias_grad,
        value_bias_grad,
        out_bias_grad,
        first_gain_grad,
        first_shift_grad,
        outer_bias_grad,
        second_gain_grad,
        second_shift_grad,
    ) = [small[i * model_width : (i + 1) * model_width] for i in range(8)]
    inner_bias_grad = lax.dynamic_slice(
        small, (8 * model_width + ffn_place * unit_share,), (unit_share,)
    )
    return (
        output,
        cls_states,
        input_grad,
        joint_proj_grad,
        query_bias_grad,
        value_bias_grad,
        out_proj_grad,
        out_bias_grad,
        first_gain_grad,
        first_shift_grad,
        inner_proj_grad,
        inner_bias_grad,
        outer_proj_grad,
        outer_bias_grad,
        second_gain_grad,
        second_shift_grad,
    )


def x_or1(v):
    return v + 1 - 2 * (v % 2)


def x_or2(v):
    return v + 2 - 4 * ((v // 2) % 2)


def z_peer(place, turn):
    deep = place // 4
    if turn & 1:
        deep = x_or1(deep)
    if turn & 2:
        deep = x_or2(deep)
    return deep * 4 + place % 4


def y_peer(place):
    return (place // 4) * 4 + ((place // 2 + 1) % 2) * 2 + place % 2


def c_peer(place):
    return x_or1(place)


def nt_dot(left_side, right_side):
    return lax.dot_general(
        left_side, right_side, (((1,), (1,)), ((), ())), preferred_element_type=jnp.float32
    )


def tn_dot(left_side, right_side):
    return lax.dot_general(
        left_side, right_side, (((0,), (0,)), ((), ())), preferred_element_type=jnp.float32
    )


def nn_dot(left_side, right_side):
    return lax.dot_general(
        left_side, right_side, (((1,), (0,)), ((), ())), preferred_element_type=jnp.float32
    )


def greet(place, side):
    barrier = pltpu.get_barrier_semaphore()
    peers = [
        (z_peer(place, 1), side),
        (z_peer(place, 2), side),
        (z_peer(place, 3), side),
        (y_peer(place), side),
        (c_peer(place), side),
        (place, 1 - side),
    ]
    for peer in peers:
        pl.semaphore_signal(barrier, inc=1, device_id=peer, device_id_type=MESH)
    pl.semaphore_wait(barrier, 6)


def remote(source, target, send_sem, recv_sem, device):
    return pltpu.make_async_remote_copy(
        src_ref=source,
        dst_ref=target,
        send_sem=send_sem,
        recv_sem=recv_sem,
        device_id=device,
        device_id_type=MESH,
    )


class Spread:
    def __init__(self, own, whole, place, side, rows, sems):
        self.own, self.whole, self.place, self.side, self.rows = own, whole, place, side, rows
        self.up_s, self.up_r, self.dn_s, self.dn_r, self.y_s, self.y_r = sems[:6]
        self.x_s, self.x_r, self.c_s, self.c_r, self.d_s, self.d_r = sems[6:]
        self.third = rows // 3
        self.deep = place // 4

    def span(self, source, offset, count):
        start = pl.multiple_of(source * self.rows + offset, 16)
        return self.whole.at[pl.ds(start, count)]

    def slab(self, source):
        return self.span(source, self.side * self.third, 2 * self.third)

    def edge(self, source, mine=True):
        side = self.side if mine else 1 - self.side
        return self.span(source, side * 2 * self.third, self.third)

    def own_slab(self):
        start = pl.multiple_of(self.side * self.third, 16)
        return self.own.at[pl.ds(start, 2 * self.third)]

    def source_of(self, step, up, cross=False):
        base = y_peer(self.place) if cross else self.place
        if step is None:
            return base
        return base - 4 * (step + 1) if up else base + 4 * (step + 1)

    def has(self, step, up):
        if step is None:
            return None
        return self.deep >= step + 1 if up else self.deep + step + 1 <= 3

    def hop(self, step, up, first=False):
        source = self.place if step == 0 else self.source_of(step - 1, up)
        piece = self.own_slab() if step == 0 else self.slab(source)
        send, recv = (self.up_s, self.up_r) if up else (self.dn_s, self.dn_r)
        device = (self.place + 4 if up else self.place - 4, self.side)
        return remote(piece, self.slab(source), send.at[step], recv.at[step], device)

    def hop_in(self, step, up):
        source = self.source_of(step, up)
        send, recv = (self.up_s, self.up_r) if up else (self.dn_s, self.dn_r)
        return remote(
            self.slab(source), self.slab(source), send.at[step], recv.at[step], (self.place, 1 - self.side)
        )

    def over_y(self, source, own=False):
        index = source // 4
        piece = self.own_slab() if own else self.slab(source)
        return remote(
            piece, self.slab(source), self.y_s.at[index], self.y_r.at[index], (y_peer(self.place), self.side)
        )

    def over_x(self, source, mine=True):
        index = source // 2
        piece = self.edge(source, mine)
        return remote(
            piece, piece, self.x_s.at[index], self.x_r.at[index], (self.place, 1 - self.side)
        )

    def over_c(self, source):
        index = source // 2
        return remote(
            self.slab(source),
            self.slab(source),
            self.c_s.at[index],
            self.c_r.at[index],
            (c_peer(self.place), self.side),
        )

    def over_d(self, source):
        index = source // 2
        piece = self.edge(source, False)
        return remote(piece, piece, self.d_s.at[index], self.d_r.at[index], (c_peer(self.place), self.side))

    def over_own(self):
        index = self.place // 2
        return remote(
            self.own,
            self.span(self.place, 0, self.rows),
            self.c_s.at[index],
            self.c_r.at[index],
            (c_peer(self.place), self.side),
        )

    def start(self):
        @pl.when(self.deep < 3)
        def _():
            self.hop(0, True).start()

        @pl.when(self.deep > 0)
        def _():
            self.hop(0, False).start()

        self.over_y(self.place, own=True).start()
        self.over_own().start()

    def z_event(self, step):
        for up in (True, False):

            @pl.when(self.has(step, up))
            def _(up=up):
                source = self.source_of(step, up)
                self.hop_in(step, up).wait_recv()
                if step < 2:

                    @pl.when(self.deep < 3 if up else self.deep > 0)
                    def _():
                        self.hop(step + 1, up).start()

                self.over_y(source).start()
                self.over_x(source).start()
                self.over_c(source).start()

    def each(self, step, work):
        if step is None:
            work(True)
            return
        for up in (True, False):

            @pl.when(self.has(step, up))
            def _(up=up):
                work(up)

    def y_event(self, step):
        def work(up):
            source = self.source_of(step, up, cross=True)
            self.over_y(source).wait_recv()
            self.over_x(source).start()
            self.over_c(source).start()

        self.each(step, work)

    def x_event(self, step, cross):
        def work(up):
            source = self.source_of(step, up, cross=cross)
            self.over_x(source, False).wait_recv()
            self.over_d(source).start()

        self.each(step, work)

    def finish(self):
        other = c_peer(self.place) % 2
        own = c_peer(self.place)
        for index in range(8):
            source = 2 * index + other

            @pl.when(source != own)
            def _(source=source):
                self.over_c(source).wait_recv()
                self.over_d(source).wait_recv()

            @pl.when(source == own)
            def _(source=source):
                remote(
                    self.own,
                    self.span(source, 0, self.rows),
                    self.c_s.at[index],
                    self.c_r.at[index],
                    (c_peer(self.place), self.side),
                ).wait_recv()

    def drain(self):
        for up in (True, False):
            for step in range(3):
                limit = self.deep < 3 if up else self.deep > 0
                if step > 0:
                    limit = jnp.logical_and(limit, self.has(step - 1, up))

                @pl.when(limit)
                def _(step=step, up=up):
                    self.hop(step, up).wait_send()

        for index in range(4):
            source = 4 * index + self.place % 4
            self.over_y(source).wait_send()
        mine = self.place % 2
        for index in range(8):
            source = 2 * index + mine

            @pl.when(source != self.place)
            def _(source=source):
                self.over_x(source).wait_send()
                self.over_c(source).wait_send()
                self.over_d(source).wait_send()

            @pl.when(source == self.place)
            def _():
                self.over_own().wait_send()


def forward_kernel(
    tokens,
    joint_proj,
    joint_bias,
    out_proj,
    out_bias,
    first_gain,
    first_shift,
    inner_own,
    outer_own,
    inner_bias,
    outer_bias,
    second_gain,
    second_shift,
    seg_down,
    seg_over,
    head_mask,
    unit_mask,
    cls_at,
    out_grad,
    output,
    cls_out,
    inner_out,
    outer_out,
    probs_out,
    joint_out,
    context_out,
    normed_out,
    scale_out,
    act_out,
    slope_out,
    sum_grad_out,
    small_out,
    inner_all,
    outer_all,
    probs,
    joint,
    context,
    mask_bias,
    act,
    slope,
    first_low,
    wide,
    save_sem,
    *sems,
):
    place, side = lax.axis_index("ffn"), lax.axis_index("tok")
    rows_total = tokens.shape[0]
    units = inner_all.shape[0]
    share = inner_own.shape[0]
    width = tokens.shape[1]
    half = rows_total // 2
    greet(place, side)
    inner = Spread(inner_own, inner_all, place, side, share, sems[:12])
    outer = Spread(outer_own, outer_all, place, side, share, sems[12:])
    inner.start()
    outer.start()
    own_rows = pl.ds(pl.multiple_of(place * share, 16), share)
    inner_all[own_rows, :] = inner_own[...]
    outer_all[own_rows, :] = outer_own[...]
    saves = []

    def save(source, target, index):
        pltpu.make_async_copy(source, target, save_sem.at[index]).start()
        saves.append((source, target, index))

    mask_bias[...] = jnp.where(seg_down[...] == seg_over[...], 0.0, -1e30)

    def joint_step(j, carry):
        cols = pl.ds(pl.multiple_of(j * 256, 256), 256)
        joint[:, cols] = (nn_dot(tokens[...], joint_proj[:, cols]) + joint_bias[:, cols]).astype(
            jnp.bfloat16
        )
        return carry

    lax.fori_loop(0, 3 * width // 256, joint_step, 0)
    save(joint, joint_out, 0)
    events = [
        lambda: inner.z_event(0),
        lambda: outer.z_event(0),
        lambda: inner.y_event(None),
        lambda: inner.z_event(1),
        lambda: outer.y_event(None),
        lambda: inner.y_event(0),
        lambda: outer.z_event(1),
        lambda: inner.x_event(0, False),
        lambda: inner.x_event(None, True),
        lambda: outer.y_event(0),
        lambda: inner.z_event(2),
        lambda: outer.x_event(0, False),
        lambda: outer.x_event(None, True),
        lambda: inner.y_event(1),
        lambda: outer.z_event(2),
        lambda: inner.x_event(1, False),
        lambda: inner.x_event(0, True),
        lambda: outer.y_event(1),
        lambda: inner.y_event(2),
        lambda: outer.x_event(1, False),
        lambda: outer.x_event(0, True),
        lambda: inner.x_event(2, False),
        lambda: inner.x_event(1, True),
        lambda: outer.y_event(2),
        lambda: inner.x_event(2, True),
        lambda: outer.x_event(2, False),
        lambda: outer.x_event(1, True),
        lambda: outer.x_event(2, True),
    ]
    events[0]()
    slots = {0: events[1:4], 1: events[4:6], 2: events[6:10], 3: events[10:14], 4: events[14:18], 5: events[18:22]}
    first_half = (lax.broadcasted_iota(jnp.int32, (1, 128), 1) < DH).astype(jnp.bfloat16)
    halves = (first_half, 1 - first_half)
    factor = 1.4426950408889634 / math.sqrt(DH)
    pairs = HEADS // 2

    def pair_step(p, carry):
        cols = [pl.ds(pl.multiple_of(s * width + p * 128, 128), 128) for s in range(3)]
        out_cols = pl.ds(pl.multiple_of(p * 128, 128), 128)
        keys, values = joint[:, cols[1]], joint[:, cols[2]]
        for b in range(2):
            lanes = slice(b * half, (b + 1) * half)
            queries = joint[lanes, cols[0]]
            total = None
            for a in range(2):
                scores = nt_dot(keys * halves[a], queries) * factor + mask_bias[:, lanes]
                weights = jnp.exp2(scores - jnp.max(scores, axis=0, keepdims=True))
                weights = weights * (1.0 / jnp.sum(weights, axis=0, keepdims=True))
                low = weights.astype(jnp.bfloat16)
                probs[2 * p + a, :, lanes] = low
                part = tn_dot(low, values * halves[a])
                total = part if total is None else total + part
            context[lanes, out_cols] = (total * head_mask[:, out_cols]).astype(jnp.bfloat16)
        pltpu.make_async_copy(
            probs.at[pl.ds(2 * p, 2)], probs_out.at[pl.ds(2 * p, 2)], save_sem.at[6 + p]
        ).start()
        for slot, todo in slots.items():

            @pl.when(p == slot)
            def _(todo=todo):
                for event in todo:
                    event()

        return carry

    lax.fori_loop(0, pairs, pair_step, 0)
    save(context, context_out, 1)
    for j in range(width // 256):
        cols = slice(j * 256, (j + 1) * 256)
        wide[:, cols] = nn_dot(context[...], out_proj[:, cols])

    def first_norm(i, carry):
        rows = pl.ds(pl.multiple_of(i * 128, 128), 128)
        total = tokens[rows, :].astype(jnp.float32) + (wide[rows, :] + out_bias[...])
        centred = total - jnp.mean(total, axis=-1, keepdims=True)
        scale = lax.rsqrt(jnp.mean(centred * centred, axis=-1, keepdims=True) + 1e-12)
        normed = centred * scale
        normed_out[rows, :] = normed
        scale_out[rows, :] = scale
        first_low[rows, :] = (normed * first_gain[...] + first_shift[...]).astype(jnp.bfloat16)
        return carry

    lax.fori_loop(0, rows_total // 128, first_norm, 0)
    for event in events[22:25]:
        event()
    inner.finish()
    save(inner_all, inner_out, 2)
    unit_slots = {0: events[25:26], 3: events[26:27], 6: events[27:]}

    def unit_step(j, carry):
        cols = pl.ds(pl.multiple_of(j * 256, 256), 256)
        for b in range(2):
            rows = slice(b * half, (b + 1) * half)
            pre = nt_dot(first_low[rows, :], inner_all[cols, :]) + inner_bias[:, cols]
            gate = 0.5 + 0.5 * lax.erf(pre * 0.7071067811865476)
            on = unit_mask[:, cols]
            act[rows, cols] = (pre * gate * on).astype(jnp.bfloat16)
            slope[rows, cols] = (
                (gate + pre * jnp.exp(-0.5 * pre * pre) * 0.3989422804014327) * on
            ).astype(jnp.bfloat16)
        for slot, todo in unit_slots.items():

            @pl.when(j == slot)
            def _(todo=todo):
                for event in todo:
                    event()

        return carry

    lax.fori_loop(0, units // 256, unit_step, 0)
    save(act, act_out, 3)
    save(slope, slope_out, 4)
    outer.finish()
    save(outer_all, outer_out, 5)
    for j in range(width // 256):
        cols = slice(j * 256, (j + 1) * 256)
        wide[:, cols] = nn_dot(act[...], outer_all[:, cols])
    small_out[...] = jnp.zeros_like(small_out)

    def second_norm(i, carry):
        rows = pl.ds(pl.multiple_of(i * 128, 128), 128)
        first = normed_out[rows, :] * first_gain[...] + first_shift[...]
        total = first + (wide[rows, :] + outer_bias[...])
        centred = total - jnp.mean(total, axis=-1, keepdims=True)
        scale = lax.rsqrt(jnp.mean(centred * centred, axis=-1, keepdims=True) + 1e-12)
        normed = centred * scale
        second = normed * second_gain[...] + second_shift[...]
        wide[rows, :] = second
        output[rows, :] = second.astype(jnp.bfloat16)
        grad = out_grad[rows, :].astype(jnp.float32)
        scaled = grad * second_gain[...]
        back = scale * (
            scaled
            - jnp.mean(scaled, axis=-1, keepdims=True)
            - normed * jnp.mean(scaled * normed, axis=-1, keepdims=True)
        )
        sum_grad_out[rows, :] = back
        low = back.astype(jnp.bfloat16).astype(jnp.float32)
        small_out[0:1, :] += jnp.sum(grad * normed, axis=0, keepdims=True)
        small_out[1:2, :] += jnp.sum(grad, axis=0, keepdims=True)
        small_out[2:3, :] += jnp.sum(low, axis=0, keepdims=True)
        return carry

    lax.fori_loop(0, rows_total // 128, second_norm, 0)
    for j in range(SEGS):
        cls_out[j : j + 1, :] = wide[pl.ds(cls_at[0, j], 1), :]
    inner.drain()
    outer.drain()
    for source, target, index in saves:
        pltpu.make_async_copy(source, target, save_sem.at[index]).wait()
    for p in range(pairs):
        pltpu.make_async_copy(
            probs.at[pl.ds(2 * p, 2)], probs_out.at[pl.ds(2 * p, 2)], save_sem.at[6 + p]
        ).wait()


def run_forward(args, share, units, rows_total, width):
    sems = []
    for unused in range(2):
        for count in (3, 3, 3, 3, 4, 4, 8, 8, 8, 8, 8, 8):
            sems.append(pltpu.SemaphoreType.DMA((count,)))
    bf, fp = jnp.bfloat16, jnp.float32
    shape = jax.ShapeDtypeStruct
    vmem = pl.BlockSpec(memory_space=pltpu.VMEM)
    anywhere = pl.BlockSpec(memory_space=pl.ANY)
    in_specs = [vmem] * 17 + [pl.BlockSpec(memory_space=pltpu.SMEM), vmem]
    return pl.pallas_call(
        forward_kernel,
        out_shape=(
            shape((rows_total, width), bf),
            shape((SEGS, width), fp),
            shape((units, width), bf),
            shape((units, width), bf),
            shape((HEADS, rows_total, rows_total), bf),
            shape((rows_total, 3 * width), bf),
            shape((rows_total, width), bf),
            shape((rows_total, width), fp),
            shape((rows_total, 1), fp),
            shape((rows_total, units), bf),
            shape((rows_total, units), bf),
            shape((rows_total, width), fp),
            shape((16, width), fp),
        ),
        in_specs=in_specs,
        out_specs=(
            vmem, vmem, anywhere, anywhere, anywhere, anywhere, anywhere, vmem, vmem, anywhere, anywhere, vmem, vmem,
        ),
        scratch_shapes=[
            pltpu.VMEM((units, width), bf),
            pltpu.VMEM((units, width), bf),
            pltpu.VMEM((HEADS, rows_total, rows_total), bf),
            pltpu.VMEM((rows_total, 3 * width), bf),
            pltpu.VMEM((rows_total, width), bf),
            pltpu.VMEM((rows_total, rows_total), fp),
            pltpu.VMEM((rows_total, units), bf),
            pltpu.VMEM((rows_total, units), bf),
            pltpu.VMEM((rows_total, width), bf),
            pltpu.VMEM((rows_total, width), fp),
            pltpu.SemaphoreType.DMA((6 + HEADS // 2,)),
        ]
        + sems,
        compiler_params=pltpu.CompilerParams(
            collective_id=0, has_side_effects=True, vmem_limit_bytes=64 * 1024 * 1024 - 65536
        ),
        name="forward",
    )(*args)


def backward_kernel(
    act_in,
    slope_in,
    sum_grad_in,
    outer_in,
    inner_in,
    normed_in,
    joint_in,
    context_in,
    probs_in,
    tokens_in,
    joint_proj_in,
    out_proj_in,
    scale,
    small_in,
    first_gain,
    first_shift,
    head_mask,
    input_grad,
    summed_out,
    outer_grad,
    inner_grad,
    small_out,
    act,
    slope,
    weight,
    probs,
    joint,
    context,
    normed,
    grad,
    tokens,
    tokens_over,
    joint_proj,
    out_proj,
    low,
    first_low,
    outer_sum,
    inner_sum,
    outer_c,
    outer_x,
    outer_y,
    outer_z,
    inner_c,
    inner_y,
    inner_z,
    inner_own,
    inner_far,
    parts,
    part_c,
    part_a,
    part_b,
    part_z,
    joint_grad,
    context_grad,
    small,
    small_far,
    load_sem,
    probs_sem,
    keep_sem,
    *sems,
):
    place, side = lax.axis_index("ffn"), lax.axis_index("tok")
    core, flank, deep = place % 2, (place // 2) % 2, place // 4
    rows_total, units = act.shape
    width = grad.shape[1]
    half = rows_total // 2
    share = inner_own.shape[0]
    bf, fp = jnp.bfloat16, jnp.float32
    sem_names = (
        "oc", "ox", "oy", "oz", "of", "ic", "iy", "iz", "ix", "ac", "aa", "ab", "az", "gz", "gb", "ga", "gc", "bt"
    )
    send = dict(zip(sem_names, sems[: len(sem_names)]))
    recv = dict(zip(sem_names, sems[len(sem_names) :]))
    made = {}

    def define(name, index, source, target, device):
        made[(name,) + index] = lambda: remote(
            source(), target(), send[name].at[index], recv[name].at[index], device
        )

    def go(name, *index):
        made[(name,) + index]().start()

    def got(name, *index):
        made[(name,) + index]().wait_recv()

    peer_x, peer_y, peer_c = (place, 1 - side), (y_peer(place), side), (c_peer(place), side)
    peer_z = [None] + [(z_peer(place, turn), side) for turn in (1, 2, 3)]
    deep_of = [z_peer(place, turn) // 4 if turn else deep for turn in range(4)]
    third = share // 2

    def shard(turn, y, c, offset=0, count=None):
        start = ((deep_of[turn] * 2 + y) * 2 + c) * share + offset
        return pl.ds(pl.multiple_of(start, 16), share if count is None else count)

    for t in range(4):
        for y in range(2):
            define(
                "oc", (t, y), lambda t=t, y=y: outer_sum.at[shard(t, y, 1 - core)], lambda t=t, y=y: outer_c.at[t, y], peer_c
            )
            define(
                "ic", (t, y), lambda t=t, y=y: inner_sum.at[shard(t, y, 1 - core)], lambda t=t, y=y: inner_c.at[t, y], peer_c
            )
            define(
                "ox",
                (t, y),
                lambda t=t, y=y: outer_sum.at[shard(t, y, core, (1 - side) * third, third)],
                lambda t=t, y=y: outer_x.at[t, y],
                peer_x,
            )
        define(
            "oy",
            (t,),
            lambda t=t: outer_sum.at[shard(t, 1 - flank, core, side * third, third)],
            lambda t=t: outer_y.at[t],
            peer_y,
        )
        define(
            "iy", (t,), lambda t=t: inner_sum.at[shard(t, 1 - flank, core)], lambda t=t: inner_y.at[t], peer_y
        )
        if t:
            define(
                "oz",
                (t - 1,),
                lambda t=t: outer_sum.at[shard(t, flank, core, side * third, third)],
                lambda t=t: outer_z.at[t - 1],
                peer_z[t],
            )
            define(
                "iz",
                (t - 1,),
                lambda t=t: inner_sum.at[shard(t, flank, core)],
                lambda t=t: inner_z.at[t - 1],
                peer_z[t],
            )
    own_part = pl.ds(pl.multiple_of(side * third, 16), third)
    define("of", (0,), lambda: outer_grad.at[own_part], lambda: outer_grad.at[own_part], peer_x)
    define("ix", (0,), lambda: inner_own, lambda: inner_far, peer_x)

    def add(target, source):
        target[...] = (target[...].astype(fp) + source[...].astype(fp)).astype(bf)

    def outer_to_x(t):
        for y in range(2):
            got("oc", t, y)
            add(outer_sum.at[shard(t, y, core)], outer_c.at[t, y])
            go("ox", t, y)

    def outer_to_y(t):
        for y in range(2):
            got("ox", t, y)
            add(outer_sum.at[shard(t, y, core, side * third, third)], outer_x.at[t, y])
        go("oy", t)

    def outer_to_z(t):
        got("oy", t)
        add(outer_sum.at[shard(t, flank, core, side * third, third)], outer_y.at[t])
        if t:
            go("oz", t - 1)

    def outer_end():
        total = outer_sum[shard(0, flank, core, side * third, third), :].astype(fp)
        for t in range(3):
            got("oz", t)
            total = total + outer_z[t].astype(fp)
        outer_grad[own_part, :] = total.astype(bf)
        go("of", 0)

    def inner_to_y(t):
        for y in range(2):
            got("ic", t, y)
            add(inner_sum.at[shard(t, y, core)], inner_c.at[t, y])
        go("iy", t)

    def inner_to_z(t):
        got("iy", t)
        add(inner_sum.at[shard(t, flank, core)], inner_y.at[t])
        if t:
            go("iz", t - 1)

    def inner_end():
        total = inner_sum[shard(0, flank, core), :].astype(fp)
        for t in range(3):
            got("iz", t)
            total = total + inner_z[t].astype(fp)
        inner_own[...] = total.astype(bf)
        go("ix", 0)

    def inner_last():
        got("ix", 0)
        inner_grad[...] = inner_own[...].astype(fp) + inner_far[...].astype(fp)

    quarter = width // 2

    def cols_of(c):
        return pl.ds(pl.multiple_of(c * quarter, 128), quarter)

    def rows_of(j, depth, flips=(0, 0), z=None):
        first, second = (side, flank) if j % 2 == 0 else (flank, side)
        if flips[0]:
            first = 1 - first
        if flips[1]:
            second = 1 - second
        start, count = first * (width // 2), width // 2
        if depth > 1:
            start, count = start + second * (width // 4), width // 4
        if depth > 2:
            start, count = start + (deep if z is None else z) * (width // 16), width // 16
        return pl.ds(pl.multiple_of(start, 16), count)

    for j in range(4):
        near, far = (peer_x, peer_y) if j % 2 == 0 else (peer_y, peer_x)
        define("ac", (j,), lambda j=j: parts.at[j, :, cols_of(1 - core)], lambda j=j: part_c.at[j], peer_c)
        define(
            "aa", (j,), lambda j=j: parts.at[j, rows_of(j, 1, (1, 0)), cols_of(core)], lambda j=j: part_a.at[j], near
        )
        define(
            "ab", (j,), lambda j=j: parts.at[j, rows_of(j, 2, (0, 1)), cols_of(core)], lambda j=j: part_b.at[j], far
        )
        for t in (1, 2, 3):
            define(
                "az",
                (j, t - 1),
                lambda j=j, t=t: parts.at[j, rows_of(j, 3, z=deep_of[t]), cols_of(core)],
                lambda j=j, t=t: part_z.at[j, t - 1],
                peer_z[t],
            )
            define(
                "gz",
                (j, t - 1),
                lambda j=j: parts.at[j, rows_of(j, 3), cols_of(core)],
                lambda j=j: summed_out.at[j, rows_of(j, 3), cols_of(core)],
                peer_z[t],
            )

        def place_of(depth, j=j):
            if depth:
                return lambda: summed_out.at[j, rows_of(j, depth), cols_of(core)]
            return lambda: summed_out.at[j, :, cols_of(core)]

        define("gb", (j,), place_of(2), place_of(2), far)
        define("ga", (j,), place_of(1), place_of(1), near)
        define("gc", (j,), place_of(0), place_of(0), peer_c)

    def keep(j):
        return pltpu.make_async_copy(
            parts.at[j, rows_of(j, 3), cols_of(core)], summed_out.at[j, rows_of(j, 3), cols_of(core)], keep_sem.at[j]
        )

    def sum_1(j):
        got("ac", j)
        add(parts.at[j, :, cols_of(core)], part_c.at[j])
        go("aa", j)

    def sum_2(j):
        got("aa", j)
        add(parts.at[j, rows_of(j, 1), cols_of(core)], part_a.at[j])
        go("ab", j)

    def sum_3(j):
        got("ab", j)
        add(parts.at[j, rows_of(j, 2), cols_of(core)], part_b.at[j])
        for t in range(3):
            go("az", j, t)

    def sum_4(j):
        total = parts[j, rows_of(j, 3), cols_of(core)].astype(fp)
        for t in range(3):
            got("az", j, t)
            total = total + part_z[j, t].astype(fp)
        parts[j, rows_of(j, 3), cols_of(core)] = total.astype(bf)
        for t in range(3):
            go("gz", j, t)
        keep(j).start()

    def sum_5(j):
        keep(j).wait()
        for t in range(3):
            remote(
                summed_out.at[j, rows_of(j, 3, z=deep_of[t + 1]), cols_of(core)],
                summed_out.at[j, rows_of(j, 3, z=deep_of[t + 1]), cols_of(core)],
                send["gz"].at[j, t],
                recv["gz"].at[j, t],
                peer_z[t + 1],
            ).wait_recv()
        go("gb", j)

    def arrive(name, j, depth, flips, c=None):
        cols = cols_of(core if c is None else c)
        piece = summed_out.at[j, rows_of(j, depth, flips), cols] if depth else summed_out.at[j, :, cols]
        remote(piece, piece, send[name].at[j], recv[name].at[j], peer_x).wait_recv()

    def sum_6(j):
        arrive("gb", j, 2, (0, 1))
        go("ga", j)

    def sum_7(j):
        arrive("ga", j, 1, (1, 0))
        go("gc", j)

    def sum_8(j):
        arrive("gc", j, 0, (0, 0), 1 - core)

    ring = (peer_c, peer_x, peer_y, peer_z[1], peer_z[2])
    for i, peer in enumerate(ring):
        define("bt", (i,), lambda i=i: small.at[i], lambda i=i: small_far.at[i], peer)

    def small_step(i):
        got("bt", i)
        if i < 4:
            small[i + 1] = small[i] + small_far[i]
            go("bt", i + 1)
        else:
            small_out[...] = small[i] + small_far[i]

    loads = [
        (sum_grad_in, grad),
        (act_in, act),
        (outer_in, weight),
        (slope_in, slope),
        (normed_in, normed),
        (context_in, context),
        (out_proj_in, out_proj),
        (tokens_in, tokens),
        (joint_in, joint),
        (joint_proj_in, joint_proj),
        (inner_in, weight),
    ]

    def load(i):
        return pltpu.make_async_copy(loads[i][0], loads[i][1], load_sem.at[i])

    def fetch(p):
        return pltpu.make_async_copy(
            probs_in.at[pl.ds(2 * p, 2)], probs.at[p % 2], probs_sem.at[p % 2]
        )

    for i in range(10):
        load(i).start()
    fetch(0).start()
    greet(place, side)
    small[0] = small_in[...]
    load(0).wait()
    low[...] = grad[...].astype(bf)
    load(1).wait()

    def outer_group(t):
        base = deep_of[t] * (4 * share)

        def body(i, carry):
            here = pl.ds(pl.multiple_of(base + i * 256, 256), 256)
            outer_sum[here, :] = tn_dot(act[:, here], low[...]).astype(bf)
            return carry

        lax.fori_loop(0, 4 * share // 256, body, 0)
        for y in range(2):
            go("oc", t, y)

    outer_group(3)
    outer_group(2)
    outer_to_x(3)
    outer_group(1)
    outer_to_x(2)
    outer_group(0)
    outer_to_x(1)
    load(2).wait()
    load(3).wait()
    slots = {
        0: [lambda: outer_to_x(0)],
        4: [lambda: outer_to_y(3)],
        9: [lambda: outer_to_y(2)],
        11: [lambda: outer_to_z(3)],
    }

    def at_slot(index, table):
        for slot, todo in table.items():

            @pl.when(index == slot)
            def _(todo=todo):
                for event in todo:
                    event()

    def pre_step(j, carry):
        cols = pl.ds(pl.multiple_of(j * 256, 256), 256)
        for b in range(2):
            rows = slice(b * half, (b + 1) * half)
            back = nt_dot(low[rows, :], weight[cols, :])
            act[rows, cols] = (back * slope[rows, cols].astype(fp)).astype(bf)
        bias_cols = pl.ds(pl.multiple_of((j % 3) * 256, 256), 256)
        small[0, pl.ds(8 + j // 3, 1), bias_cols] = jnp.sum(
            act[:, cols].astype(fp), axis=0, keepdims=True
        )
        at_slot(j, slots)
        return carry

    lax.fori_loop(0, units // 256, pre_step, 0)
    load(10).start()
    load(4).wait()

    def first_step(i, carry):
        rows = pl.ds(pl.multiple_of(i * 128, 128), 128)
        first_low[rows, :] = (normed[rows, :] * first_gain[...] + first_shift[...]).astype(bf)
        return carry

    lax.fori_loop(0, rows_total // 128, first_step, 0)

    def inner_group(t):
        base = deep_of[t] * (4 * share)

        def body(i, carry):
            here = pl.ds(pl.multiple_of(base + i * 256, 256), 256)
            inner_sum[here, :] = tn_dot(act[:, here], first_low[...]).astype(bf)
            return carry

        lax.fori_loop(0, 4 * share // 256, body, 0)
        for y in range(2):
            go("ic", t, y)

    inner_group(3)
    inner_group(2)
    inner_to_y(3)
    outer_to_y(1)
    inner_group(1)
    inner_to_y(2)
    outer_to_z(2)
    inner_group(0)
    inner_to_y(1)
    load(10).wait()
    for j in range(width // 256):
        cols = slice(j * 256, (j + 1) * 256)
        grad[:, cols] += nn_dot(act[...], weight[:, cols])
        if j == 0:
            inner_to_y(0)
        if j == 1:
            outer_to_y(0)
    outer_to_z(1)
    inner_to_z(3)

    def norm_step(i, carry):
        rows = pl.ds(pl.multiple_of(i * 128, 128), 128)
        incoming, unit = grad[rows, :], normed[rows, :]
        small[0, 3:4, :] += jnp.sum(incoming * unit, axis=0, keepdims=True)
        small[0, 4:5, :] += jnp.sum(incoming, axis=0, keepdims=True)
        scaled = incoming * first_gain[...]
        back = scale[rows, :] * (
            scaled
            - jnp.mean(scaled, axis=-1, keepdims=True)
            - unit * jnp.mean(scaled * unit, axis=-1, keepdims=True)
        )
        grad[rows, :] = back
        back_low = back.astype(bf)
        low[rows, :] = back_low
        small[0, 5:6, :] += jnp.sum(back_low.astype(fp), axis=0, keepdims=True)
        return carry

    lax.fori_loop(0, rows_total // 128, norm_step, 0)
    load(5).wait()
    for j in range(width // 256):
        cols = slice(j * 256, (j + 1) * 256)
        parts[0, cols, :] = tn_dot(context[:, cols], low[...]).astype(bf)
    go("ac", 0)
    outer_to_z(0)
    inner_to_z(2)
    load(6).wait()
    for j in range(width // 256):
        cols = slice(j * 256, (j + 1) * 256)
        context_grad[:, cols] = nt_dot(low[...], out_proj[cols, :]).astype(bf) * head_mask[
            :, cols
        ].astype(bf)
    sum_1(0)
    load(7).wait()
    for j in range(width // 128):
        cols = slice(j * 128, (j + 1) * 128)
        tokens_over[cols, :] = tokens[:, cols].T
    inner_to_z(1)
    load(8).wait()
    first_half = (lax.broadcasted_iota(jnp.int32, (1, 128), 1) < DH).astype(bf)
    halves = (first_half, 1 - first_half)
    factor = 1.0 / math.sqrt(DH)
    pairs = HEADS // 2
    pair_slots = {
        0: [lambda: sum_2(0), lambda: inner_to_z(0), outer_end],
        1: [lambda: go("ac", 1), lambda: sum_3(0)],
        2: [lambda: sum_1(1), lambda: sum_4(0), lambda: got("of", 0), inner_end],
        3: [lambda: go("ac", 2), lambda: sum_2(1), lambda: sum_5(0), inner_last],
        4: [lambda: sum_1(2), lambda: sum_3(1), lambda: sum_6(0)],
        5: [
            lambda: go("ac", 3),
            lambda: sum_4(1),
            lambda: sum_2(2),
            lambda: sum_7(0),
            lambda: go("bt", 0),
        ],
    }

    def pair_step(p, carry):
        @pl.when(p + 1 < pairs)
        def _():
            fetch(p + 1).start()

        fetch(p).wait()
        slot = p % 2
        cols = [pl.ds(pl.multiple_of(s * width + p * 128, 128), 128) for s in range(3)]
        out_cols = pl.ds(pl.multiple_of(p * 128, 128), 128)
        keys, values = joint[:, cols[1]], joint[:, cols[2]]
        value_part, key_part = None, None
        for b in range(2):
            lanes = slice(b * half, (b + 1) * half)
            queries, incoming = joint[lanes, cols[0]], context_grad[lanes, out_cols]
            query_part = None
            for a in range(2):
                weights_low = probs[slot, a, :, lanes]
                weights = weights_low.astype(fp)
                product = nt_dot(values * halves[a], incoming) * weights
                score_grad = (
                    product - weights * jnp.sum(product, axis=0, keepdims=True)
                ).astype(bf)
                part = nn_dot(weights_low, incoming * halves[a])
                value_part = part if value_part is None else value_part + part
                part = nn_dot(score_grad, queries * halves[a])
                key_part = part if key_part is None else key_part + part
                part = tn_dot(score_grad, keys * halves[a])
                query_part = part if query_part is None else query_part + part
            joint_grad[lanes, cols[0]] = (query_part * factor).astype(bf)
        joint_grad[:, cols[1]] = (key_part * factor).astype(bf)
        joint_grad[:, cols[2]] = value_part.astype(bf)
        small[0, 6:7, out_cols] = jnp.sum(
            joint_grad[:, cols[0]].astype(fp), axis=0, keepdims=True
        )
        small[0, 7:8, out_cols] = jnp.sum(
            joint_grad[:, cols[2]].astype(fp), axis=0, keepdims=True
        )

        @pl.when(p % 2 == 1)
        def _():
            index = (p + 1) // 2
            for s in range(3):
                source = pl.ds(pl.multiple_of(s * width + (index - 1) * 256, 256), 256)
                parts[index, :, s * 256 : (s + 1) * 256] = nn_dot(
                    tokens_over[...], joint_grad[:, source]
                ).astype(bf)

        at_slot(p, pair_slots)
        return carry

    lax.fori_loop(0, pairs, pair_step, 0)
    load(9).wait()
    between = {
        0: [lambda: sum_1(3), lambda: sum_5(1), lambda: sum_3(2), lambda: small_step(0)],
        1: [lambda: sum_8(0), lambda: small_step(1)],
        2: [lambda: sum_6(1), lambda: sum_4(2), lambda: small_step(2)],
    }
    for j in range(width // 256):
        cols = slice(j * 256, (j + 1) * 256)
        grad[:, cols] += nt_dot(joint_grad[...], joint_proj[cols, :])
        for event in between[j]:
            event()
    result = pltpu.make_async_copy(grad, input_grad, keep_sem.at[4])
    result.start()
    sum_2(3)
    sum_5(2)
    sum_7(1)
    small_step(3)
    sum_3(3)
    sum_6(2)
    small_step(4)
    sum_4(3)
    sum_7(2)
    sum_5(3)
    sum_8(1)
    sum_6(3)
    sum_8(2)
    sum_7(3)
    sum_8(3)
    result.wait()
    for build in made.values():
        build().wait_send()


def run_backward(args, share, units, rows_total, width):
    bf, fp = jnp.bfloat16, jnp.float32
    shape = jax.ShapeDtypeStruct
    vmem = pl.BlockSpec(memory_space=pltpu.VMEM)
    anywhere = pl.BlockSpec(memory_space=pl.ANY)
    third = share // 2
    counts = [
        (4, 2), (4, 2), (4,), (3,), (1,), (4, 2), (4,), (3,), (1,),
        (4,), (4,), (4,), (4, 3), (4, 3), (4,), (4,), (4,), (5,),
    ]
    sems = [pltpu.SemaphoreType.DMA(count) for unused in range(2) for count in counts]
    quarter = width // 2
    return pl.pallas_call(
        backward_kernel,
        out_shape=(
            shape((rows_total, width), fp),
            shape((4, width, width), bf),
            shape((share, width), bf),
            shape((share, width), fp),
            shape((16, width), fp),
        ),
        in_specs=[anywhere] * 12 + [vmem] * 5,
        out_specs=(anywhere, anywhere, vmem, vmem, vmem),
        scratch_shapes=[
            pltpu.VMEM((rows_total, units), bf),
            pltpu.VMEM((rows_total, units), bf),
            pltpu.VMEM((units, width), bf),
            pltpu.VMEM((2, 2, rows_total, rows_total), bf),
            pltpu.VMEM((rows_total, 3 * width), bf),
            pltpu.VMEM((rows_total, width), bf),
            pltpu.VMEM((rows_total, width), fp),
            pltpu.VMEM((rows_total, width), fp),
            pltpu.VMEM((rows_total, width), bf),
            pltpu.VMEM((width, rows_total), bf),
            pltpu.VMEM((width, 3 * width), bf),
            pltpu.VMEM((width, width), bf),
            pltpu.VMEM((rows_total, width), bf),
            pltpu.VMEM((rows_total, width), bf),
            pltpu.VMEM((units, width), bf),
            pltpu.VMEM((units, width), bf),
            pltpu.VMEM((4, 2, share, width), bf),
            pltpu.VMEM((4, 2, third, width), bf),
            pltpu.VMEM((4, third, width), bf),
            pltpu.VMEM((3, third, width), bf),
            pltpu.VMEM((4, 2, share, width), bf),
            pltpu.VMEM((4, share, width), bf),
            pltpu.VMEM((3, share, width), bf),
            pltpu.VMEM((share, width), bf),
            pltpu.VMEM((share, width), bf),
            pltpu.VMEM((4, width, width), bf),
            pltpu.VMEM((4, width, quarter), bf),
            pltpu.VMEM((4, width // 2, quarter), bf),
            pltpu.VMEM((4, width // 4, quarter), bf),
            pltpu.VMEM((4, 3, width // 16, quarter), bf),
            pltpu.VMEM((rows_total, 3 * width), bf),
            pltpu.VMEM((rows_total, width), bf),
            pltpu.VMEM((5, 16, width), fp),
            pltpu.VMEM((5, 16, width), fp),
            pltpu.SemaphoreType.DMA((11,)),
            pltpu.SemaphoreType.DMA((2,)),
            pltpu.SemaphoreType.DMA((5,)),
        ]
        + sems,
        compiler_params=pltpu.CompilerParams(
            collective_id=1, has_side_effects=True, vmem_limit_bytes=64 * 1024 * 1024 - 65536
        ),
        name="backward",
    )(*args)


def on_device_fast(
    tokens,
    joint_proj,
    query_bias,
    value_bias,
    out_proj,
    out_bias,
    first_gain,
    first_shift,
    inner_proj,
    inner_bias,
    outer_proj,
    outer_bias,
    second_gain,
    second_shift,
    segment_ids,
    cls_positions,
    widths,
    out_grad,
):
    tok_rows, model_width = tokens.shape
    seq_rows = cls_positions.shape[0]
    seq_len = tok_rows // seq_rows
    unit_share = inner_proj.shape[1]
    ffn_count = lax.axis_size("ffn")
    tok_count = lax.axis_size("tok")
    ffn_place = lax.axis_index("ffn")
    tok_place = lax.axis_index("tok")
    per_group = seq_rows * ffn_count * tok_count // MB
    batches = jnp.arange(MB, dtype=jnp.int32)
    own_group = (ffn_place * tok_count + tok_place) * seq_rows // per_group
    own_pick = (batches == own_group).astype(jnp.int32)
    heads_kept = jnp.sum(own_pick * widths[:, 1])
    head_on = (jnp.arange(HEADS, dtype=jnp.int32) < heads_kept).astype(jnp.float32)
    factor = 1.0 / math.sqrt(DH)
    unit_total = unit_share * ffn_count
    own_kept = jnp.sum(own_pick * widths[:, 0])
    neuron_on = (jnp.arange(unit_total, dtype=jnp.int32) < own_kept).astype(jnp.float32)
    zero_bias = jnp.zeros((model_width,), jnp.bfloat16)
    joint_bias = jnp.concatenate([query_bias, zero_bias, value_bias]).astype(jnp.float32)
    inner_bias_all = lax.all_gather(inner_bias, "ffn", axis=0, tiled=True).astype(jnp.float32)
    head_mask = jnp.repeat(head_on, DH)
    (
        output, cls_states, inner_rows, outer_rows, probs_again, joint_flat, context_low,
        first_normed, first_scale, act_low, slope_low, sum_grad, small_a,
    ) = run_forward(
        (
            tokens, joint_proj, joint_bias[None], out_proj, out_bias.astype(jnp.float32)[None],
            first_gain[None], first_shift[None], inner_proj.T, outer_proj, inner_bias_all[None],
            outer_bias.astype(jnp.float32)[None], second_gain[None], second_shift[None],
            segment_ids[:, None], segment_ids[None], head_mask[None], neuron_on[None],
            cls_positions, out_grad,
        ),
        unit_share, unit_total, tok_rows, model_width,
    )
    input_grad, summed, outer_part, inner_part, small = run_backward(
        (
            act_low, slope_low, sum_grad, outer_rows, inner_rows, first_normed, joint_flat,
            context_low, probs_again, tokens, joint_proj, out_proj, first_scale, small_a,
            first_gain[None], first_shift[None], head_mask[None],
        ),
        unit_share, unit_total, tok_rows, model_width,
    )
    cls_states = cls_states[None]
    outer_proj_grad = outer_part.astype(jnp.float32)
    inner_proj_grad = inner_part.T
    out_proj_grad = summed[0].astype(jnp.float32)
    joint_proj_grad = (
        summed[1:]
        .astype(jnp.float32)
        .reshape(3, model_width, 3, model_width // 3)
        .transpose(1, 2, 0, 3)
        .reshape(model_width, 3 * model_width)
    )
    second_gain_grad, second_shift_grad, outer_bias_grad = small[0], small[1], small[2]
    first_gain_grad, first_shift_grad, out_bias_grad = small[3], small[4], small[5]
    query_bias_grad, value_bias_grad = small[6], small[7]
    inner_bias_grad = lax.dynamic_slice(
        small[8:12].reshape(-1), (ffn_place * unit_share,), (unit_share,)
    )
    return (
        output,
        cls_states,
        input_grad,
        joint_proj_grad,
        query_bias_grad,
        value_bias_grad,
        out_proj_grad,
        out_bias_grad,
        first_gain_grad,
        first_shift_grad,
        inner_proj_grad,
        inner_bias_grad,
        outer_proj_grad,
        outer_bias_grad,
        second_gain_grad,
        second_shift_grad,
    )


def solution(mesh):
    return jax.shard_map(
        on_device_fast if mesh.shape["ffn"] == 16 and mesh.shape["tok"] == 2 else on_device,
        mesh=mesh,
        in_specs=(
            P(("ffn", "tok"), None),
            P(),
            P(),
            P(),
            P(),
            P(),
            P(),
            P(),
            P(None, "ffn"),
            P("ffn"),
            P("ffn", None),
            P(),
            P(),
            P(),
            P(("ffn", "tok")),
            P(("ffn", "tok"), None),
            P(),
            P(("ffn", "tok"), None),
        ),
        out_specs=(
            P(("ffn", "tok"), None),
            P(("ffn", "tok"), None, None),
            P(("ffn", "tok"), None),
            P(),
            P(),
            P(),
            P(),
            P(),
            P(),
            P(),
            P(None, "ffn"),
            P("ffn"),
            P("ffn", None),
            P(),
            P(),
            P(),
        ),
        check_vma=False,
    )
```

```python
import math

import jax
import jax.numpy as jnp
from jax import lax
from jax.experimental import pallas as pl
from jax.experimental.pallas import tpu as pltpu
from jax.sharding import PartitionSpec as P

MESH = pl.DeviceIdType.MESH
HEADS = 12
DH = 64
MB = 2
SEGS = 4


def normalize(inputs, gain_vec, shift_vec):
    row_mean = jnp.mean(inputs, axis=-1, keepdims=True)
    centred = inputs - row_mean
    row_scale = lax.rsqrt(jnp.mean(centred * centred, axis=-1, keepdims=True) + 1e-12)
    normed = centred * row_scale
    return (normed * gain_vec + shift_vec, normed, row_scale)


def normalize_back(incoming, normed, row_scale, gain_vec):
    gain_grad = jnp.sum(incoming * normed, axis=0)
    shift_grad = jnp.sum(incoming, axis=0)
    scaled_grad = incoming * gain_vec
    inputs_grad = row_scale * (
        scaled_grad
        - jnp.mean(scaled_grad, axis=-1, keepdims=True)
        - normed * jnp.mean(scaled_grad * normed, axis=-1, keepdims=True)
    )
    return (inputs_grad, gain_grad, shift_grad)


def gelu_slope(inputs):
    return (
        0.5 * (1.0 + lax.erf(inputs * 0.7071067811865476))
        + inputs * jnp.exp(-0.5 * inputs * inputs) * 0.3989422804014327
    )


def contract_rows(left_side, right_side):
    return lax.dot_general(
        left_side, right_side, (((0,), (0,)), ((), ())), preferred_element_type=jnp.float32
    )


def contract_cols(left_side, right_side):
    return lax.dot_general(
        left_side, right_side, (((1,), (1,)), ((), ())), preferred_element_type=jnp.float32
    )


def on_device(
    tokens,
    joint_proj,
    query_bias,
    value_bias,
    out_proj,
    out_bias,
    first_gain,
    first_shift,
    inner_proj,
    inner_bias,
    outer_proj,
    outer_bias,
    second_gain,
    second_shift,
    segment_ids,
    cls_positions,
    widths,
    out_grad,
):
    tok_rows, model_width = tokens.shape
    seq_rows = cls_positions.shape[0]
    seq_len = tok_rows // seq_rows
    unit_share = inner_proj.shape[1]
    ffn_count = lax.axis_size("ffn")
    tok_count = lax.axis_size("tok")
    ffn_place = lax.axis_index("ffn")
    tok_place = lax.axis_index("tok")
    per_group = seq_rows * ffn_count * tok_count // MB
    batches = jnp.arange(MB, dtype=jnp.int32)
    own_group = (ffn_place * tok_count + tok_place) * seq_rows // per_group
    own_pick = (batches == own_group).astype(jnp.int32)
    heads_kept = jnp.sum(own_pick * widths[:, 1])
    head_on = (jnp.arange(HEADS, dtype=jnp.int32) < heads_kept).astype(jnp.float32)
    factor = 1.0 / math.sqrt(DH)
    zero_bias = jnp.zeros((model_width,), jnp.bfloat16)
    joint_bias = jnp.concatenate([query_bias, zero_bias, value_bias])
    joint_low = (
        jnp.dot(tokens, joint_proj, preferred_element_type=jnp.float32) + joint_bias
    ).astype(jnp.bfloat16)
    joint_low = joint_low.reshape(seq_rows, seq_len, 3, HEADS, DH)
    queries = joint_low[:, :, 0]
    key_heads = joint_low[:, :, 1]
    value_heads = joint_low[:, :, 2]
    segments = segment_ids.reshape(seq_rows, seq_len)
    same_doc = (segments[:, :, None] == segments[:, None, :])[:, None]

    def scores_of(query_rows, key_rows):
        raw_scores = (
            jnp.einsum("rqhd,rkhd->rhqk", query_rows, key_rows, preferred_element_type=jnp.float32)
            * factor
        )
        return jnp.where(same_doc, raw_scores, -1e30)

    scores = scores_of(queries, key_heads)
    row_peak = jnp.max(scores, axis=-1, keepdims=True)
    log_total = row_peak + jnp.log(jnp.sum(jnp.exp(scores - row_peak), axis=-1, keepdims=True))
    probs_low = jnp.exp(scores - log_total).astype(jnp.bfloat16)
    context = (
        jnp.einsum("rhqk,rkhd->rqhd", probs_low, value_heads, preferred_element_type=jnp.float32)
        * head_on[:, None]
    )
    context_low = context.astype(jnp.bfloat16).reshape(tok_rows, model_width)
    attn_out = jnp.dot(context_low, out_proj, preferred_element_type=jnp.float32) + out_bias
    first_out, first_normed, first_scale = normalize(
        tokens.astype(jnp.float32) + attn_out, first_gain, first_shift
    )
    first_low = first_out.astype(jnp.bfloat16)
    unit_total = unit_share * ffn_count
    stacked = lax.all_gather(
        jnp.stack([inner_proj.T, outer_proj]), "ffn", axis=1, tiled=True
    )
    inner_rows, outer_rows = stacked[0], stacked[1]
    inner_bias_all = lax.all_gather(inner_bias, "ffn", axis=0, tiled=True)
    own_kept = jnp.sum(own_pick * widths[:, 0])
    neuron_on = (jnp.arange(unit_total, dtype=jnp.int32) < own_kept).astype(jnp.float32)
    pre_act = contract_cols(first_low, inner_rows) + inner_bias_all
    act_low = (jax.nn.gelu(pre_act, approximate=False) * neuron_on).astype(jnp.bfloat16)
    ffn_out = jnp.dot(act_low, outer_rows, preferred_element_type=jnp.float32) + outer_bias
    second_out, second_normed, second_scale = normalize(
        first_out + ffn_out, second_gain, second_shift
    )
    output = second_out.astype(jnp.bfloat16)
    cls_states = jnp.take_along_axis(
        second_out.reshape(seq_rows, seq_len, model_width), cls_positions[:, :, None], axis=1
    )
    sum_grad, second_gain_grad, second_shift_grad = normalize_back(
        out_grad.astype(jnp.float32), second_normed, second_scale, second_gain
    )
    ffn_grad = sum_grad.astype(jnp.bfloat16)
    outer_bias_grad = jnp.sum(ffn_grad.astype(jnp.float32), axis=0)
    outer_proj_grad = contract_rows(act_low, ffn_grad)
    act_grad = contract_cols(ffn_grad, outer_rows)
    pre_grad = (act_grad * (gelu_slope(pre_act) * neuron_on)).astype(jnp.bfloat16)
    inner_bias_sum = jnp.sum(pre_grad.astype(jnp.float32), axis=0)
    inner_rows_grad = contract_rows(pre_grad, first_low)
    first_back = jnp.dot(pre_grad, inner_rows, preferred_element_type=jnp.float32)
    unit_grads = jnp.stack(
        [inner_rows_grad.astype(jnp.bfloat16), outer_proj_grad.astype(jnp.bfloat16)]
    )
    unit_grads = lax.psum_scatter(unit_grads, "ffn", scatter_dimension=1, tiled=True)
    unit_grads = lax.psum(unit_grads, "tok").astype(jnp.float32)
    inner_proj_grad, outer_proj_grad = unit_grads[0].T, unit_grads[1]
    first_grad = sum_grad + first_back
    attn_sum_grad, first_gain_grad, first_shift_grad = normalize_back(
        first_grad, first_normed, first_scale, first_gain
    )
    attn_grad = attn_sum_grad.astype(jnp.bfloat16)
    out_bias_grad = jnp.sum(attn_grad.astype(jnp.float32), axis=0)
    out_proj_grad = contract_rows(context_low, attn_grad)
    context_grad = (
        contract_cols(attn_grad, out_proj)
        .astype(jnp.bfloat16)
        .reshape(seq_rows, seq_len, HEADS, DH)
    )
    context_grad = context_grad * head_on.astype(jnp.bfloat16)[:, None]
    scores = scores_of(queries, key_heads)
    probs = jnp.exp(scores - log_total)
    probs_again = probs.astype(jnp.bfloat16)
    value_part = jnp.einsum(
        "rhqk,rqhd->rkhd", probs_again, context_grad, preferred_element_type=jnp.float32
    )
    prob_grad = jnp.einsum(
        "rqhd,rkhd->rhqk", context_grad, value_heads, preferred_element_type=jnp.float32
    )
    score_grad = (probs * (prob_grad - jnp.sum(probs * prob_grad, axis=-1, keepdims=True))).astype(
        jnp.bfloat16
    )
    query_part = (
        jnp.einsum("rhqk,rkhd->rqhd", score_grad, key_heads, preferred_element_type=jnp.float32)
        * factor
    )
    key_part = (
        jnp.einsum("rhqk,rqhd->rkhd", score_grad, queries, preferred_element_type=jnp.float32)
        * factor
    )
    joint_grad = (
        jnp.stack([query_part, key_part, value_part], axis=2)
        .astype(jnp.bfloat16)
        .reshape(tok_rows, 3 * model_width)
    )
    joint_bias_grad = jnp.sum(joint_grad.astype(jnp.float32), axis=0)
    query_bias_grad = joint_bias_grad[:model_width]
    value_bias_grad = joint_bias_grad[2 * model_width :]
    joint_proj_grad = contract_rows(tokens, joint_grad)
    input_grad = attn_sum_grad + contract_cols(joint_grad, joint_proj)
    joint_proj_grad, out_proj_grad = lax.psum(
        (joint_proj_grad.astype(jnp.bfloat16), out_proj_grad.astype(jnp.bfloat16)),
        ("ffn", "tok"),
    )
    joint_proj_grad = joint_proj_grad.astype(jnp.float32)
    out_proj_grad = out_proj_grad.astype(jnp.float32)
    small = [
        query_bias_grad,
        value_bias_grad,
        out_bias_grad,
        first_gain_grad,
        first_shift_grad,
        outer_bias_grad,
        second_gain_grad,
        second_shift_grad,
        inner_bias_sum,
    ]
    small = lax.psum(jnp.concatenate(small), ("ffn", "tok"))
    (
        query_bias_grad,
        value_bias_grad,
        out_bias_grad,
        first_gain_grad,
        first_shift_grad,
        outer_bias_grad,
        second_gain_grad,
        second_shift_grad,
    ) = [small[i * model_width : (i + 1) * model_width] for i in range(8)]
    inner_bias_grad = lax.dynamic_slice(
        small, (8 * model_width + ffn_place * unit_share,), (unit_share,)
    )
    return (
        output,
        cls_states,
        input_grad,
        joint_proj_grad,
        query_bias_grad,
        value_bias_grad,
        out_proj_grad,
        out_bias_grad,
        first_gain_grad,
        first_shift_grad,
        inner_proj_grad,
        inner_bias_grad,
        outer_proj_grad,
        outer_bias_grad,
        second_gain_grad,
        second_shift_grad,
    )


def x_or1(v):
    return v + 1 - 2 * (v % 2)


def x_or2(v):
    return v + 2 - 4 * ((v // 2) % 2)


def z_peer(place, turn):
    deep = place // 4
    if turn & 1:
        deep = x_or1(deep)
    if turn & 2:
        deep = x_or2(deep)
    return deep * 4 + place % 4


def y_peer(place):
    return (place // 4) * 4 + ((place // 2 + 1) % 2) * 2 + place % 2


def c_peer(place):
    return x_or1(place)


def nt_dot(left_side, right_side):
    return lax.dot_general(
        left_side, right_side, (((1,), (1,)), ((), ())), preferred_element_type=jnp.float32
    )


def tn_dot(left_side, right_side):
    return lax.dot_general(
        left_side, right_side, (((0,), (0,)), ((), ())), preferred_element_type=jnp.float32
    )


def nn_dot(left_side, right_side):
    return lax.dot_general(
        left_side, right_side, (((1,), (0,)), ((), ())), preferred_element_type=jnp.float32
    )


def greet(place, side):
    barrier = pltpu.get_barrier_semaphore()
    peers = [
        (z_peer(place, 1), side),
        (z_peer(place, 2), side),
        (z_peer(place, 3), side),
        (y_peer(place), side),
        (c_peer(place), side),
        (place, 1 - side),
    ]
    for peer in peers:
        pl.semaphore_signal(barrier, inc=1, device_id=peer, device_id_type=MESH)
    pl.semaphore_wait(barrier, 6)


def remote(source, target, send_sem, recv_sem, device):
    return pltpu.make_async_remote_copy(
        src_ref=source,
        dst_ref=target,
        send_sem=send_sem,
        recv_sem=recv_sem,
        device_id=device,
        device_id_type=MESH,
    )


class Spread:
    def __init__(self, own, whole, place, side, rows, sems):
        self.own, self.whole, self.place, self.side, self.rows = own, whole, place, side, rows
        self.up_s, self.up_r, self.dn_s, self.dn_r, self.y_s, self.y_r = sems[:6]
        self.x_s, self.x_r, self.c_s, self.c_r, self.d_s, self.d_r = sems[6:]
        self.third = rows // 3
        self.deep = place // 4

    def span(self, source, offset, count):
        start = pl.multiple_of(source * self.rows + offset, 16)
        return self.whole.at[pl.ds(start, count)]

    def slab(self, source):
        return self.span(source, self.side * self.third, 2 * self.third)

    def edge(self, source, mine=True):
        side = self.side if mine else 1 - self.side
        return self.span(source, side * 2 * self.third, self.third)

    def own_slab(self):
        start = pl.multiple_of(self.side * self.third, 16)
        return self.own.at[pl.ds(start, 2 * self.third)]

    def source_of(self, step, up, cross=False):
        base = y_peer(self.place) if cross else self.place
        if step is None:
            return base
        return base - 4 * (step + 1) if up else base + 4 * (step + 1)

    def has(self, step, up):
        if step is None:
            return None
        return self.deep >= step + 1 if up else self.deep + step + 1 <= 3

    def hop(self, step, up, first=False):
        source = self.place if step == 0 else self.source_of(step - 1, up)
        piece = self.own_slab() if step == 0 else self.slab(source)
        send, recv = (self.up_s, self.up_r) if up else (self.dn_s, self.dn_r)
        device = (self.place + 4 if up else self.place - 4, self.side)
        return remote(piece, self.slab(source), send.at[step], recv.at[step], device)

    def hop_in(self, step, up):
        source = self.source_of(step, up)
        send, recv = (self.up_s, self.up_r) if up else (self.dn_s, self.dn_r)
        return remote(
            self.slab(source), self.slab(source), send.at[step], recv.at[step], (self.place, 1 - self.side)
        )

    def over_y(self, source, own=False):
        index = source // 4
        piece = self.own_slab() if own else self.slab(source)
        return remote(
            piece, self.slab(source), self.y_s.at[index], self.y_r.at[index], (y_peer(self.place), self.side)
        )

    def over_x(self, source, mine=True):
        index = source // 2
        piece = self.edge(source, mine)
        return remote(
            piece, piece, self.x_s.at[index], self.x_r.at[index], (self.place, 1 - self.side)
        )

    def over_c(self, source):
        index = source // 2
        return remote(
            self.slab(source),
            self.slab(source),
            self.c_s.at[index],
            self.c_r.at[index],
            (c_peer(self.place), self.side),
        )

    def over_d(self, source):
        index = source // 2
        piece = self.edge(source, False)
        return remote(piece, piece, self.d_s.at[index], self.d_r.at[index], (c_peer(self.place), self.side))

    def over_own(self):
        index = self.place // 2
        return remote(
            self.own,
            self.span(self.place, 0, self.rows),
            self.c_s.at[index],
            self.c_r.at[index],
            (c_peer(self.place), self.side),
        )

    def start(self):
        @pl.when(self.deep < 3)
        def _():
            self.hop(0, True).start()

        @pl.when(self.deep > 0)
        def _():
            self.hop(0, False).start()

        self.over_y(self.place, own=True).start()
        self.over_own().start()

    def z_event(self, step):
        for up in (True, False):

            @pl.when(self.has(step, up))
            def _(up=up):
                source = self.source_of(step, up)
                self.hop_in(step, up).wait_recv()
                if step < 2:

                    @pl.when(self.deep < 3 if up else self.deep > 0)
                    def _():
                        self.hop(step + 1, up).start()

                self.over_y(source).start()
                self.over_x(source).start()
                self.over_c(source).start()

    def each(self, step, work):
        if step is None:
            work(True)
            return
        for up in (True, False):

            @pl.when(self.has(step, up))
            def _(up=up):
                work(up)

    def y_event(self, step):
        def work(up):
            source = self.source_of(step, up, cross=True)
            self.over_y(source).wait_recv()
            self.over_x(source).start()
            self.over_c(source).start()

        self.each(step, work)

    def x_event(self, step, cross):
        def work(up):
            source = self.source_of(step, up, cross=cross)
            self.over_x(source, False).wait_recv()
            self.over_d(source).start()

        self.each(step, work)

    def finish(self):
        other = c_peer(self.place) % 2
        own = c_peer(self.place)
        for index in range(8):
            source = 2 * index + other

            @pl.when(source != own)
            def _(source=source):
                self.over_c(source).wait_recv()
                self.over_d(source).wait_recv()

            @pl.when(source == own)
            def _(source=source):
                remote(
                    self.own,
                    self.span(source, 0, self.rows),
                    self.c_s.at[index],
                    self.c_r.at[index],
                    (c_peer(self.place), self.side),
                ).wait_recv()

    def drain(self):
        for up in (True, False):
            for step in range(3):
                limit = self.deep < 3 if up else self.deep > 0
                if step > 0:
                    limit = jnp.logical_and(limit, self.has(step - 1, up))

                @pl.when(limit)
                def _(step=step, up=up):
                    self.hop(step, up).wait_send()

        for index in range(4):
            source = 4 * index + self.place % 4
            self.over_y(source).wait_send()
        mine = self.place % 2
        for index in range(8):
            source = 2 * index + mine

            @pl.when(source != self.place)
            def _(source=source):
                self.over_x(source).wait_send()
                self.over_c(source).wait_send()
                self.over_d(source).wait_send()

            @pl.when(source == self.place)
            def _():
                self.over_own().wait_send()


def row_of(vector):
    return vector[...].astype(jnp.float32).reshape(1, vector.shape[0])


def kept_of(widths, place, side, kind):
    return widths[(place * 2 + side) * MB // 32, kind]


def first_lanes(count, start, kept):
    lane = lax.broadcasted_iota(jnp.int32, (1, count), 1) + start
    return jnp.where(lane < kept, 1.0, 0.0)


def forward_kernel(
    tokens,
    joint_proj,
    query_bias,
    value_bias,
    out_proj,
    out_bias,
    first_gain,
    first_shift,
    inner_own,
    outer_own,
    bias_own,
    outer_bias,
    second_gain,
    second_shift,
    seg_over,
    widths,
    cls_at,
    out_grad,
    output,
    cls_out,
    inner_out,
    outer_out,
    probs_out,
    joint_out,
    context_out,
    normed_out,
    scale_out,
    act_out,
    slope_out,
    sum_grad_out,
    small_out,
    inner_all,
    outer_all,
    probs,
    joint,
    context,
    mask_bias,
    act,
    slope,
    first_low,
    wide,
    bias_all,
    inner_bias,
    joint_bias,
    save_sem,
    bias_send,
    bias_recv,
    *sems,
):
    place, side = lax.axis_index("ffn"), lax.axis_index("tok")
    out_bias, outer_bias = row_of(out_bias), row_of(outer_bias)
    first_gain, first_shift = row_of(first_gain), row_of(first_shift)
    second_gain, second_shift = row_of(second_gain), row_of(second_shift)
    rows_total = tokens.shape[0]
    units = inner_all.shape[0]
    share = inner_own.shape[0]
    width = tokens.shape[1]
    half = rows_total // 2
    kept_units = kept_of(widths, place, side, 0)
    own_bias = pltpu.make_async_copy(bias_own, bias_all.at[place], save_sem.at[12])
    own_bias.start()
    joint_bias[:, 0:width] = row_of(query_bias)
    joint_bias[:, width : 2 * width] = jnp.zeros((1, width), jnp.float32)
    joint_bias[:, 2 * width :] = row_of(value_bias)
    own_bias.wait()

    def bias_hop(step):
        peer = (c_peer(place), y_peer(place), z_peer(place, 1), z_peer(place, 2))[step]
        count = 1 << step
        piece = bias_all.at[pl.ds(place // count * count, count)]
        return remote(piece, piece, bias_send.at[step], bias_recv.at[step], (peer, side))

    def bias_event(step):
        bias_hop(step - 1).wait_recv()
        if step < 4:
            bias_hop(step).start()

    greet(place, side)
    inner = Spread(inner_own, inner_all, place, side, share, sems[:12])
    outer = Spread(outer_own, outer_all, place, side, share, sems[12:])
    inner.start()
    outer.start()
    bias_hop(0).start()
    own_rows = pl.ds(pl.multiple_of(place * share, 16), share)
    inner_all[own_rows, :] = inner_own[...]
    outer_all[own_rows, :] = outer_own[...]
    saves = []

    def save(source, target, index):
        pltpu.make_async_copy(source, target, save_sem.at[index]).start()
        saves.append((source, target, index))

    kind = lax.broadcasted_iota(jnp.int32, (128, rows_total), 0)
    kinds = jnp.where(kind == seg_over[...], 1.0, 0.0).astype(jnp.bfloat16)
    for b in range(2):
        lanes = slice(b * half, (b + 1) * half)
        mask_bias[:, lanes] = jnp.where(tn_dot(kinds, kinds[:, lanes]) > 0.5, 0.0, -1e30)

    def joint_step(j, carry):
        cols = pl.ds(pl.multiple_of(j * 256, 256), 256)
        joint[:, cols] = (nn_dot(tokens[...], joint_proj[:, cols]) + joint_bias[:, cols]).astype(
            jnp.bfloat16
        )
        return carry

    lax.fori_loop(0, 3 * width // 256, joint_step, 0)
    save(joint, joint_out, 0)
    events = [
        lambda: inner.z_event(0),
        lambda: outer.z_event(0),
        lambda: inner.y_event(None),
        lambda: inner.z_event(1),
        lambda: outer.y_event(None),
        lambda: inner.y_event(0),
        lambda: outer.z_event(1),
        lambda: inner.x_event(0, False),
        lambda: inner.x_event(None, True),
        lambda: outer.y_event(0),
        lambda: inner.z_event(2),
        lambda: outer.x_event(0, False),
        lambda: outer.x_event(None, True),
        lambda: inner.y_event(1),
        lambda: outer.z_event(2),
        lambda: inner.x_event(1, False),
        lambda: inner.x_event(0, True),
        lambda: outer.y_event(1),
        lambda: inner.y_event(2),
        lambda: outer.x_event(1, False),
        lambda: outer.x_event(0, True),
        lambda: inner.x_event(2, False),
        lambda: inner.x_event(1, True),
        lambda: outer.y_event(2),
        lambda: inner.x_event(2, True),
        lambda: outer.x_event(2, False),
        lambda: outer.x_event(1, True),
        lambda: outer.x_event(2, True),
    ]
    events[0]()
    bias_event(1)
    slots = {0: events[1:4], 1: events[4:6], 2: events[6:10], 3: events[10:14], 4: events[14:18], 5: events[18:22]}
    slots[0].append(lambda: bias_event(2))
    slots[2].append(lambda: bias_event(3))
    slots[4].append(lambda: bias_event(4))
    first_half = (lax.broadcasted_iota(jnp.int32, (1, 128), 1) < DH).astype(jnp.bfloat16)
    halves = (first_half, 1 - first_half)
    factor = 1.4426950408889634 / math.sqrt(DH)
    pairs = HEADS // 2

    def pair_step(p, carry):
        cols = [pl.ds(pl.multiple_of(s * width + p * 128, 128), 128) for s in range(3)]
        out_cols = pl.ds(pl.multiple_of(p * 128, 128), 128)
        keys, values = joint[:, cols[1]], joint[:, cols[2]]
        for b in range(2):
            lanes = slice(b * half, (b + 1) * half)
            queries = joint[lanes, cols[0]]
            total = None
            for a in range(2):
                scores = nt_dot(keys * halves[a], queries) * factor + mask_bias[:, lanes]
                weights = jnp.exp2(scores - jnp.max(scores, axis=0, keepdims=True))
                weights = weights * (1.0 / jnp.sum(weights, axis=0, keepdims=True))
                low = weights.astype(jnp.bfloat16)
                probs[2 * p + a, :, lanes] = low
                part = tn_dot(low, values * halves[a])
                total = part if total is None else total + part
            context[lanes, out_cols] = (
                total * first_lanes(128, p * 128, kept_of(widths, place, side, 1) * DH)
            ).astype(jnp.bfloat16)
        pltpu.make_async_copy(
            probs.at[pl.ds(2 * p, 2)], probs_out.at[pl.ds(2 * p, 2)], save_sem.at[6 + p]
        ).start()
        for slot, todo in slots.items():

            @pl.when(p == slot)
            def _(todo=todo):
                for event in todo:
                    event()

        return carry

    lax.fori_loop(0, pairs, pair_step, 0)
    save(context, context_out, 1)
    for j in range(width // 256):
        cols = slice(j * 256, (j + 1) * 256)
        wide[:, cols] = nn_dot(context[...], out_proj[:, cols])

    def first_norm(i, carry):
        rows = pl.ds(pl.multiple_of(i * 128, 128), 128)
        total = tokens[rows, :].astype(jnp.float32) + (wide[rows, :] + out_bias)
        centred = total - jnp.mean(total, axis=-1, keepdims=True)
        scale = lax.rsqrt(jnp.mean(centred * centred, axis=-1, keepdims=True) + 1e-12)
        normed = centred * scale
        normed_out[rows, :] = normed
        scale_out[rows, :] = scale
        first_low[rows, :] = (normed * first_gain + first_shift).astype(jnp.bfloat16)
        return carry

    lax.fori_loop(0, rows_total // 128, first_norm, 0)
    for event in events[22:25]:
        event()
    for q in range(units // (2 * share)):
        inner_bias[:, q * 2 * share : (q + 1) * 2 * share] = (
            bias_all[2 * q, 0:1, :] + bias_all[2 * q + 1, 0:1, :]
        )
    inner.finish()
    save(inner_all, inner_out, 2)
    unit_slots = {0: events[25:26], 3: events[26:27], 6: events[27:]}

    def unit_step(j, carry):
        cols = pl.ds(pl.multiple_of(j * 256, 256), 256)
        for b in range(2):
            rows = slice(b * half, (b + 1) * half)
            pre = nt_dot(first_low[rows, :], inner_all[cols, :]) + inner_bias[:, cols]
            gate = 0.5 + 0.5 * lax.erf(pre * 0.7071067811865476)
            on = first_lanes(256, j * 256, kept_units)
            act[rows, cols] = (pre * gate * on).astype(jnp.bfloat16)
            slope[rows, cols] = (
                (gate + pre * jnp.exp(-0.5 * pre * pre) * 0.3989422804014327) * on
            ).astype(jnp.bfloat16)
        for slot, todo in unit_slots.items():

            @pl.when(j == slot)
            def _(todo=todo):
                for event in todo:
                    event()

        return carry

    lax.fori_loop(0, units // 256, unit_step, 0)
    save(act, act_out, 3)
    save(slope, slope_out, 4)
    outer.finish()
    save(outer_all, outer_out, 5)
    for j in range(width // 256):
        cols = slice(j * 256, (j + 1) * 256)
        wide[:, cols] = nn_dot(act[...], outer_all[:, cols])
    small_out[...] = jnp.zeros_like(small_out)

    def second_norm(i, carry):
        rows = pl.ds(pl.multiple_of(i * 128, 128), 128)
        first = normed_out[rows, :] * first_gain + first_shift
        total = first + (wide[rows, :] + outer_bias)
        centred = total - jnp.mean(total, axis=-1, keepdims=True)
        scale = lax.rsqrt(jnp.mean(centred * centred, axis=-1, keepdims=True) + 1e-12)
        normed = centred * scale
        second = normed * second_gain + second_shift
        wide[rows, :] = second
        output[rows, :] = second.astype(jnp.bfloat16)
        grad = out_grad[rows, :].astype(jnp.float32)
        scaled = grad * second_gain
        back = scale * (
            scaled
            - jnp.mean(scaled, axis=-1, keepdims=True)
            - normed * jnp.mean(scaled * normed, axis=-1, keepdims=True)
        )
        sum_grad_out[rows, :] = back
        low = back.astype(jnp.bfloat16).astype(jnp.float32)
        small_out[0:1, :] += jnp.sum(grad * normed, axis=0, keepdims=True)
        small_out[1:2, :] += jnp.sum(grad, axis=0, keepdims=True)
        small_out[2:3, :] += jnp.sum(low, axis=0, keepdims=True)
        return carry

    lax.fori_loop(0, rows_total // 128, second_norm, 0)
    for j in range(SEGS):
        cls_out[j : j + 1, :] = wide[pl.ds(cls_at[0, j], 1), :]
    inner.drain()
    outer.drain()
    for step in range(4):
        bias_hop(step).wait_send()
    for source, target, index in saves:
        pltpu.make_async_copy(source, target, save_sem.at[index]).wait()
    for p in range(pairs):
        pltpu.make_async_copy(
            probs.at[pl.ds(2 * p, 2)], probs_out.at[pl.ds(2 * p, 2)], save_sem.at[6 + p]
        ).wait()


def run_forward(args, share, units, rows_total, width):
    sems = []
    for unused in range(2):
        for count in (3, 3, 3, 3, 4, 4, 8, 8, 8, 8, 8, 8):
            sems.append(pltpu.SemaphoreType.DMA((count,)))
    bf, fp = jnp.bfloat16, jnp.float32
    shape = jax.ShapeDtypeStruct
    vmem = pl.BlockSpec(memory_space=pltpu.VMEM)
    anywhere = pl.BlockSpec(memory_space=pl.ANY)
    smem = pl.BlockSpec(memory_space=pltpu.SMEM)
    in_specs = [vmem] * 15 + [smem, smem, vmem]
    return pl.pallas_call(
        forward_kernel,
        out_shape=(
            shape((rows_total, width), bf),
            shape((SEGS, width), fp),
            shape((units, width), bf),
            shape((units, width), bf),
            shape((HEADS, rows_total, rows_total), bf),
            shape((rows_total, 3 * width), bf),
            shape((rows_total, width), bf),
            shape((rows_total, width), fp),
            shape((rows_total, 1), fp),
            shape((rows_total, units), bf),
            shape((rows_total, units), bf),
            shape((rows_total, width), fp),
            shape((16, width), fp),
        ),
        in_specs=in_specs,
        out_specs=(
            vmem, vmem, anywhere, anywhere, anywhere, anywhere, anywhere, vmem, vmem, anywhere, anywhere, vmem, vmem,
        ),
        scratch_shapes=[
            pltpu.VMEM((units, width), bf),
            pltpu.VMEM((units, width), bf),
            pltpu.VMEM((HEADS, rows_total, rows_total), bf),
            pltpu.VMEM((rows_total, 3 * width), bf),
            pltpu.VMEM((rows_total, width), bf),
            pltpu.VMEM((rows_total, rows_total), fp),
            pltpu.VMEM((rows_total, units), bf),
            pltpu.VMEM((rows_total, units), bf),
            pltpu.VMEM((rows_total, width), bf),
            pltpu.VMEM((rows_total, width), fp),
            pltpu.VMEM((units // share, 8, 2 * share), fp),
            pltpu.VMEM((1, units), fp),
            pltpu.VMEM((1, 3 * width), fp),
            pltpu.SemaphoreType.DMA((7 + HEADS // 2,)),
            pltpu.SemaphoreType.DMA((4,)),
            pltpu.SemaphoreType.DMA((4,)),
        ]
        + sems,
        compiler_params=pltpu.CompilerParams(
            collective_id=0, has_side_effects=True, vmem_limit_bytes=64 * 1024 * 1024 - 65536
        ),
        name="forward",
    )(*args)


def backward_kernel(
    act_in,
    slope_in,
    sum_grad_in,
    outer_in,
    inner_in,
    normed_in,
    joint_in,
    context_in,
    probs_in,
    tokens_in,
    joint_proj_in,
    out_proj_in,
    scale,
    small_in,
    first_gain,
    first_shift,
    widths,
    input_grad,
    summed_out,
    outer_grad,
    inner_grad,
    small_out,
    act,
    slope,
    weight,
    probs,
    joint,
    context,
    normed,
    grad,
    tokens,
    tokens_over,
    joint_proj,
    out_proj,
    low,
    first_low,
    outer_sum,
    inner_sum,
    outer_c,
    outer_x,
    outer_y,
    outer_z,
    inner_c,
    inner_y,
    inner_z,
    inner_own,
    inner_far,
    parts,
    part_c,
    part_a,
    part_b,
    part_z,
    joint_grad,
    context_grad,
    small,
    small_far,
    load_sem,
    probs_sem,
    keep_sem,
    *sems,
):
    place, side = lax.axis_index("ffn"), lax.axis_index("tok")
    core, flank, deep = place % 2, (place // 2) % 2, place // 4
    first_gain, first_shift = row_of(first_gain), row_of(first_shift)
    kept_lanes = kept_of(widths, place, side, 1) * DH
    rows_total, units = act.shape
    width = grad.shape[1]
    half = rows_total // 2
    share = inner_own.shape[0]
    bf, fp = jnp.bfloat16, jnp.float32
    sem_names = (
        "oc", "ox", "oy", "oz", "of", "ic", "iy", "iz", "ix", "ac", "aa", "ab", "az", "gz", "gb", "ga", "gc", "bt"
    )
    send = dict(zip(sem_names, sems[: len(sem_names)]))
    recv = dict(zip(sem_names, sems[len(sem_names) :]))
    made = {}

    def define(name, index, source, target, device):
        made[(name,) + index] = lambda: remote(
            source(), target(), send[name].at[index], recv[name].at[index], device
        )

    def go(name, *index):
        made[(name,) + index]().start()

    def got(name, *index):
        made[(name,) + index]().wait_recv()

    peer_x, peer_y, peer_c = (place, 1 - side), (y_peer(place), side), (c_peer(place), side)
    peer_z = [None] + [(z_peer(place, turn), side) for turn in (1, 2, 3)]
    deep_of = [z_peer(place, turn) // 4 if turn else deep for turn in range(4)]
    third = share // 2

    def shard(turn, y, c, offset=0, count=None):
        start = ((deep_of[turn] * 2 + y) * 2 + c) * share + offset
        return pl.ds(pl.multiple_of(start, 16), share if count is None else count)

    for t in range(4):
        for y in range(2):
            define(
                "oc", (t, y), lambda t=t, y=y: outer_sum.at[shard(t, y, 1 - core)], lambda t=t, y=y: outer_c.at[t, y], peer_c
            )
            define(
                "ic", (t, y), lambda t=t, y=y: inner_sum.at[shard(t, y, 1 - core)], lambda t=t, y=y: inner_c.at[t, y], peer_c
            )
            define(
                "ox",
                (t, y),
                lambda t=t, y=y: outer_sum.at[shard(t, y, core, (1 - side) * third, third)],
                lambda t=t, y=y: outer_x.at[t, y],
                peer_x,
            )
        define(
            "oy",
            (t,),
            lambda t=t: outer_sum.at[shard(t, 1 - flank, core, side * third, third)],
            lambda t=t: outer_y.at[t],
            peer_y,
        )
        define(
            "iy", (t,), lambda t=t: inner_sum.at[shard(t, 1 - flank, core)], lambda t=t: inner_y.at[t], peer_y
        )
        if t:
            define(
                "oz",
                (t - 1,),
                lambda t=t: outer_sum.at[shard(t, flank, core, side * third, third)],
                lambda t=t: outer_z.at[t - 1],
                peer_z[t],
            )
            define(
                "iz",
                (t - 1,),
                lambda t=t: inner_sum.at[shard(t, flank, core)],
                lambda t=t: inner_z.at[t - 1],
                peer_z[t],
            )
    own_part = pl.ds(pl.multiple_of(side * third, 16), third)
    define("of", (0,), lambda: outer_grad.at[own_part], lambda: outer_grad.at[own_part], peer_x)
    define("ix", (0,), lambda: inner_own, lambda: inner_far, peer_x)

    def add(target, source):
        target[...] = (target[...].astype(fp) + source[...].astype(fp)).astype(bf)

    def outer_to_x(t):
        for y in range(2):
            got("oc", t, y)
            add(outer_sum.at[shard(t, y, core)], outer_c.at[t, y])
            go("ox", t, y)

    def outer_to_y(t):
        for y in range(2):
            got("ox", t, y)
            add(outer_sum.at[shard(t, y, core, side * third, third)], outer_x.at[t, y])
        go("oy", t)

    def outer_to_z(t):
        got("oy", t)
        add(outer_sum.at[shard(t, flank, core, side * third, third)], outer_y.at[t])
        if t:
            go("oz", t - 1)

    def outer_end():
        total = outer_sum[shard(0, flank, core, side * third, third), :].astype(fp)
        for t in range(3):
            got("oz", t)
            total = total + outer_z[t].astype(fp)
        outer_grad[own_part, :] = total.astype(bf)
        go("of", 0)

    def inner_to_y(t):
        for y in range(2):
            got("ic", t, y)
            add(inner_sum.at[shard(t, y, core)], inner_c.at[t, y])
        go("iy", t)

    def inner_to_z(t):
        got("iy", t)
        add(inner_sum.at[shard(t, flank, core)], inner_y.at[t])
        if t:
            go("iz", t - 1)

    def inner_end():
        total = inner_sum[shard(0, flank, core), :].astype(fp)
        for t in range(3):
            got("iz", t)
            total = total + inner_z[t].astype(fp)
        inner_own[...] = total.astype(bf)
        go("ix", 0)

    def inner_last():
        got("ix", 0)
        inner_grad[...] = inner_own[...].astype(fp) + inner_far[...].astype(fp)

    quarter = width // 2

    def cols_of(c):
        return pl.ds(pl.multiple_of(c * quarter, 128), quarter)

    def rows_of(j, depth, flips=(0, 0), z=None):
        first, second = (side, flank) if j % 2 == 0 else (flank, side)
        if flips[0]:
            first = 1 - first
        if flips[1]:
            second = 1 - second
        start, count = first * (width // 2), width // 2
        if depth > 1:
            start, count = start + second * (width // 4), width // 4
        if depth > 2:
            start, count = start + (deep if z is None else z) * (width // 16), width // 16
        return pl.ds(pl.multiple_of(start, 16), count)

    for j in range(4):
        near, far = (peer_x, peer_y) if j % 2 == 0 else (peer_y, peer_x)
        define("ac", (j,), lambda j=j: parts.at[j, :, cols_of(1 - core)], lambda j=j: part_c.at[j], peer_c)
        define(
            "aa", (j,), lambda j=j: parts.at[j, rows_of(j, 1, (1, 0)), cols_of(core)], lambda j=j: part_a.at[j], near
        )
        define(
            "ab", (j,), lambda j=j: parts.at[j, rows_of(j, 2, (0, 1)), cols_of(core)], lambda j=j: part_b.at[j], far
        )
        for t in (1, 2, 3):
            define(
                "az",
                (j, t - 1),
                lambda j=j, t=t: parts.at[j, rows_of(j, 3, z=deep_of[t]), cols_of(core)],
                lambda j=j, t=t: part_z.at[j, t - 1],
                peer_z[t],
            )
            define(
                "gz",
                (j, t - 1),
                lambda j=j: parts.at[j, rows_of(j, 3), cols_of(core)],
                lambda j=j: summed_out.at[j, rows_of(j, 3), cols_of(core)],
                peer_z[t],
            )

        def place_of(depth, j=j):
            if depth:
                return lambda: summed_out.at[j, rows_of(j, depth), cols_of(core)]
            return lambda: summed_out.at[j, :, cols_of(core)]

        define("gb", (j,), place_of(2), place_of(2), far)
        define("ga", (j,), place_of(1), place_of(1), near)
        define("gc", (j,), place_of(0), place_of(0), peer_c)

    def keep(j):
        return pltpu.make_async_copy(
            parts.at[j, rows_of(j, 3), cols_of(core)], summed_out.at[j, rows_of(j, 3), cols_of(core)], keep_sem.at[j]
        )

    def sum_1(j):
        got("ac", j)
        add(parts.at[j, :, cols_of(core)], part_c.at[j])
        go("aa", j)

    def sum_2(j):
        got("aa", j)
        add(parts.at[j, rows_of(j, 1), cols_of(core)], part_a.at[j])
        go("ab", j)

    def sum_3(j):
        got("ab", j)
        add(parts.at[j, rows_of(j, 2), cols_of(core)], part_b.at[j])
        for t in range(3):
            go("az", j, t)

    def sum_4(j):
        total = parts[j, rows_of(j, 3), cols_of(core)].astype(fp)
        for t in range(3):
            got("az", j, t)
            total = total + part_z[j, t].astype(fp)
        parts[j, rows_of(j, 3), cols_of(core)] = total.astype(bf)
        for t in range(3):
            go("gz", j, t)
        keep(j).start()

    def sum_5(j):
        keep(j).wait()
        for t in range(3):
            remote(
                summed_out.at[j, rows_of(j, 3, z=deep_of[t + 1]), cols_of(core)],
                summed_out.at[j, rows_of(j, 3, z=deep_of[t + 1]), cols_of(core)],
                send["gz"].at[j, t],
                recv["gz"].at[j, t],
                peer_z[t + 1],
            ).wait_recv()
        go("gb", j)

    def arrive(name, j, depth, flips, c=None):
        cols = cols_of(core if c is None else c)
        piece = summed_out.at[j, rows_of(j, depth, flips), cols] if depth else summed_out.at[j, :, cols]
        remote(piece, piece, send[name].at[j], recv[name].at[j], peer_x).wait_recv()

    def sum_6(j):
        arrive("gb", j, 2, (0, 1))
        go("ga", j)

    def sum_7(j):
        arrive("ga", j, 1, (1, 0))
        go("gc", j)

    def sum_8(j):
        arrive("gc", j, 0, (0, 0), 1 - core)

    ring = (peer_c, peer_x, peer_y, peer_z[1], peer_z[2])
    for i, peer in enumerate(ring):
        define("bt", (i,), lambda i=i: small.at[i], lambda i=i: small_far.at[i], peer)

    def small_step(i):
        got("bt", i)
        if i < 4:
            small[i + 1] = small[i] + small_far[i]
            go("bt", i + 1)
        else:
            small_out[...] = small[i] + small_far[i]

    loads = [
        (sum_grad_in, grad),
        (act_in, act),
        (outer_in, weight),
        (slope_in, slope),
        (normed_in, normed),
        (context_in, context),
        (out_proj_in, out_proj),
        (tokens_in, tokens),
        (joint_in, joint),
        (joint_proj_in, joint_proj),
        (inner_in, weight),
    ]

    def load(i):
        return pltpu.make_async_copy(loads[i][0], loads[i][1], load_sem.at[i])

    def fetch(p):
        return pltpu.make_async_copy(
            probs_in.at[pl.ds(2 * p, 2)], probs.at[p % 2], probs_sem.at[p % 2]
        )

    for i in range(10):
        load(i).start()
    fetch(0).start()
    greet(place, side)
    small[0] = small_in[...]
    load(0).wait()
    low[...] = grad[...].astype(bf)
    load(1).wait()

    def outer_group(t):
        base = deep_of[t] * (4 * share)

        def body(i, carry):
            here = pl.ds(pl.multiple_of(base + i * 256, 256), 256)
            outer_sum[here, :] = tn_dot(act[:, here], low[...]).astype(bf)
            return carry

        lax.fori_loop(0, 4 * share // 256, body, 0)
        for y in range(2):
            go("oc", t, y)

    outer_group(3)
    outer_group(2)
    outer_to_x(3)
    outer_group(1)
    outer_to_x(2)
    outer_group(0)
    outer_to_x(1)
    load(2).wait()
    load(3).wait()
    slots = {
        0: [lambda: outer_to_x(0)],
        4: [lambda: outer_to_y(3)],
        9: [lambda: outer_to_y(2)],
        11: [lambda: outer_to_z(3)],
    }

    def at_slot(index, table):
        for slot, todo in table.items():

            @pl.when(index == slot)
            def _(todo=todo):
                for event in todo:
                    event()

    def pre_step(j, carry):
        cols = pl.ds(pl.multiple_of(j * 256, 256), 256)
        for b in range(2):
            rows = slice(b * half, (b + 1) * half)
            back = nt_dot(low[rows, :], weight[cols, :])
            act[rows, cols] = (back * slope[rows, cols].astype(fp)).astype(bf)
        bias_cols = pl.ds(pl.multiple_of((j % 3) * 256, 256), 256)
        small[0, pl.ds(8 + j // 3, 1), bias_cols] = jnp.sum(
            act[:, cols].astype(fp), axis=0, keepdims=True
        )
        at_slot(j, slots)
        return carry

    lax.fori_loop(0, units // 256, pre_step, 0)
    load(10).start()
    load(4).wait()

    def first_step(i, carry):
        rows = pl.ds(pl.multiple_of(i * 128, 128), 128)
        first_low[rows, :] = (normed[rows, :] * first_gain + first_shift).astype(bf)
        return carry

    lax.fori_loop(0, rows_total // 128, first_step, 0)

    def inner_group(t):
        base = deep_of[t] * (4 * share)

        def body(i, carry):
            here = pl.ds(pl.multiple_of(base + i * 256, 256), 256)
            inner_sum[here, :] = tn_dot(act[:, here], first_low[...]).astype(bf)
            return carry

        lax.fori_loop(0, 4 * share // 256, body, 0)
        for y in range(2):
            go("ic", t, y)

    inner_group(3)
    inner_group(2)
    inner_to_y(3)
    outer_to_y(1)
    inner_group(1)
    inner_to_y(2)
    outer_to_z(2)
    inner_group(0)
    inner_to_y(1)
    load(10).wait()
    for j in range(width // 256):
        cols = slice(j * 256, (j + 1) * 256)
        grad[:, cols] += nn_dot(act[...], weight[:, cols])
        if j == 0:
            inner_to_y(0)
        if j == 1:
            outer_to_y(0)
    outer_to_z(1)
    inner_to_z(3)

    def norm_step(i, carry):
        rows = pl.ds(pl.multiple_of(i * 128, 128), 128)
        incoming, unit = grad[rows, :], normed[rows, :]
        small[0, 3:4, :] += jnp.sum(incoming * unit, axis=0, keepdims=True)
        small[0, 4:5, :] += jnp.sum(incoming, axis=0, keepdims=True)
        scaled = incoming * first_gain
        back = scale[rows, :] * (
            scaled
            - jnp.mean(scaled, axis=-1, keepdims=True)
            - unit * jnp.mean(scaled * unit, axis=-1, keepdims=True)
        )
        grad[rows, :] = back
        back_low = back.astype(bf)
        low[rows, :] = back_low
        small[0, 5:6, :] += jnp.sum(back_low.astype(fp), axis=0, keepdims=True)
        return carry

    lax.fori_loop(0, rows_total // 128, norm_step, 0)
    load(5).wait()
    for j in range(width // 256):
        cols = slice(j * 256, (j + 1) * 256)
        parts[0, cols, :] = tn_dot(context[:, cols], low[...]).astype(bf)
    go("ac", 0)
    outer_to_z(0)
    inner_to_z(2)
    load(6).wait()
    for j in range(width // 256):
        cols = slice(j * 256, (j + 1) * 256)
        context_grad[:, cols] = (
            nt_dot(low[...], out_proj[cols, :]) * first_lanes(256, j * 256, kept_lanes)
        ).astype(bf)
    sum_1(0)
    load(7).wait()
    for j in range(width // 128):
        cols = slice(j * 128, (j + 1) * 128)
        tokens_over[cols, :] = tokens[:, cols].T
    inner_to_z(1)
    load(8).wait()
    first_half = (lax.broadcasted_iota(jnp.int32, (1, 128), 1) < DH).astype(bf)
    halves = (first_half, 1 - first_half)
    factor = 1.0 / math.sqrt(DH)
    pairs = HEADS // 2
    pair_slots = {
        0: [lambda: sum_2(0), lambda: inner_to_z(0), outer_end],
        1: [lambda: go("ac", 1), lambda: sum_3(0)],
        2: [lambda: sum_1(1), lambda: sum_4(0), lambda: got("of", 0), inner_end],
        3: [lambda: go("ac", 2), lambda: sum_2(1), lambda: sum_5(0), inner_last],
        4: [lambda: sum_1(2), lambda: sum_3(1), lambda: sum_6(0)],
        5: [
            lambda: go("ac", 3),
            lambda: sum_4(1),
            lambda: sum_2(2),
            lambda: sum_7(0),
            lambda: go("bt", 0),
        ],
    }

    def pair_step(p, carry):
        @pl.when(p + 1 < pairs)
        def _():
            fetch(p + 1).start()

        fetch(p).wait()
        slot = p % 2
        cols = [pl.ds(pl.multiple_of(s * width + p * 128, 128), 128) for s in range(3)]
        out_cols = pl.ds(pl.multiple_of(p * 128, 128), 128)
        keys, values = joint[:, cols[1]], joint[:, cols[2]]
        value_part, key_part = None, None
        for b in range(2):
            lanes = slice(b * half, (b + 1) * half)
            queries, incoming = joint[lanes, cols[0]], context_grad[lanes, out_cols]
            query_part = None
            for a in range(2):
                weights_low = probs[slot, a, :, lanes]
                weights = weights_low.astype(fp)
                product = nt_dot(values * halves[a], incoming) * weights
                score_grad = (
                    product - weights * jnp.sum(product, axis=0, keepdims=True)
                ).astype(bf)
                part = nn_dot(weights_low, incoming * halves[a])
                value_part = part if value_part is None else value_part + part
                part = nn_dot(score_grad, queries * halves[a])
                key_part = part if key_part is None else key_part + part
                part = tn_dot(score_grad, keys * halves[a])
                query_part = part if query_part is None else query_part + part
            joint_grad[lanes, cols[0]] = (query_part * factor).astype(bf)
        joint_grad[:, cols[1]] = (key_part * factor).astype(bf)
        joint_grad[:, cols[2]] = value_part.astype(bf)
        small[0, 6:7, out_cols] = jnp.sum(
            joint_grad[:, cols[0]].astype(fp), axis=0, keepdims=True
        )
        small[0, 7:8, out_cols] = jnp.sum(
            joint_grad[:, cols[2]].astype(fp), axis=0, keepdims=True
        )

        @pl.when(p % 2 == 1)
        def _():
            index = (p + 1) // 2
            for s in range(3):
                source = pl.ds(pl.multiple_of(s * width + (index - 1) * 256, 256), 256)
                parts[index, :, s * 256 : (s + 1) * 256] = nn_dot(
                    tokens_over[...], joint_grad[:, source]
                ).astype(bf)

        at_slot(p, pair_slots)
        return carry

    lax.fori_loop(0, pairs, pair_step, 0)
    load(9).wait()
    between = {
        0: [lambda: sum_1(3), lambda: sum_5(1), lambda: sum_3(2), lambda: small_step(0)],
        1: [lambda: sum_8(0), lambda: small_step(1)],
        2: [lambda: sum_6(1), lambda: sum_4(2), lambda: small_step(2)],
    }
    for j in range(width // 256):
        cols = slice(j * 256, (j + 1) * 256)
        grad[:, cols] += nt_dot(joint_grad[...], joint_proj[cols, :])
        for event in between[j]:
            event()
    result = pltpu.make_async_copy(grad, input_grad, keep_sem.at[4])
    result.start()
    sum_2(3)
    sum_5(2)
    sum_7(1)
    small_step(3)
    sum_3(3)
    sum_6(2)
    small_step(4)
    sum_4(3)
    sum_7(2)
    sum_5(3)
    sum_8(1)
    sum_6(3)
    sum_8(2)
    sum_7(3)
    sum_8(3)
    result.wait()
    for build in made.values():
        build().wait_send()


def run_backward(args, share, units, rows_total, width):
    bf, fp = jnp.bfloat16, jnp.float32
    shape = jax.ShapeDtypeStruct
    vmem = pl.BlockSpec(memory_space=pltpu.VMEM)
    anywhere = pl.BlockSpec(memory_space=pl.ANY)
    third = share // 2
    counts = [
        (4, 2), (4, 2), (4,), (3,), (1,), (4, 2), (4,), (3,), (1,),
        (4,), (4,), (4,), (4, 3), (4, 3), (4,), (4,), (4,), (5,),
    ]
    sems = [pltpu.SemaphoreType.DMA(count) for unused in range(2) for count in counts]
    quarter = width // 2
    return pl.pallas_call(
        backward_kernel,
        out_shape=(
            shape((rows_total, width), fp),
            shape((4, width, width), bf),
            shape((share, width), bf),
            shape((share, width), fp),
            shape((16, width), fp),
        ),
        in_specs=[anywhere] * 12 + [vmem] * 4 + [pl.BlockSpec(memory_space=pltpu.SMEM)],
        out_specs=(anywhere, anywhere, vmem, vmem, vmem),
        scratch_shapes=[
            pltpu.VMEM((rows_total, units), bf),
            pltpu.VMEM((rows_total, units), bf),
            pltpu.VMEM((units, width), bf),
            pltpu.VMEM((2, 2, rows_total, rows_total), bf),
            pltpu.VMEM((rows_total, 3 * width), bf),
            pltpu.VMEM((rows_total, width), bf),
            pltpu.VMEM((rows_total, width), fp),
            pltpu.VMEM((rows_total, width), fp),
            pltpu.VMEM((rows_total, width), bf),
            pltpu.VMEM((width, rows_total), bf),
            pltpu.VMEM((width, 3 * width), bf),
            pltpu.VMEM((width, width), bf),
            pltpu.VMEM((rows_total, width), bf),
            pltpu.VMEM((rows_total, width), bf),
            pltpu.VMEM((units, width), bf),
            pltpu.VMEM((units, width), bf),
            pltpu.VMEM((4, 2, share, width), bf),
            pltpu.VMEM((4, 2, third, width), bf),
            pltpu.VMEM((4, third, width), bf),
            pltpu.VMEM((3, third, width), bf),
            pltpu.VMEM((4, 2, share, width), bf),
            pltpu.VMEM((4, share, width), bf),
            pltpu.VMEM((3, share, width), bf),
            pltpu.VMEM((share, width), bf),
            pltpu.VMEM((share, width), bf),
            pltpu.VMEM((4, width, width), bf),
            pltpu.VMEM((4, width, quarter), bf),
            pltpu.VMEM((4, width // 2, quarter), bf),
            pltpu.VMEM((4, width // 4, quarter), bf),
            pltpu.VMEM((4, 3, width // 16, quarter), bf),
            pltpu.VMEM((rows_total, 3 * width), bf),
            pltpu.VMEM((rows_total, width), bf),
            pltpu.VMEM((5, 16, width), fp),
            pltpu.VMEM((5, 16, width), fp),
            pltpu.SemaphoreType.DMA((11,)),
            pltpu.SemaphoreType.DMA((2,)),
            pltpu.SemaphoreType.DMA((5,)),
        ]
        + sems,
        compiler_params=pltpu.CompilerParams(
            collective_id=1, has_side_effects=True, vmem_limit_bytes=64 * 1024 * 1024 - 65536
        ),
        name="backward",
    )(*args)


def on_device_fast(
    tokens,
    joint_proj,
    query_bias,
    value_bias,
    out_proj,
    out_bias,
    first_gain,
    first_shift,
    inner_proj,
    inner_bias,
    outer_proj,
    outer_bias,
    second_gain,
    second_shift,
    segment_ids,
    cls_positions,
    widths,
    out_grad,
):
    tok_rows, model_width = tokens.shape
    unit_share = inner_proj.shape[1]
    ffn_count = lax.axis_size("ffn")
    ffn_place = lax.axis_index("ffn")
    unit_total = unit_share * ffn_count
    shifted = jnp.arange(2 * unit_share, dtype=jnp.int32) // unit_share == ffn_place % 2
    bias_block = jnp.where(shifted, jnp.tile(inner_bias, 2).astype(jnp.float32), 0.0)
    bias_block = jnp.broadcast_to(bias_block, (8, 2 * unit_share))
    (
        output, cls_states, inner_rows, outer_rows, probs_again, joint_flat, context_low,
        first_normed, first_scale, act_low, slope_low, sum_grad, small_a,
    ) = run_forward(
        (
            tokens, joint_proj, query_bias, value_bias, out_proj, out_bias, first_gain, first_shift,
            inner_proj.T, outer_proj, bias_block, outer_bias, second_gain, second_shift,
            segment_ids[None], widths, cls_positions, out_grad,
        ),
        unit_share, unit_total, tok_rows, model_width,
    )
    input_grad, summed, outer_part, inner_part, small = run_backward(
        (
            act_low, slope_low, sum_grad, outer_rows, inner_rows, first_normed, joint_flat,
            context_low, probs_again, tokens, joint_proj, out_proj, first_scale, small_a,
            first_gain, first_shift, widths,
        ),
        unit_share, unit_total, tok_rows, model_width,
    )
    cls_states = cls_states[None]
    outer_proj_grad = outer_part.astype(jnp.float32)
    inner_proj_grad = inner_part.T
    out_proj_grad = summed[0].astype(jnp.float32)
    joint_proj_grad = jnp.concatenate(
        [summed[1 + i, :, s * 256 : (s + 1) * 256] for s in range(3) for i in range(3)], axis=1
    ).astype(jnp.float32)
    second_gain_grad, second_shift_grad, outer_bias_grad = small[0], small[1], small[2]
    first_gain_grad, first_shift_grad, out_bias_grad = small[3], small[4], small[5]
    query_bias_grad, value_bias_grad = small[6], small[7]
    inner_bias_grad = lax.dynamic_slice(
        small[8:12].reshape(-1), (ffn_place * unit_share,), (unit_share,)
    )
    return (
        output,
        cls_states,
        input_grad,
        joint_proj_grad,
        query_bias_grad,
        value_bias_grad,
        out_proj_grad,
        out_bias_grad,
        first_gain_grad,
        first_shift_grad,
        inner_proj_grad,
        inner_bias_grad,
        outer_proj_grad,
        outer_bias_grad,
        second_gain_grad,
        second_shift_grad,
    )


def solution(mesh):
    return jax.shard_map(
        on_device_fast if mesh.shape["ffn"] == 16 and mesh.shape["tok"] == 2 else on_device,
        mesh=mesh,
        in_specs=(
            P(("ffn", "tok"), None),
            P(),
            P(),
            P(),
            P(),
            P(),
            P(),
            P(),
            P(None, "ffn"),
            P("ffn"),
            P("ffn", None),
            P(),
            P(),
            P(),
            P(("ffn", "tok")),
            P(("ffn", "tok"), None),
            P(),
            P(("ffn", "tok"), None),
        ),
        out_specs=(
            P(("ffn", "tok"), None),
            P(("ffn", "tok"), None, None),
            P(("ffn", "tok"), None),
            P(),
            P(),
            P(),
            P(),
            P(),
            P(),
            P(),
            P(None, "ffn"),
            P("ffn"),
            P("ffn", None),
            P(),
            P(),
            P(),
        ),
        check_vma=False,
    )
```

```python
import math

import jax
import jax.numpy as jnp
from jax import lax
from jax.experimental import pallas as pl
from jax.experimental.pallas import tpu as pltpu
from jax.sharding import PartitionSpec as P

MESH = pl.DeviceIdType.MESH
HEADS = 12
DH = 64
MB = 2
SEGS = 4


def normalize(inputs, gain_vec, shift_vec):
    row_mean = jnp.mean(inputs, axis=-1, keepdims=True)
    centred = inputs - row_mean
    row_scale = lax.rsqrt(jnp.mean(centred * centred, axis=-1, keepdims=True) + 1e-12)
    normed = centred * row_scale
    return (normed * gain_vec + shift_vec, normed, row_scale)


def normalize_back(incoming, normed, row_scale, gain_vec):
    gain_grad = jnp.sum(incoming * normed, axis=0)
    shift_grad = jnp.sum(incoming, axis=0)
    scaled_grad = incoming * gain_vec
    inputs_grad = row_scale * (
        scaled_grad
        - jnp.mean(scaled_grad, axis=-1, keepdims=True)
        - normed * jnp.mean(scaled_grad * normed, axis=-1, keepdims=True)
    )
    return (inputs_grad, gain_grad, shift_grad)


def gelu_slope(inputs):
    return (
        0.5 * (1.0 + lax.erf(inputs * 0.7071067811865476))
        + inputs * jnp.exp(-0.5 * inputs * inputs) * 0.3989422804014327
    )


def contract_rows(left_side, right_side):
    return lax.dot_general(
        left_side, right_side, (((0,), (0,)), ((), ())), preferred_element_type=jnp.float32
    )


def contract_cols(left_side, right_side):
    return lax.dot_general(
        left_side, right_side, (((1,), (1,)), ((), ())), preferred_element_type=jnp.float32
    )


def on_device(
    tokens,
    joint_proj,
    query_bias,
    value_bias,
    out_proj,
    out_bias,
    first_gain,
    first_shift,
    inner_proj,
    inner_bias,
    outer_proj,
    outer_bias,
    second_gain,
    second_shift,
    segment_ids,
    cls_positions,
    widths,
    out_grad,
):
    tok_rows, model_width = tokens.shape
    seq_rows = cls_positions.shape[0]
    seq_len = tok_rows // seq_rows
    unit_share = inner_proj.shape[1]
    ffn_count = lax.axis_size("ffn")
    tok_count = lax.axis_size("tok")
    ffn_place = lax.axis_index("ffn")
    tok_place = lax.axis_index("tok")
    per_group = seq_rows * ffn_count * tok_count // MB
    batches = jnp.arange(MB, dtype=jnp.int32)
    own_group = (ffn_place * tok_count + tok_place) * seq_rows // per_group
    own_pick = (batches == own_group).astype(jnp.int32)
    heads_kept = jnp.sum(own_pick * widths[:, 1])
    head_on = (jnp.arange(HEADS, dtype=jnp.int32) < heads_kept).astype(jnp.float32)
    factor = 1.0 / math.sqrt(DH)
    zero_bias = jnp.zeros((model_width,), jnp.bfloat16)
    joint_bias = jnp.concatenate([query_bias, zero_bias, value_bias])
    joint_low = (
        jnp.dot(tokens, joint_proj, preferred_element_type=jnp.float32) + joint_bias
    ).astype(jnp.bfloat16)
    joint_low = joint_low.reshape(seq_rows, seq_len, 3, HEADS, DH)
    queries = joint_low[:, :, 0]
    key_heads = joint_low[:, :, 1]
    value_heads = joint_low[:, :, 2]
    segments = segment_ids.reshape(seq_rows, seq_len)
    same_doc = (segments[:, :, None] == segments[:, None, :])[:, None]

    def scores_of(query_rows, key_rows):
        raw_scores = (
            jnp.einsum("rqhd,rkhd->rhqk", query_rows, key_rows, preferred_element_type=jnp.float32)
            * factor
        )
        return jnp.where(same_doc, raw_scores, -1e30)

    scores = scores_of(queries, key_heads)
    row_peak = jnp.max(scores, axis=-1, keepdims=True)
    log_total = row_peak + jnp.log(jnp.sum(jnp.exp(scores - row_peak), axis=-1, keepdims=True))
    probs_low = jnp.exp(scores - log_total).astype(jnp.bfloat16)
    context = (
        jnp.einsum("rhqk,rkhd->rqhd", probs_low, value_heads, preferred_element_type=jnp.float32)
        * head_on[:, None]
    )
    context_low = context.astype(jnp.bfloat16).reshape(tok_rows, model_width)
    attn_out = jnp.dot(context_low, out_proj, preferred_element_type=jnp.float32) + out_bias
    first_out, first_normed, first_scale = normalize(
        tokens.astype(jnp.float32) + attn_out, first_gain, first_shift
    )
    first_low = first_out.astype(jnp.bfloat16)
    unit_total = unit_share * ffn_count
    stacked = lax.all_gather(
        jnp.stack([inner_proj.T, outer_proj]), "ffn", axis=1, tiled=True
    )
    inner_rows, outer_rows = stacked[0], stacked[1]
    inner_bias_all = lax.all_gather(inner_bias, "ffn", axis=0, tiled=True)
    own_kept = jnp.sum(own_pick * widths[:, 0])
    neuron_on = (jnp.arange(unit_total, dtype=jnp.int32) < own_kept).astype(jnp.float32)
    pre_act = contract_cols(first_low, inner_rows) + inner_bias_all
    act_low = (jax.nn.gelu(pre_act, approximate=False) * neuron_on).astype(jnp.bfloat16)
    ffn_out = jnp.dot(act_low, outer_rows, preferred_element_type=jnp.float32) + outer_bias
    second_out, second_normed, second_scale = normalize(
        first_out + ffn_out, second_gain, second_shift
    )
    output = second_out.astype(jnp.bfloat16)
    cls_states = jnp.take_along_axis(
        second_out.reshape(seq_rows, seq_len, model_width), cls_positions[:, :, None], axis=1
    )
    sum_grad, second_gain_grad, second_shift_grad = normalize_back(
        out_grad.astype(jnp.float32), second_normed, second_scale, second_gain
    )
    ffn_grad = sum_grad.astype(jnp.bfloat16)
    outer_bias_grad = jnp.sum(ffn_grad.astype(jnp.float32), axis=0)
    outer_proj_grad = contract_rows(act_low, ffn_grad)
    act_grad = contract_cols(ffn_grad, outer_rows)
    pre_grad = (act_grad * (gelu_slope(pre_act) * neuron_on)).astype(jnp.bfloat16)
    inner_bias_sum = jnp.sum(pre_grad.astype(jnp.float32), axis=0)
    inner_rows_grad = contract_rows(pre_grad, first_low)
    first_back = jnp.dot(pre_grad, inner_rows, preferred_element_type=jnp.float32)
    unit_grads = jnp.stack(
        [inner_rows_grad.astype(jnp.bfloat16), outer_proj_grad.astype(jnp.bfloat16)]
    )
    unit_grads = lax.psum_scatter(unit_grads, "ffn", scatter_dimension=1, tiled=True)
    unit_grads = lax.psum(unit_grads, "tok").astype(jnp.float32)
    inner_proj_grad, outer_proj_grad = unit_grads[0].T, unit_grads[1]
    first_grad = sum_grad + first_back
    attn_sum_grad, first_gain_grad, first_shift_grad = normalize_back(
        first_grad, first_normed, first_scale, first_gain
    )
    attn_grad = attn_sum_grad.astype(jnp.bfloat16)
    out_bias_grad = jnp.sum(attn_grad.astype(jnp.float32), axis=0)
    out_proj_grad = contract_rows(context_low, attn_grad)
    context_grad = (
        contract_cols(attn_grad, out_proj)
        .astype(jnp.bfloat16)
        .reshape(seq_rows, seq_len, HEADS, DH)
    )
    context_grad = context_grad * head_on.astype(jnp.bfloat16)[:, None]
    scores = scores_of(queries, key_heads)
    probs = jnp.exp(scores - log_total)
    probs_again = probs.astype(jnp.bfloat16)
    value_part = jnp.einsum(
        "rhqk,rqhd->rkhd", probs_again, context_grad, preferred_element_type=jnp.float32
    )
    prob_grad = jnp.einsum(
        "rqhd,rkhd->rhqk", context_grad, value_heads, preferred_element_type=jnp.float32
    )
    score_grad = (probs * (prob_grad - jnp.sum(probs * prob_grad, axis=-1, keepdims=True))).astype(
        jnp.bfloat16
    )
    query_part = (
        jnp.einsum("rhqk,rkhd->rqhd", score_grad, key_heads, preferred_element_type=jnp.float32)
        * factor
    )
    key_part = (
        jnp.einsum("rhqk,rqhd->rkhd", score_grad, queries, preferred_element_type=jnp.float32)
        * factor
    )
    joint_grad = (
        jnp.stack([query_part, key_part, value_part], axis=2)
        .astype(jnp.bfloat16)
        .reshape(tok_rows, 3 * model_width)
    )
    joint_bias_grad = jnp.sum(joint_grad.astype(jnp.float32), axis=0)
    query_bias_grad = joint_bias_grad[:model_width]
    value_bias_grad = joint_bias_grad[2 * model_width :]
    joint_proj_grad = contract_rows(tokens, joint_grad)
    input_grad = attn_sum_grad + contract_cols(joint_grad, joint_proj)
    joint_proj_grad, out_proj_grad = lax.psum(
        (joint_proj_grad.astype(jnp.bfloat16), out_proj_grad.astype(jnp.bfloat16)),
        ("ffn", "tok"),
    )
    joint_proj_grad = joint_proj_grad.astype(jnp.float32)
    out_proj_grad = out_proj_grad.astype(jnp.float32)
    small = [
        query_bias_grad,
        value_bias_grad,
        out_bias_grad,
        first_gain_grad,
        first_shift_grad,
        outer_bias_grad,
        second_gain_grad,
        second_shift_grad,
        inner_bias_sum,
    ]
    small = lax.psum(jnp.concatenate(small), ("ffn", "tok"))
    (
        query_bias_grad,
        value_bias_grad,
        out_bias_grad,
        first_gain_grad,
        first_shift_grad,
        outer_bias_grad,
        second_gain_grad,
        second_shift_grad,
    ) = [small[i * model_width : (i + 1) * model_width] for i in range(8)]
    inner_bias_grad = lax.dynamic_slice(
        small, (8 * model_width + ffn_place * unit_share,), (unit_share,)
    )
    return (
        output,
        cls_states,
        input_grad,
        joint_proj_grad,
        query_bias_grad,
        value_bias_grad,
        out_proj_grad,
        out_bias_grad,
        first_gain_grad,
        first_shift_grad,
        inner_proj_grad,
        inner_bias_grad,
        outer_proj_grad,
        outer_bias_grad,
        second_gain_grad,
        second_shift_grad,
    )


def x_or1(v):
    return v + 1 - 2 * (v % 2)


def x_or2(v):
    return v + 2 - 4 * ((v // 2) % 2)


def z_peer(place, turn):
    deep = place // 4
    if turn & 1:
        deep = x_or1(deep)
    if turn & 2:
        deep = x_or2(deep)
    return deep * 4 + place % 4


def y_peer(place):
    return (place // 4) * 4 + ((place // 2 + 1) % 2) * 2 + place % 2


def c_peer(place):
    return x_or1(place)


def nt_dot(left_side, right_side):
    return lax.dot_general(
        left_side, right_side, (((1,), (1,)), ((), ())), preferred_element_type=jnp.float32
    )


def tn_dot(left_side, right_side):
    return lax.dot_general(
        left_side, right_side, (((0,), (0,)), ((), ())), preferred_element_type=jnp.float32
    )


def nn_dot(left_side, right_side):
    return lax.dot_general(
        left_side, right_side, (((1,), (0,)), ((), ())), preferred_element_type=jnp.float32
    )


def greet(place, side):
    barrier = pltpu.get_barrier_semaphore()
    peers = [
        (z_peer(place, 1), side),
        (z_peer(place, 2), side),
        (z_peer(place, 3), side),
        (y_peer(place), side),
        (c_peer(place), side),
        (place, 1 - side),
    ]
    for peer in peers:
        pl.semaphore_signal(barrier, inc=1, device_id=peer, device_id_type=MESH)
    pl.semaphore_wait(barrier, 6)


def remote(source, target, send_sem, recv_sem, device):
    return pltpu.make_async_remote_copy(
        src_ref=source,
        dst_ref=target,
        send_sem=send_sem,
        recv_sem=recv_sem,
        device_id=device,
        device_id_type=MESH,
    )


class Spread:
    def __init__(self, own, whole, place, side, rows, sems):
        self.own, self.whole, self.place, self.side, self.rows = own, whole, place, side, rows
        self.up_s, self.up_r, self.dn_s, self.dn_r, self.y_s, self.y_r = sems[:6]
        self.x_s, self.x_r, self.c_s, self.c_r, self.d_s, self.d_r = sems[6:]
        self.third = rows // 3
        self.deep = place // 4

    def span(self, source, offset, count):
        start = pl.multiple_of(source * self.rows + offset, 16)
        return self.whole.at[pl.ds(start, count)]

    def slab(self, source):
        return self.span(source, self.side * self.third, 2 * self.third)

    def edge(self, source, mine=True):
        side = self.side if mine else 1 - self.side
        return self.span(source, side * 2 * self.third, self.third)

    def own_slab(self):
        start = pl.multiple_of(self.side * self.third, 16)
        return self.own.at[pl.ds(start, 2 * self.third)]

    def source_of(self, step, up, cross=False):
        base = y_peer(self.place) if cross else self.place
        if step is None:
            return base
        return base - 4 * (step + 1) if up else base + 4 * (step + 1)

    def has(self, step, up):
        if step is None:
            return None
        return self.deep >= step + 1 if up else self.deep + step + 1 <= 3

    def hop(self, step, up, first=False):
        source = self.place if step == 0 else self.source_of(step - 1, up)
        piece = self.own_slab() if step == 0 else self.slab(source)
        send, recv = (self.up_s, self.up_r) if up else (self.dn_s, self.dn_r)
        device = (self.place + 4 if up else self.place - 4, self.side)
        return remote(piece, self.slab(source), send.at[step], recv.at[step], device)

    def hop_in(self, step, up):
        source = self.source_of(step, up)
        send, recv = (self.up_s, self.up_r) if up else (self.dn_s, self.dn_r)
        return remote(
            self.slab(source), self.slab(source), send.at[step], recv.at[step], (self.place, 1 - self.side)
        )

    def over_y(self, source, own=False):
        index = source // 4
        piece = self.own_slab() if own else self.slab(source)
        return remote(
            piece, self.slab(source), self.y_s.at[index], self.y_r.at[index], (y_peer(self.place), self.side)
        )

    def over_x(self, source, mine=True):
        index = source // 2
        piece = self.edge(source, mine)
        return remote(
            piece, piece, self.x_s.at[index], self.x_r.at[index], (self.place, 1 - self.side)
        )

    def over_c(self, source):
        index = source // 2
        return remote(
            self.slab(source),
            self.slab(source),
            self.c_s.at[index],
            self.c_r.at[index],
            (c_peer(self.place), self.side),
        )

    def over_d(self, source):
        index = source // 2
        piece = self.edge(source, False)
        return remote(piece, piece, self.d_s.at[index], self.d_r.at[index], (c_peer(self.place), self.side))

    def over_own(self):
        index = self.place // 2
        return remote(
            self.own,
            self.span(self.place, 0, self.rows),
            self.c_s.at[index],
            self.c_r.at[index],
            (c_peer(self.place), self.side),
        )

    def start(self):
        @pl.when(self.deep < 3)
        def _():
            self.hop(0, True).start()

        @pl.when(self.deep > 0)
        def _():
            self.hop(0, False).start()

        self.over_y(self.place, own=True).start()
        self.over_own().start()

    def z_event(self, step):
        for up in (True, False):

            @pl.when(self.has(step, up))
            def _(up=up):
                source = self.source_of(step, up)
                self.hop_in(step, up).wait_recv()
                if step < 2:

                    @pl.when(self.deep < 3 if up else self.deep > 0)
                    def _():
                        self.hop(step + 1, up).start()

                self.over_y(source).start()
                self.over_x(source).start()
                self.over_c(source).start()

    def each(self, step, work):
        if step is None:
            work(True)
            return
        for up in (True, False):

            @pl.when(self.has(step, up))
            def _(up=up):
                work(up)

    def y_event(self, step):
        def work(up):
            source = self.source_of(step, up, cross=True)
            self.over_y(source).wait_recv()
            self.over_x(source).start()
            self.over_c(source).start()

        self.each(step, work)

    def x_event(self, step, cross):
        def work(up):
            source = self.source_of(step, up, cross=cross)
            self.over_x(source, False).wait_recv()
            self.over_d(source).start()

        self.each(step, work)

    def finish(self):
        other = c_peer(self.place) % 2
        own = c_peer(self.place)
        for index in range(8):
            source = 2 * index + other

            @pl.when(source != own)
            def _(source=source):
                self.over_c(source).wait_recv()
                self.over_d(source).wait_recv()

            @pl.when(source == own)
            def _(source=source):
                remote(
                    self.own,
                    self.span(source, 0, self.rows),
                    self.c_s.at[index],
                    self.c_r.at[index],
                    (c_peer(self.place), self.side),
                ).wait_recv()

    def drain(self):
        for up in (True, False):
            for step in range(3):
                limit = self.deep < 3 if up else self.deep > 0
                if step > 0:
                    limit = jnp.logical_and(limit, self.has(step - 1, up))

                @pl.when(limit)
                def _(step=step, up=up):
                    self.hop(step, up).wait_send()

        for index in range(4):
            source = 4 * index + self.place % 4
            self.over_y(source).wait_send()
        mine = self.place % 2
        for index in range(8):
            source = 2 * index + mine

            @pl.when(source != self.place)
            def _(source=source):
                self.over_x(source).wait_send()
                self.over_c(source).wait_send()
                self.over_d(source).wait_send()

            @pl.when(source == self.place)
            def _():
                self.over_own().wait_send()


def row_of(vector):
    return vector[...].astype(jnp.float32).reshape(1, vector.shape[0])


def kept_of(widths, place, side, kind):
    return widths[(place * 2 + side) * MB // 32, kind]


def first_lanes(count, start, kept):
    lane = lax.broadcasted_iota(jnp.int32, (1, count), 1) + start
    return jnp.where(lane < kept, 1.0, 0.0)


def forward_kernel(
    tokens,
    joint_proj,
    query_bias,
    value_bias,
    out_proj,
    out_bias,
    first_gain,
    first_shift,
    inner_own,
    outer_own,
    bias_own,
    outer_bias,
    second_gain,
    second_shift,
    seg_over,
    widths,
    cls_at,
    out_grad,
    output,
    cls_out,
    inner_out,
    outer_out,
    probs_out,
    joint_out,
    context_out,
    normed_out,
    scale_out,
    act_out,
    slope_out,
    sum_grad_out,
    small_out,
    inner_all,
    outer_all,
    probs,
    joint,
    context,
    mask_bias,
    act,
    slope,
    first_low,
    wide,
    bias_all,
    inner_bias,
    joint_bias,
    save_sem,
    bias_send,
    bias_recv,
    *sems,
):
    place, side = lax.axis_index("ffn"), lax.axis_index("tok")
    out_bias, outer_bias = row_of(out_bias), row_of(outer_bias)
    first_gain, first_shift = row_of(first_gain), row_of(first_shift)
    second_gain, second_shift = row_of(second_gain), row_of(second_shift)
    rows_total = tokens.shape[0]
    units = inner_all.shape[0]
    share = inner_own.shape[0]
    width = tokens.shape[1]
    half = rows_total // 2
    kept_units = kept_of(widths, place, side, 0)
    own_bias = pltpu.make_async_copy(bias_own, bias_all.at[place], save_sem.at[12])
    own_bias.start()
    joint_bias[:, 0:width] = row_of(query_bias)
    joint_bias[:, width : 2 * width] = jnp.zeros((1, width), jnp.float32)
    joint_bias[:, 2 * width :] = row_of(value_bias)
    own_bias.wait()

    def bias_hop(step):
        peer = (c_peer(place), y_peer(place), z_peer(place, 1), z_peer(place, 2))[step]
        count = 1 << step
        piece = bias_all.at[pl.ds(place // count * count, count)]
        return remote(piece, piece, bias_send.at[step], bias_recv.at[step], (peer, side))

    def bias_event(step):
        bias_hop(step - 1).wait_recv()
        if step < 4:
            bias_hop(step).start()

    greet(place, side)
    inner = Spread(inner_own, inner_all, place, side, share, sems[:12])
    outer = Spread(outer_own, outer_all, place, side, share, sems[12:])
    inner.start()
    outer.start()
    bias_hop(0).start()
    own_rows = pl.ds(pl.multiple_of(place * share, 16), share)
    inner_all[own_rows, :] = inner_own[...]
    outer_all[own_rows, :] = outer_own[...]
    saves = []

    def save(source, target, index):
        pltpu.make_async_copy(source, target, save_sem.at[index]).start()
        saves.append((source, target, index))

    kind = lax.broadcasted_iota(jnp.int32, (128, rows_total), 0)
    kinds = jnp.where(kind == seg_over[...], 1.0, 0.0).astype(jnp.bfloat16)
    for b in range(2):
        lanes = slice(b * half, (b + 1) * half)
        mask_bias[:, lanes] = jnp.where(tn_dot(kinds, kinds[:, lanes]) > 0.5, 0.0, -1e30)

    def joint_step(j, carry):
        cols = pl.ds(pl.multiple_of(j * 256, 256), 256)
        joint[:, cols] = (nn_dot(tokens[...], joint_proj[:, cols]) + joint_bias[:, cols]).astype(
            jnp.bfloat16
        )
        return carry

    lax.fori_loop(0, 3 * width // 256, joint_step, 0)
    save(joint, joint_out, 0)
    events = [
        lambda: inner.z_event(0),
        lambda: outer.z_event(0),
        lambda: inner.y_event(None),
        lambda: inner.z_event(1),
        lambda: outer.y_event(None),
        lambda: inner.y_event(0),
        lambda: outer.z_event(1),
        lambda: inner.x_event(0, False),
        lambda: inner.x_event(None, True),
        lambda: outer.y_event(0),
        lambda: inner.z_event(2),
        lambda: outer.x_event(0, False),
        lambda: outer.x_event(None, True),
        lambda: inner.y_event(1),
        lambda: outer.z_event(2),
        lambda: inner.x_event(1, False),
        lambda: inner.x_event(0, True),
        lambda: outer.y_event(1),
        lambda: inner.y_event(2),
        lambda: outer.x_event(1, False),
        lambda: outer.x_event(0, True),
        lambda: inner.x_event(2, False),
        lambda: inner.x_event(1, True),
        lambda: outer.y_event(2),
        lambda: inner.x_event(2, True),
        lambda: outer.x_event(2, False),
        lambda: outer.x_event(1, True),
        lambda: outer.x_event(2, True),
    ]
    events[0]()
    bias_event(1)
    slots = {0: events[1:4], 1: events[4:6], 2: events[6:10], 3: events[10:14], 4: events[14:18], 5: events[18:22]}
    slots[0].append(lambda: bias_event(2))
    slots[2].append(lambda: bias_event(3))
    slots[4].append(lambda: bias_event(4))
    first_half = (lax.broadcasted_iota(jnp.int32, (1, 128), 1) < DH).astype(jnp.bfloat16)
    halves = (first_half, 1 - first_half)
    factor = 1.4426950408889634 / math.sqrt(DH)
    pairs = HEADS // 2

    def pair_step(p, carry):
        cols = [pl.ds(pl.multiple_of(s * width + p * 128, 128), 128) for s in range(3)]
        out_cols = pl.ds(pl.multiple_of(p * 128, 128), 128)
        keys, values = joint[:, cols[1]], joint[:, cols[2]]
        for b in range(2):
            lanes = slice(b * half, (b + 1) * half)
            queries = joint[lanes, cols[0]]
            total = None
            for a in range(2):
                scores = nt_dot(keys * halves[a], queries) * factor + mask_bias[:, lanes]
                weights = jnp.exp2(scores - jnp.max(scores, axis=0, keepdims=True))
                weights = weights * (1.0 / jnp.sum(weights, axis=0, keepdims=True))
                low = weights.astype(jnp.bfloat16)
                probs[2 * p + a, :, lanes] = low
                part = tn_dot(low, values * halves[a])
                total = part if total is None else total + part
            context[lanes, out_cols] = (
                total * first_lanes(128, p * 128, kept_of(widths, place, side, 1) * DH)
            ).astype(jnp.bfloat16)
        pltpu.make_async_copy(
            probs.at[pl.ds(2 * p, 2)], probs_out.at[pl.ds(2 * p, 2)], save_sem.at[6 + p]
        ).start()
        for slot, todo in slots.items():

            @pl.when(p == slot)
            def _(todo=todo):
                for event in todo:
                    event()

        return carry

    lax.fori_loop(0, pairs, pair_step, 0)
    save(context, context_out, 1)
    for j in range(width // 256):
        cols = slice(j * 256, (j + 1) * 256)
        wide[:, cols] = nn_dot(context[...], out_proj[:, cols])

    def first_norm(i, carry):
        rows = pl.ds(pl.multiple_of(i * 128, 128), 128)
        total = tokens[rows, :].astype(jnp.float32) + (wide[rows, :] + out_bias)
        centred = total - jnp.mean(total, axis=-1, keepdims=True)
        scale = lax.rsqrt(jnp.mean(centred * centred, axis=-1, keepdims=True) + 1e-12)
        normed = centred * scale
        normed_out[rows, :] = normed
        scale_out[rows, :] = scale
        first_low[rows, :] = (normed * first_gain + first_shift).astype(jnp.bfloat16)
        return carry

    lax.fori_loop(0, rows_total // 128, first_norm, 0)
    for event in events[22:25]:
        event()
    for q in range(units // (2 * share)):
        inner_bias[:, q * 2 * share : (q + 1) * 2 * share] = (
            bias_all[2 * q, 0:1, :] + bias_all[2 * q + 1, 0:1, :]
        )
    inner.finish()
    save(inner_all, inner_out, 2)
    unit_slots = {0: events[25:26], 3: events[26:27], 6: events[27:]}

    def unit_step(j, carry):
        cols = pl.ds(pl.multiple_of(j * 256, 256), 256)
        for b in range(2):
            rows = slice(b * half, (b + 1) * half)
            pre = nt_dot(first_low[rows, :], inner_all[cols, :]) + inner_bias[:, cols]
            gate = 0.5 + 0.5 * lax.erf(pre * 0.7071067811865476)
            on = first_lanes(256, j * 256, kept_units)
            act[rows, cols] = (pre * gate * on).astype(jnp.bfloat16)
            slope[rows, cols] = (
                (gate + pre * jnp.exp(-0.5 * pre * pre) * 0.3989422804014327) * on
            ).astype(jnp.bfloat16)
        for slot, todo in unit_slots.items():

            @pl.when(j == slot)
            def _(todo=todo):
                for event in todo:
                    event()

        return carry

    lax.fori_loop(0, units // 256, unit_step, 0)
    save(act, act_out, 3)
    save(slope, slope_out, 4)
    outer.finish()
    save(outer_all, outer_out, 5)
    for j in range(width // 256):
        cols = slice(j * 256, (j + 1) * 256)
        wide[:, cols] = nn_dot(act[...], outer_all[:, cols])
    small_out[...] = jnp.zeros_like(small_out)

    def second_norm(i, carry):
        rows = pl.ds(pl.multiple_of(i * 128, 128), 128)
        first = normed_out[rows, :] * first_gain + first_shift
        total = first + (wide[rows, :] + outer_bias)
        centred = total - jnp.mean(total, axis=-1, keepdims=True)
        scale = lax.rsqrt(jnp.mean(centred * centred, axis=-1, keepdims=True) + 1e-12)
        normed = centred * scale
        second = normed * second_gain + second_shift
        wide[rows, :] = second
        output[rows, :] = second.astype(jnp.bfloat16)
        grad = out_grad[rows, :].astype(jnp.float32)
        scaled = grad * second_gain
        back = scale * (
            scaled
            - jnp.mean(scaled, axis=-1, keepdims=True)
            - normed * jnp.mean(scaled * normed, axis=-1, keepdims=True)
        )
        sum_grad_out[rows, :] = back
        low = back.astype(jnp.bfloat16).astype(jnp.float32)
        small_out[0:1, :] += jnp.sum(grad * normed, axis=0, keepdims=True)
        small_out[1:2, :] += jnp.sum(grad, axis=0, keepdims=True)
        small_out[2:3, :] += jnp.sum(low, axis=0, keepdims=True)
        return carry

    lax.fori_loop(0, rows_total // 128, second_norm, 0)
    for j in range(SEGS):
        cls_out[j : j + 1, :] = wide[pl.ds(cls_at[0, j], 1), :]
    inner.drain()
    outer.drain()
    for step in range(4):
        bias_hop(step).wait_send()
    for source, target, index in saves:
        pltpu.make_async_copy(source, target, save_sem.at[index]).wait()
    for p in range(pairs):
        pltpu.make_async_copy(
            probs.at[pl.ds(2 * p, 2)], probs_out.at[pl.ds(2 * p, 2)], save_sem.at[6 + p]
        ).wait()


def run_forward(args, share, units, rows_total, width):
    sems = []
    for unused in range(2):
        for count in (3, 3, 3, 3, 4, 4, 8, 8, 8, 8, 8, 8):
            sems.append(pltpu.SemaphoreType.DMA((count,)))
    bf, fp = jnp.bfloat16, jnp.float32
    shape = jax.ShapeDtypeStruct
    vmem = pl.BlockSpec(memory_space=pltpu.VMEM)
    anywhere = pl.BlockSpec(memory_space=pl.ANY)
    smem = pl.BlockSpec(memory_space=pltpu.SMEM)
    in_specs = [vmem] * 15 + [smem, smem, vmem]
    return pl.pallas_call(
        forward_kernel,
        out_shape=(
            shape((rows_total, width), bf),
            shape((SEGS, width), fp),
            shape((units, width), bf),
            shape((units, width), bf),
            shape((HEADS, rows_total, rows_total), bf),
            shape((rows_total, 3 * width), bf),
            shape((rows_total, width), bf),
            shape((rows_total, width), fp),
            shape((rows_total, 1), fp),
            shape((rows_total, units), bf),
            shape((rows_total, units), bf),
            shape((rows_total, width), fp),
            shape((16, width), fp),
        ),
        in_specs=in_specs,
        out_specs=(
            vmem, vmem, anywhere, anywhere, anywhere, anywhere, anywhere, vmem, vmem, anywhere, anywhere, vmem, vmem,
        ),
        scratch_shapes=[
            pltpu.VMEM((units, width), bf),
            pltpu.VMEM((units, width), bf),
            pltpu.VMEM((HEADS, rows_total, rows_total), bf),
            pltpu.VMEM((rows_total, 3 * width), bf),
            pltpu.VMEM((rows_total, width), bf),
            pltpu.VMEM((rows_total, rows_total), fp),
            pltpu.VMEM((rows_total, units), bf),
            pltpu.VMEM((rows_total, units), bf),
            pltpu.VMEM((rows_total, width), bf),
            pltpu.VMEM((rows_total, width), fp),
            pltpu.VMEM((units // share, 8, 2 * share), fp),
            pltpu.VMEM((1, units), fp),
            pltpu.VMEM((1, 3 * width), fp),
            pltpu.SemaphoreType.DMA((7 + HEADS // 2,)),
            pltpu.SemaphoreType.DMA((4,)),
            pltpu.SemaphoreType.DMA((4,)),
        ]
        + sems,
        compiler_params=pltpu.CompilerParams(
            collective_id=0, has_side_effects=True, vmem_limit_bytes=64 * 1024 * 1024 - 65536
        ),
        name="forward",
    )(*args)


def backward_kernel(
    act_in,
    slope_in,
    sum_grad_in,
    outer_in,
    inner_in,
    normed_in,
    joint_in,
    context_in,
    probs_in,
    tokens_in,
    joint_proj_in,
    out_proj_in,
    scale,
    small_in,
    first_gain,
    first_shift,
    widths,
    input_grad,
    summed_out,
    outer_grad,
    inner_grad,
    small_out,
    act,
    slope,
    weight,
    probs,
    joint,
    context,
    normed,
    grad,
    tokens,
    tokens_over,
    out_proj,
    low,
    first_low,
    sums,
    far_c,
    far_x,
    far_y,
    far_z,
    far_v,
    far_w,
    own,
    far_u,
    parts,
    part_c,
    part_a,
    part_b,
    part_z,
    joint_grad,
    context_grad,
    small,
    small_far,
    load_sem,
    probs_sem,
    keep_sem,
    *sems,
):
    place, side = lax.axis_index("ffn"), lax.axis_index("tok")
    core, flank, deep = place % 2, (place // 2) % 2, place // 4
    first_gain, first_shift = row_of(first_gain), row_of(first_shift)
    kept_lanes = kept_of(widths, place, side, 1) * DH
    rows_total, units = act.shape
    width = grad.shape[1]
    half = rows_total // 2
    share = own.shape[1]
    bf, fp = jnp.bfloat16, jnp.float32
    sem_names = (
        "c", "x", "y", "z", "v", "w", "f", "u", "ac", "aa", "ab", "az", "gz", "gb", "ga", "gc", "bt"
    )
    send = dict(zip(sem_names, sems[: len(sem_names)]))
    recv = dict(zip(sem_names, sems[len(sem_names) :]))
    made = {}

    def define(name, index, source, target, device):
        made[(name,) + index] = lambda: remote(
            source(), target(), send[name].at[index], recv[name].at[index], device
        )

    def go(name, *index):
        made[(name,) + index]().start()

    def got(name, *index):
        made[(name,) + index]().wait_recv()

    peer_x, peer_y, peer_c = (place, 1 - side), (y_peer(place), side), (c_peer(place), side)
    peer_z = [None] + [(z_peer(place, turn), side) for turn in (1, 2, 3)]
    deep_of = [z_peer(place, turn) // 4 if turn else deep for turn in range(4)]
    third = share // 2

    def shard(turn, y, c, offset=0, count=None):
        start = ((deep_of[turn] * 2 + y) * 2 + c) * share + offset
        return pl.ds(pl.multiple_of(start, 16), share if count is None else count)

    left, right = slice(0, width // 2), slice(width // 2, width)
    own_part = pl.ds(pl.multiple_of(side * third, 16), third)

    def half_shard(t, y, offset):
        return shard(t, y, core, offset * third, third)

    for m in range(2):
        for t in range(4):
            for y in range(2):
                define(
                    "c", (m, t, y), lambda m=m, t=t, y=y: sums.at[m, shard(t, y, 1 - core)], lambda m=m, t=t, y=y: far_c.at[m, t, y], peer_c
                )
                define(
                    "x", (m, t, y), lambda m=m, t=t, y=y: sums.at[m, half_shard(t, y, 1 - side), left], lambda m=m, t=t, y=y: far_x.at[m, t, y], peer_x
                )
            define(
                "y", (m, t), lambda m=m, t=t: sums.at[m, half_shard(t, 1 - flank, side), left], lambda m=m, t=t: far_y.at[m, t], peer_y
            )
            define(
                "v", (m, t), lambda m=m, t=t: sums.at[m, shard(t, 1 - flank, core), right], lambda m=m, t=t: far_v.at[m, t], peer_y
            )
            if t:
                define(
                    "z", (m, t - 1), lambda m=m, t=t: sums.at[m, half_shard(t, flank, side), left], lambda m=m, t=t: far_z.at[m, t - 1], peer_z[t]
                )
                define(
                    "w", (m, t - 1), lambda m=m, t=t: sums.at[m, shard(t, flank, core), right], lambda m=m, t=t: far_w.at[m, t - 1], peer_z[t]
                )
        define("f", (m,), lambda m=m: own.at[m, own_part, left], lambda m=m: own.at[m, own_part, left], peer_x)
        define("u", (m,), lambda m=m: own.at[m, :, right], lambda m=m: far_u.at[m], peer_x)
    grads = (outer_grad, inner_grad)

    def add(target, source):
        target[...] = (target[...].astype(fp) + source[...].astype(fp)).astype(bf)

    def to_xy(m, t):
        for y in range(2):
            got("c", m, t, y)
            add(sums.at[m, shard(t, y, core)], far_c.at[m, t, y])
            go("x", m, t, y)
        go("v", m, t)

    def x_to_y(m, t):
        for y in range(2):
            got("x", m, t, y)
            add(sums.at[m, half_shard(t, y, side), left], far_x.at[m, t, y])
        go("y", m, t)

    def y_to_z(m, t):
        got("y", m, t)
        add(sums.at[m, half_shard(t, flank, side), left], far_y.at[m, t])
        if t:
            go("z", m, t - 1)

    def v_to_w(m, t):
        got("v", m, t)
        add(sums.at[m, shard(t, flank, core), right], far_v.at[m, t])
        if t:
            go("w", m, t - 1)

    def z_end(m):
        total = sums[m, half_shard(0, flank, side), left].astype(fp)
        for t in range(3):
            got("z", m, t)
            total = total + far_z[m, t].astype(fp)
        own[m, own_part, left] = total.astype(bf)
        go("f", m)

    def w_end(m):
        total = sums[m, shard(0, flank, core), right].astype(fp)
        for t in range(3):
            got("w", m, t)
            total = total + far_w[m, t].astype(fp)
        own[m, :, right] = total.astype(bf)
        go("u", m)

    def f_last(m):
        got("f", m)
        grads[m][:, left] = own[m, :, left].astype(fp)

    def u_last(m):
        got("u", m)
        grads[m][:, right] = own[m, :, right].astype(fp) + far_u[m].astype(fp)

    quarter = width // 2

    def cols_of(c):
        return pl.ds(pl.multiple_of(c * quarter, 128), quarter)

    def rows_of(j, depth, flips=(0, 0), z=None):
        first, second = (side, flank) if j % 2 == 0 else (flank, side)
        if flips[0]:
            first = 1 - first
        if flips[1]:
            second = 1 - second
        start, count = first * (width // 2), width // 2
        if depth > 1:
            start, count = start + second * (width // 4), width // 4
        if depth > 2:
            start, count = start + (deep if z is None else z) * (width // 16), width // 16
        return pl.ds(pl.multiple_of(start, 16), count)

    for j in range(4):
        near, far = (peer_x, peer_y) if j % 2 == 0 else (peer_y, peer_x)
        define("ac", (j,), lambda j=j: parts.at[j, :, cols_of(1 - core)], lambda j=j: part_c.at[j], peer_c)
        define(
            "aa", (j,), lambda j=j: parts.at[j, rows_of(j, 1, (1, 0)), cols_of(core)], lambda j=j: part_a.at[j], near
        )
        define(
            "ab", (j,), lambda j=j: parts.at[j, rows_of(j, 2, (0, 1)), cols_of(core)], lambda j=j: part_b.at[j], far
        )
        for t in (1, 2, 3):
            define(
                "az",
                (j, t - 1),
                lambda j=j, t=t: parts.at[j, rows_of(j, 3, z=deep_of[t]), cols_of(core)],
                lambda j=j, t=t: part_z.at[j, t - 1],
                peer_z[t],
            )
            define(
                "gz",
                (j, t - 1),
                lambda j=j: parts.at[j, rows_of(j, 3), cols_of(core)],
                lambda j=j: summed_out.at[j, rows_of(j, 3), cols_of(core)],
                peer_z[t],
            )

        def place_of(depth, j=j):
            if depth:
                return lambda: summed_out.at[j, rows_of(j, depth), cols_of(core)]
            return lambda: summed_out.at[j, :, cols_of(core)]

        define("gb", (j,), place_of(2), place_of(2), far)
        define("ga", (j,), place_of(1), place_of(1), near)
        define("gc", (j,), place_of(0), place_of(0), peer_c)

    def keep(j):
        return pltpu.make_async_copy(
            parts.at[j, rows_of(j, 3), cols_of(core)], summed_out.at[j, rows_of(j, 3), cols_of(core)], keep_sem.at[j]
        )

    def sum_1(j):
        got("ac", j)
        add(parts.at[j, :, cols_of(core)], part_c.at[j])
        go("aa", j)

    def sum_2(j):
        got("aa", j)
        add(parts.at[j, rows_of(j, 1), cols_of(core)], part_a.at[j])
        go("ab", j)

    def sum_3(j):
        got("ab", j)
        add(parts.at[j, rows_of(j, 2), cols_of(core)], part_b.at[j])
        for t in range(3):
            go("az", j, t)

    def sum_4(j):
        total = parts[j, rows_of(j, 3), cols_of(core)].astype(fp)
        for t in range(3):
            got("az", j, t)
            total = total + part_z[j, t].astype(fp)
        parts[j, rows_of(j, 3), cols_of(core)] = total.astype(bf)
        for t in range(3):
            go("gz", j, t)
        keep(j).start()

    def sum_5(j):
        keep(j).wait()
        for t in range(3):
            remote(
                summed_out.at[j, rows_of(j, 3, z=deep_of[t + 1]), cols_of(core)],
                summed_out.at[j, rows_of(j, 3, z=deep_of[t + 1]), cols_of(core)],
                send["gz"].at[j, t],
                recv["gz"].at[j, t],
                peer_z[t + 1],
            ).wait_recv()
        go("gb", j)

    def arrive(name, j, depth, flips, c=None):
        cols = cols_of(core if c is None else c)
        piece = summed_out.at[j, rows_of(j, depth, flips), cols] if depth else summed_out.at[j, :, cols]
        remote(piece, piece, send[name].at[j], recv[name].at[j], peer_x).wait_recv()

    def sum_6(j):
        arrive("gb", j, 2, (0, 1))
        go("ga", j)

    def sum_7(j):
        arrive("ga", j, 1, (1, 0))
        go("gc", j)

    def sum_8(j):
        arrive("gc", j, 0, (0, 0), 1 - core)

    ring = (peer_c, peer_x, peer_y, peer_z[1], peer_z[2])
    for i, peer in enumerate(ring):
        define("bt", (i,), lambda i=i: small.at[i], lambda i=i: small_far.at[i], peer)

    def small_step(i):
        got("bt", i)
        if i < 4:
            small[i + 1] = small[i] + small_far[i]
            go("bt", i + 1)
        else:
            small_out[...] = small[i] + small_far[i]

    loads = [
        (sum_grad_in, grad),
        (act_in, act),
        (outer_in, weight),
        (slope_in, slope),
        (normed_in, normed),
        (context_in, context),
        (out_proj_in, out_proj),
        (tokens_in, tokens),
        (joint_in, joint),
        (inner_in, weight),
    ]
    for s in range(3):
        block = slice(s * width, (s + 1) * width)
        loads.append((joint_proj_in.at[:, block], weight.at[block]))

    def load(i):
        return pltpu.make_async_copy(loads[i][0], loads[i][1], load_sem.at[i])

    def fetch(p):
        return pltpu.make_async_copy(
            probs_in.at[pl.ds(2 * p, 2)], probs.at[p % 2], probs_sem.at[p % 2]
        )

    for i in range(9):
        load(i).start()
    fetch(0).start()
    greet(place, side)
    small[0] = small_in[...]
    load(0).wait()
    low[...] = grad[...].astype(bf)
    load(1).wait()

    def at_slot(index, table):
        for slot, todo in table.items():

            @pl.when(index == slot)
            def _(todo=todo):
                for event in todo:
                    event()

    def outer_group(t, table):
        base = deep_of[t] * (4 * share)

        def body(i, carry):
            here = pl.ds(pl.multiple_of(base + i * 256, 256), 256)
            sums[0, here, :] = tn_dot(act[:, here], low[...]).astype(bf)
            at_slot(i, table)
            return carry

        lax.fori_loop(0, 4 * share // 256, body, 0)
        for y in range(2):
            go("c", 0, t, y)

    def inner_group(t):
        base = deep_of[t] * (4 * share)

        def body(i, carry):
            here = pl.ds(pl.multiple_of(base + i * 256, 256), 256)
            sums[1, here, :] = tn_dot(act[:, here], first_low[...]).astype(bf)
            return carry

        lax.fori_loop(0, 4 * share // 256, body, 0)
        for y in range(2):
            go("c", 1, t, y)

    outer_group(3, {})
    outer_group(2, {})
    outer_group(1, {})
    outer_group(0, {})
    load(2).wait()
    load(3).wait()
    pre_slots = {0: [lambda: to_xy(0, 3)], 1: [lambda: to_xy(0, 2)], 2: [lambda: to_xy(0, 1)], 4: [lambda: to_xy(0, 0)], 5: [lambda: x_to_y(0, 3), lambda: v_to_w(0, 3)], 10: [lambda: x_to_y(0, 2), lambda: v_to_w(0, 2)]}

    def pre_step(j, carry):
        cols = pl.ds(pl.multiple_of(j * 256, 256), 256)
        for b in range(2):
            rows = slice(b * half, (b + 1) * half)
            back = nt_dot(low[rows, :], weight[cols, :])
            act[rows, cols] = (back * slope[rows, cols].astype(fp)).astype(bf)
        bias_cols = pl.ds(pl.multiple_of((j % 3) * 256, 256), 256)
        small[0, pl.ds(8 + j // 3, 1), bias_cols] = jnp.sum(
            act[:, cols].astype(fp), axis=0, keepdims=True
        )
        at_slot(j, pre_slots)
        return carry

    lax.fori_loop(0, units // 256, pre_step, 0)
    load(9).start()
    load(4).wait()

    def first_step(i, carry):
        rows = pl.ds(pl.multiple_of(i * 128, 128), 128)
        first_low[rows, :] = (normed[rows, :] * first_gain + first_shift).astype(bf)
        return carry

    lax.fori_loop(0, rows_total // 128, first_step, 0)
    inner_group(3)
    x_to_y(0, 1)
    v_to_w(0, 1)
    load(9).wait()
    back_slots = {1: [lambda: x_to_y(0, 0), lambda: v_to_w(0, 0)], 2: [lambda: to_xy(1, 3), lambda: y_to_z(0, 3), lambda: y_to_z(0, 2)]}
    for j in range(width // 256):
        cols = slice(j * 256, (j + 1) * 256)
        grad[:, cols] += nn_dot(act[...], weight[:, cols])
        for event in back_slots.get(j, []):
            event()

    for i in range(10, 13):
        load(i).start()

    def norm_step(i, carry):
        rows = pl.ds(pl.multiple_of(i * 128, 128), 128)
        incoming, unit = grad[rows, :], normed[rows, :]
        small[0, 3:4, :] += jnp.sum(incoming * unit, axis=0, keepdims=True)
        small[0, 4:5, :] += jnp.sum(incoming, axis=0, keepdims=True)
        scaled = incoming * first_gain
        back = scale[rows, :] * (
            scaled
            - jnp.mean(scaled, axis=-1, keepdims=True)
            - unit * jnp.mean(scaled * unit, axis=-1, keepdims=True)
        )
        grad[rows, :] = back
        back_low = back.astype(bf)
        low[rows, :] = back_low
        small[0, 5:6, :] += jnp.sum(back_low.astype(fp), axis=0, keepdims=True)
        return carry

    lax.fori_loop(0, rows_total // 128, norm_step, 0)

    load(5).wait()
    out_slots = {0: [lambda: y_to_z(0, 1)], 2: [lambda: go("ac", 0), lambda: w_end(0), lambda: y_to_z(0, 0)]}
    for j in range(width // 256):
        cols = slice(j * 256, (j + 1) * 256)
        parts[0, cols, :] = tn_dot(context[:, cols], low[...]).astype(bf)
        for event in out_slots.get(j, []):
            event()
    load(6).wait()
    context_slots = {2: [lambda: inner_group(2), lambda: x_to_y(1, 3), lambda: v_to_w(1, 3)]}
    for j in range(width // 256):
        cols = slice(j * 256, (j + 1) * 256)
        context_grad[:, cols] = (
            nt_dot(low[...], out_proj[cols, :]) * first_lanes(256, j * 256, kept_lanes)
        ).astype(bf)
        for event in context_slots.get(j, []):
            event()
    load(7).wait()
    for j in range(width // 128):
        cols = slice(j * 128, (j + 1) * 128)
        tokens_over[cols, :] = tokens[:, cols].T
    sum_1(0)
    load(8).wait()
    first_half = (lax.broadcasted_iota(jnp.int32, (1, 128), 1) < DH).astype(bf)
    halves = (first_half, 1 - first_half)
    factor = 1.0 / math.sqrt(DH)
    pairs = HEADS // 2
    pair_slots = (
        {0: [lambda: u_last(0), lambda: z_end(0)], 5: [lambda: sum_1(2)]},
        {0: [lambda: to_xy(1, 2), lambda: y_to_z(1, 3)], 1: [lambda: go("ac", 1)], 2: [lambda: sum_2(0), lambda: v_to_w(1, 2), lambda: inner_group(1), lambda: f_last(0), lambda: sum_1(1)], 3: [lambda: go("ac", 2), lambda: x_to_y(1, 2), lambda: to_xy(1, 1), lambda: sum_3(0)], 5: [lambda: go("ac", 3), lambda: x_to_y(1, 1), lambda: sum_2(1)]},
    )

    def pair_step(p, carry):
        @pl.when(p + 1 < pairs)
        def _():
            fetch(p + 1).start()

        fetch(p).wait()
        slot = p % 2
        cols = [pl.ds(pl.multiple_of(s * width + p * 128, 128), 128) for s in range(3)]
        out_cols = pl.ds(pl.multiple_of(p * 128, 128), 128)
        keys, values = joint[:, cols[1]], joint[:, cols[2]]
        value_part, key_part = None, None
        for b in range(2):
            lanes = slice(b * half, (b + 1) * half)
            queries, incoming = joint[lanes, cols[0]], context_grad[lanes, out_cols]
            query_part = None
            for a in range(2):
                weights_low = probs[slot, a, :, lanes]
                weights = weights_low.astype(fp)
                product = nt_dot(values * halves[a], incoming) * weights
                score_grad = (
                    product - weights * jnp.sum(product, axis=0, keepdims=True)
                ).astype(bf)
                part = nn_dot(weights_low, incoming * halves[a])
                value_part = part if value_part is None else value_part + part
                part = nn_dot(score_grad, queries * halves[a])
                key_part = part if key_part is None else key_part + part
                part = tn_dot(score_grad, keys * halves[a])
                query_part = part if query_part is None else query_part + part
            joint_grad[lanes, cols[0]] = (query_part * factor).astype(bf)
        joint_grad[:, cols[1]] = (key_part * factor).astype(bf)
        joint_grad[:, cols[2]] = value_part.astype(bf)
        small[0, 6:7, out_cols] = jnp.sum(
            joint_grad[:, cols[0]].astype(fp), axis=0, keepdims=True
        )
        small[0, 7:8, out_cols] = jnp.sum(
            joint_grad[:, cols[2]].astype(fp), axis=0, keepdims=True
        )
        at_slot(p, pair_slots[0])

        @pl.when(p % 2 == 1)
        def _():
            index = (p + 1) // 2
            for s in range(3):
                source = pl.ds(pl.multiple_of(s * width + (index - 1) * 256, 256), 256)
                parts[index, :, s * 256 : (s + 1) * 256] = nn_dot(
                    tokens_over[...], joint_grad[:, source]
                ).astype(bf)

        at_slot(p, pair_slots[1])
        return carry

    lax.fori_loop(0, pairs, pair_step, 0)
    for i in range(10, 13):
        load(i).wait()
    last_slots = {0: [lambda: go("bt", 0), lambda: y_to_z(1, 2)], 2: [lambda: inner_group(0), lambda: sum_4(0), lambda: sum_1(3), lambda: v_to_w(1, 1), lambda: small_step(0)]}
    for j in range(width // 256):
        cols = slice(j * 256, (j + 1) * 256)
        total = grad[:, cols]
        for s in range(3):
            block = slice(s * width, (s + 1) * width)
            rows = slice(s * width + j * 256, s * width + (j + 1) * 256)
            total = total + nt_dot(joint_grad[:, block], weight[rows, :])
        grad[:, cols] = total
        if j == 2:
            pltpu.make_async_copy(grad, input_grad, keep_sem.at[4]).start()
        for event in last_slots.get(j, []):
            event()
    y_to_z(1, 1)
    sum_2(2)
    to_xy(1, 0)
    sum_3(1)
    small_step(1)
    sum_5(0)
    sum_2(3)
    x_to_y(1, 0)
    sum_3(2)
    sum_3(3)
    v_to_w(1, 0)
    w_end(1)
    small_step(2)
    sum_4(1)
    sum_6(0)
    u_last(1)
    y_to_z(1, 0)
    z_end(1)
    sum_4(2)
    sum_7(0)
    sum_4(3)
    small_step(3)
    f_last(1)
    sum_8(0)
    sum_5(1)
    sum_6(1)
    sum_5(2)
    sum_5(3)
    sum_7(1)
    small_step(4)
    sum_6(2)
    sum_8(1)
    sum_6(3)
    sum_7(2)
    sum_7(3)
    sum_8(2)
    sum_8(3)
    result = pltpu.make_async_copy(grad, input_grad, keep_sem.at[4])
    result.wait()
    for build in made.values():
        build().wait_send()


def run_backward(args, share, units, rows_total, width):
    bf, fp = jnp.bfloat16, jnp.float32
    shape = jax.ShapeDtypeStruct
    vmem = pl.BlockSpec(memory_space=pltpu.VMEM)
    anywhere = pl.BlockSpec(memory_space=pl.ANY)
    third = share // 2
    counts = [
        (2, 4, 2), (2, 4, 2), (2, 4), (2, 3), (2, 4), (2, 3), (2,), (2,),
        (4,), (4,), (4,), (4, 3), (4, 3), (4,), (4,), (4,), (5,),
    ]
    sems = [pltpu.SemaphoreType.DMA(count) for unused in range(2) for count in counts]
    quarter = width // 2
    return pl.pallas_call(
        backward_kernel,
        out_shape=(
            shape((rows_total, width), fp),
            shape((4, width, width), bf),
            shape((share, width), fp),
            shape((share, width), fp),
            shape((16, width), fp),
        ),
        in_specs=[anywhere] * 12 + [vmem] * 4 + [pl.BlockSpec(memory_space=pltpu.SMEM)],
        out_specs=(anywhere, anywhere, vmem, vmem, vmem),
        scratch_shapes=[
            pltpu.VMEM((rows_total, units), bf),
            pltpu.VMEM((rows_total, units), bf),
            pltpu.VMEM((units, width), bf),
            pltpu.VMEM((2, 2, rows_total, rows_total), bf),
            pltpu.VMEM((rows_total, 3 * width), bf),
            pltpu.VMEM((rows_total, width), bf),
            pltpu.VMEM((rows_total, width), fp),
            pltpu.VMEM((rows_total, width), fp),
            pltpu.VMEM((rows_total, width), bf),
            pltpu.VMEM((width, rows_total), bf),
            pltpu.VMEM((width, width), bf),
            pltpu.VMEM((rows_total, width), bf),
            pltpu.VMEM((rows_total, width), bf),
            pltpu.VMEM((2, units, width), bf),
            pltpu.VMEM((2, 4, 2, share, width), bf),
            pltpu.VMEM((2, 4, 2, third, quarter), bf),
            pltpu.VMEM((2, 4, third, quarter), bf),
            pltpu.VMEM((2, 3, third, quarter), bf),
            pltpu.VMEM((2, 4, share, quarter), bf),
            pltpu.VMEM((2, 3, share, quarter), bf),
            pltpu.VMEM((2, share, width), bf),
            pltpu.VMEM((2, share, quarter), bf),
            pltpu.VMEM((4, width, width), bf),
            pltpu.VMEM((4, width, quarter), bf),
            pltpu.VMEM((4, width // 2, quarter), bf),
            pltpu.VMEM((4, width // 4, quarter), bf),
            pltpu.VMEM((4, 3, width // 16, quarter), bf),
            pltpu.VMEM((rows_total, 3 * width), bf),
            pltpu.VMEM((rows_total, width), bf),
            pltpu.VMEM((5, 16, width), fp),
            pltpu.VMEM((5, 16, width), fp),
            pltpu.SemaphoreType.DMA((13,)),
            pltpu.SemaphoreType.DMA((2,)),
            pltpu.SemaphoreType.DMA((5,)),
        ]
        + sems,
        compiler_params=pltpu.CompilerParams(
            collective_id=1, has_side_effects=True, vmem_limit_bytes=64 * 1024 * 1024 - 65536
        ),
        name="backward",
    )(*args)


def on_device_fast(
    tokens,
    joint_proj,
    query_bias,
    value_bias,
    out_proj,
    out_bias,
    first_gain,
    first_shift,
    inner_proj,
    inner_bias,
    outer_proj,
    outer_bias,
    second_gain,
    second_shift,
    segment_ids,
    cls_positions,
    widths,
    out_grad,
):
    tok_rows, model_width = tokens.shape
    unit_share = inner_proj.shape[1]
    ffn_count = lax.axis_size("ffn")
    ffn_place = lax.axis_index("ffn")
    unit_total = unit_share * ffn_count
    shifted = jnp.arange(2 * unit_share, dtype=jnp.int32) // unit_share == ffn_place % 2
    bias_block = jnp.where(shifted, jnp.tile(inner_bias, 2).astype(jnp.float32), 0.0)
    bias_block = jnp.broadcast_to(bias_block, (8, 2 * unit_share))
    (
        output, cls_states, inner_rows, outer_rows, probs_again, joint_flat, context_low,
        first_normed, first_scale, act_low, slope_low, sum_grad, small_a,
    ) = run_forward(
        (
            tokens, joint_proj, query_bias, value_bias, out_proj, out_bias, first_gain, first_shift,
            inner_proj.T, outer_proj, bias_block, outer_bias, second_gain, second_shift,
            segment_ids[None], widths, cls_positions, out_grad,
        ),
        unit_share, unit_total, tok_rows, model_width,
    )
    input_grad, summed, outer_part, inner_part, small = run_backward(
        (
            act_low, slope_low, sum_grad, outer_rows, inner_rows, first_normed, joint_flat,
            context_low, probs_again, tokens, joint_proj, out_proj, first_scale, small_a,
            first_gain, first_shift, widths,
        ),
        unit_share, unit_total, tok_rows, model_width,
    )
    cls_states = cls_states[None]
    outer_proj_grad = outer_part
    inner_proj_grad = inner_part.T
    out_proj_grad = summed[0].astype(jnp.float32)
    joint_proj_grad = jnp.concatenate(
        [summed[1 + i, :, s * 256 : (s + 1) * 256] for s in range(3) for i in range(3)], axis=1
    ).astype(jnp.float32)
    second_gain_grad, second_shift_grad, outer_bias_grad = small[0], small[1], small[2]
    first_gain_grad, first_shift_grad, out_bias_grad = small[3], small[4], small[5]
    query_bias_grad, value_bias_grad = small[6], small[7]
    inner_bias_grad = lax.dynamic_slice(
        small[8:12].reshape(-1), (ffn_place * unit_share,), (unit_share,)
    )
    return (
        output,
        cls_states,
        input_grad,
        joint_proj_grad,
        query_bias_grad,
        value_bias_grad,
        out_proj_grad,
        out_bias_grad,
        first_gain_grad,
        first_shift_grad,
        inner_proj_grad,
        inner_bias_grad,
        outer_proj_grad,
        outer_bias_grad,
        second_gain_grad,
        second_shift_grad,
    )


def solution(mesh):
    return jax.shard_map(
        on_device_fast if mesh.shape["ffn"] == 16 and mesh.shape["tok"] == 2 else on_device,
        mesh=mesh,
        in_specs=(
            P(("ffn", "tok"), None),
            P(),
            P(),
            P(),
            P(),
            P(),
            P(),
            P(),
            P(None, "ffn"),
            P("ffn"),
            P("ffn", None),
            P(),
            P(),
            P(),
            P(("ffn", "tok")),
            P(("ffn", "tok"), None),
            P(),
            P(("ffn", "tok"), None),
        ),
        out_specs=(
            P(("ffn", "tok"), None),
            P(("ffn", "tok"), None, None),
            P(("ffn", "tok"), None),
            P(),
            P(),
            P(),
            P(),
            P(),
            P(),
            P(),
            P(None, "ffn"),
            P("ffn"),
            P("ffn", None),
            P(),
            P(),
            P(),
        ),
        check_vma=False,
    )
```

```python
import math

import jax
import jax.numpy as jnp
from jax import lax
from jax.experimental import pallas as pl
from jax.experimental.pallas import tpu as pltpu
from jax.sharding import PartitionSpec as P

MESH = pl.DeviceIdType.MESH
HEADS = 12
DH = 64
MB = 2
SEGS = 4


def normalize(inputs, gain_vec, shift_vec):
    row_mean = jnp.mean(inputs, axis=-1, keepdims=True)
    centred = inputs - row_mean
    row_scale = lax.rsqrt(jnp.mean(centred * centred, axis=-1, keepdims=True) + 1e-12)
    normed = centred * row_scale
    return (normed * gain_vec + shift_vec, normed, row_scale)


def normalize_back(incoming, normed, row_scale, gain_vec):
    gain_grad = jnp.sum(incoming * normed, axis=0)
    shift_grad = jnp.sum(incoming, axis=0)
    scaled_grad = incoming * gain_vec
    inputs_grad = row_scale * (
        scaled_grad
        - jnp.mean(scaled_grad, axis=-1, keepdims=True)
        - normed * jnp.mean(scaled_grad * normed, axis=-1, keepdims=True)
    )
    return (inputs_grad, gain_grad, shift_grad)


def gelu_slope(inputs):
    return (
        0.5 * (1.0 + lax.erf(inputs * 0.7071067811865476))
        + inputs * jnp.exp(-0.5 * inputs * inputs) * 0.3989422804014327
    )


def contract_rows(left_side, right_side):
    return lax.dot_general(
        left_side, right_side, (((0,), (0,)), ((), ())), preferred_element_type=jnp.float32
    )


def contract_cols(left_side, right_side):
    return lax.dot_general(
        left_side, right_side, (((1,), (1,)), ((), ())), preferred_element_type=jnp.float32
    )


def on_device(
    tokens,
    joint_proj,
    query_bias,
    value_bias,
    out_proj,
    out_bias,
    first_gain,
    first_shift,
    inner_proj,
    inner_bias,
    outer_proj,
    outer_bias,
    second_gain,
    second_shift,
    segment_ids,
    cls_positions,
    widths,
    out_grad,
):
    tok_rows, model_width = tokens.shape
    seq_rows = cls_positions.shape[0]
    seq_len = tok_rows // seq_rows
    unit_share = inner_proj.shape[1]
    ffn_count = lax.axis_size("ffn")
    tok_count = lax.axis_size("tok")
    ffn_place = lax.axis_index("ffn")
    tok_place = lax.axis_index("tok")
    per_group = seq_rows * ffn_count * tok_count // MB
    batches = jnp.arange(MB, dtype=jnp.int32)
    own_group = (ffn_place * tok_count + tok_place) * seq_rows // per_group
    own_pick = (batches == own_group).astype(jnp.int32)
    heads_kept = jnp.sum(own_pick * widths[:, 1])
    head_on = (jnp.arange(HEADS, dtype=jnp.int32) < heads_kept).astype(jnp.float32)
    factor = 1.0 / math.sqrt(DH)
    zero_bias = jnp.zeros((model_width,), jnp.bfloat16)
    joint_bias = jnp.concatenate([query_bias, zero_bias, value_bias])
    joint_low = (
        jnp.dot(tokens, joint_proj, preferred_element_type=jnp.float32) + joint_bias
    ).astype(jnp.bfloat16)
    joint_low = joint_low.reshape(seq_rows, seq_len, 3, HEADS, DH)
    queries = joint_low[:, :, 0]
    key_heads = joint_low[:, :, 1]
    value_heads = joint_low[:, :, 2]
    segments = segment_ids.reshape(seq_rows, seq_len)
    same_doc = (segments[:, :, None] == segments[:, None, :])[:, None]

    def scores_of(query_rows, key_rows):
        raw_scores = (
            jnp.einsum("rqhd,rkhd->rhqk", query_rows, key_rows, preferred_element_type=jnp.float32)
            * factor
        )
        return jnp.where(same_doc, raw_scores, -1e30)

    scores = scores_of(queries, key_heads)
    row_peak = jnp.max(scores, axis=-1, keepdims=True)
    log_total = row_peak + jnp.log(jnp.sum(jnp.exp(scores - row_peak), axis=-1, keepdims=True))
    probs_low = jnp.exp(scores - log_total).astype(jnp.bfloat16)
    context = (
        jnp.einsum("rhqk,rkhd->rqhd", probs_low, value_heads, preferred_element_type=jnp.float32)
        * head_on[:, None]
    )
    context_low = context.astype(jnp.bfloat16).reshape(tok_rows, model_width)
    attn_out = jnp.dot(context_low, out_proj, preferred_element_type=jnp.float32) + out_bias
    first_out, first_normed, first_scale = normalize(
        tokens.astype(jnp.float32) + attn_out, first_gain, first_shift
    )
    first_low = first_out.astype(jnp.bfloat16)
    unit_total = unit_share * ffn_count
    stacked = lax.all_gather(
        jnp.stack([inner_proj.T, outer_proj]), "ffn", axis=1, tiled=True
    )
    inner_rows, outer_rows = stacked[0], stacked[1]
    inner_bias_all = lax.all_gather(inner_bias, "ffn", axis=0, tiled=True)
    own_kept = jnp.sum(own_pick * widths[:, 0])
    neuron_on = (jnp.arange(unit_total, dtype=jnp.int32) < own_kept).astype(jnp.float32)
    pre_act = contract_cols(first_low, inner_rows) + inner_bias_all
    act_low = (jax.nn.gelu(pre_act, approximate=False) * neuron_on).astype(jnp.bfloat16)
    ffn_out = jnp.dot(act_low, outer_rows, preferred_element_type=jnp.float32) + outer_bias
    second_out, second_normed, second_scale = normalize(
        first_out + ffn_out, second_gain, second_shift
    )
    output = second_out.astype(jnp.bfloat16)
    cls_states = jnp.take_along_axis(
        second_out.reshape(seq_rows, seq_len, model_width), cls_positions[:, :, None], axis=1
    )
    sum_grad, second_gain_grad, second_shift_grad = normalize_back(
        out_grad.astype(jnp.float32), second_normed, second_scale, second_gain
    )
    ffn_grad = sum_grad.astype(jnp.bfloat16)
    outer_bias_grad = jnp.sum(ffn_grad.astype(jnp.float32), axis=0)
    outer_proj_grad = contract_rows(act_low, ffn_grad)
    act_grad = contract_cols(ffn_grad, outer_rows)
    pre_grad = (act_grad * (gelu_slope(pre_act) * neuron_on)).astype(jnp.bfloat16)
    inner_bias_sum = jnp.sum(pre_grad.astype(jnp.float32), axis=0)
    inner_rows_grad = contract_rows(pre_grad, first_low)
    first_back = jnp.dot(pre_grad, inner_rows, preferred_element_type=jnp.float32)
    unit_grads = jnp.stack(
        [inner_rows_grad.astype(jnp.bfloat16), outer_proj_grad.astype(jnp.bfloat16)]
    )
    unit_grads = lax.psum_scatter(unit_grads, "ffn", scatter_dimension=1, tiled=True)
    unit_grads = lax.psum(unit_grads, "tok").astype(jnp.float32)
    inner_proj_grad, outer_proj_grad = unit_grads[0].T, unit_grads[1]
    first_grad = sum_grad + first_back
    attn_sum_grad, first_gain_grad, first_shift_grad = normalize_back(
        first_grad, first_normed, first_scale, first_gain
    )
    attn_grad = attn_sum_grad.astype(jnp.bfloat16)
    out_bias_grad = jnp.sum(attn_grad.astype(jnp.float32), axis=0)
    out_proj_grad = contract_rows(context_low, attn_grad)
    context_grad = (
        contract_cols(attn_grad, out_proj)
        .astype(jnp.bfloat16)
        .reshape(seq_rows, seq_len, HEADS, DH)
    )
    context_grad = context_grad * head_on.astype(jnp.bfloat16)[:, None]
    scores = scores_of(queries, key_heads)
    probs = jnp.exp(scores - log_total)
    probs_again = probs.astype(jnp.bfloat16)
    value_part = jnp.einsum(
        "rhqk,rqhd->rkhd", probs_again, context_grad, preferred_element_type=jnp.float32
    )
    prob_grad = jnp.einsum(
        "rqhd,rkhd->rhqk", context_grad, value_heads, preferred_element_type=jnp.float32
    )
    score_grad = (probs * (prob_grad - jnp.sum(probs * prob_grad, axis=-1, keepdims=True))).astype(
        jnp.bfloat16
    )
    query_part = (
        jnp.einsum("rhqk,rkhd->rqhd", score_grad, key_heads, preferred_element_type=jnp.float32)
        * factor
    )
    key_part = (
        jnp.einsum("rhqk,rqhd->rkhd", score_grad, queries, preferred_element_type=jnp.float32)
        * factor
    )
    joint_grad = (
        jnp.stack([query_part, key_part, value_part], axis=2)
        .astype(jnp.bfloat16)
        .reshape(tok_rows, 3 * model_width)
    )
    joint_bias_grad = jnp.sum(joint_grad.astype(jnp.float32), axis=0)
    query_bias_grad = joint_bias_grad[:model_width]
    value_bias_grad = joint_bias_grad[2 * model_width :]
    joint_proj_grad = contract_rows(tokens, joint_grad)
    input_grad = attn_sum_grad + contract_cols(joint_grad, joint_proj)
    joint_proj_grad, out_proj_grad = lax.psum(
        (joint_proj_grad.astype(jnp.bfloat16), out_proj_grad.astype(jnp.bfloat16)),
        ("ffn", "tok"),
    )
    joint_proj_grad = joint_proj_grad.astype(jnp.float32)
    out_proj_grad = out_proj_grad.astype(jnp.float32)
    small = [
        query_bias_grad,
        value_bias_grad,
        out_bias_grad,
        first_gain_grad,
        first_shift_grad,
        outer_bias_grad,
        second_gain_grad,
        second_shift_grad,
        inner_bias_sum,
    ]
    small = lax.psum(jnp.concatenate(small), ("ffn", "tok"))
    (
        query_bias_grad,
        value_bias_grad,
        out_bias_grad,
        first_gain_grad,
        first_shift_grad,
        outer_bias_grad,
        second_gain_grad,
        second_shift_grad,
    ) = [small[i * model_width : (i + 1) * model_width] for i in range(8)]
    inner_bias_grad = lax.dynamic_slice(
        small, (8 * model_width + ffn_place * unit_share,), (unit_share,)
    )
    return (
        output,
        cls_states,
        input_grad,
        joint_proj_grad,
        query_bias_grad,
        value_bias_grad,
        out_proj_grad,
        out_bias_grad,
        first_gain_grad,
        first_shift_grad,
        inner_proj_grad,
        inner_bias_grad,
        outer_proj_grad,
        outer_bias_grad,
        second_gain_grad,
        second_shift_grad,
    )


def x_or1(v):
    return v + 1 - 2 * (v % 2)


def x_or2(v):
    return v + 2 - 4 * ((v // 2) % 2)


def z_peer(place, turn):
    deep = place // 4
    if turn & 1:
        deep = x_or1(deep)
    if turn & 2:
        deep = x_or2(deep)
    return deep * 4 + place % 4


def y_peer(place):
    return (place // 4) * 4 + ((place // 2 + 1) % 2) * 2 + place % 2


def c_peer(place):
    return x_or1(place)


def nt_dot(left_side, right_side):
    return lax.dot_general(
        left_side, right_side, (((1,), (1,)), ((), ())), preferred_element_type=jnp.float32
    )


def tn_dot(left_side, right_side):
    return lax.dot_general(
        left_side, right_side, (((0,), (0,)), ((), ())), preferred_element_type=jnp.float32
    )


def nn_dot(left_side, right_side):
    return lax.dot_general(
        left_side, right_side, (((1,), (0,)), ((), ())), preferred_element_type=jnp.float32
    )


def greet(place, side):
    barrier = pltpu.get_barrier_semaphore()
    peers = [
        (z_peer(place, 1), side),
        (z_peer(place, 2), side),
        (z_peer(place, 3), side),
        (y_peer(place), side),
        (c_peer(place), side),
        (place, 1 - side),
    ]
    for peer in peers:
        pl.semaphore_signal(barrier, inc=1, device_id=peer, device_id_type=MESH)
    pl.semaphore_wait(barrier, 6)


def remote(source, target, send_sem, recv_sem, device):
    return pltpu.make_async_remote_copy(
        src_ref=source,
        dst_ref=target,
        send_sem=send_sem,
        recv_sem=recv_sem,
        device_id=device,
        device_id_type=MESH,
    )


class Spread:
    def __init__(self, own, whole, place, side, rows, sems):
        self.own, self.whole, self.place, self.side, self.rows = own, whole, place, side, rows
        self.up_s, self.up_r, self.dn_s, self.dn_r, self.y_s, self.y_r = sems[:6]
        self.x_s, self.x_r, self.c_s, self.c_r, self.d_s, self.d_r = sems[6:]
        self.third = rows // 3
        self.deep = place // 4

    def span(self, source, offset, count):
        start = pl.multiple_of(source * self.rows + offset, 16)
        return self.whole.at[pl.ds(start, count)]

    def slab(self, source):
        return self.span(source, self.side * self.third, 2 * self.third)

    def edge(self, source, mine=True):
        side = self.side if mine else 1 - self.side
        return self.span(source, side * 2 * self.third, self.third)

    def own_slab(self):
        start = pl.multiple_of(self.side * self.third, 16)
        return self.own.at[pl.ds(start, 2 * self.third)]

    def source_of(self, step, up, cross=False):
        base = y_peer(self.place) if cross else self.place
        if step is None:
            return base
        return base - 4 * (step + 1) if up else base + 4 * (step + 1)

    def has(self, step, up):
        if step is None:
            return None
        return self.deep >= step + 1 if up else self.deep + step + 1 <= 3

    def hop(self, step, up, first=False):
        source = self.place if step == 0 else self.source_of(step - 1, up)
        piece = self.own_slab() if step == 0 else self.slab(source)
        send, recv = (self.up_s, self.up_r) if up else (self.dn_s, self.dn_r)
        device = (self.place + 4 if up else self.place - 4, self.side)
        return remote(piece, self.slab(source), send.at[step], recv.at[step], device)

    def hop_in(self, step, up):
        source = self.source_of(step, up)
        send, recv = (self.up_s, self.up_r) if up else (self.dn_s, self.dn_r)
        return remote(
            self.slab(source), self.slab(source), send.at[step], recv.at[step], (self.place, 1 - self.side)
        )

    def over_y(self, source, own=False):
        index = source // 4
        piece = self.own_slab() if own else self.slab(source)
        return remote(
            piece, self.slab(source), self.y_s.at[index], self.y_r.at[index], (y_peer(self.place), self.side)
        )

    def over_x(self, source, mine=True):
        index = source // 2
        piece = self.edge(source, mine)
        return remote(
            piece, piece, self.x_s.at[index], self.x_r.at[index], (self.place, 1 - self.side)
        )

    def over_c(self, source):
        index = source // 2
        return remote(
            self.slab(source),
            self.slab(source),
            self.c_s.at[index],
            self.c_r.at[index],
            (c_peer(self.place), self.side),
        )

    def over_d(self, source):
        index = source // 2
        piece = self.edge(source, False)
        return remote(piece, piece, self.d_s.at[index], self.d_r.at[index], (c_peer(self.place), self.side))

    def over_own(self):
        index = self.place // 2
        return remote(
            self.own,
            self.span(self.place, 0, self.rows),
            self.c_s.at[index],
            self.c_r.at[index],
            (c_peer(self.place), self.side),
        )

    def start(self):
        @pl.when(self.deep < 3)
        def _():
            self.hop(0, True).start()

        @pl.when(self.deep > 0)
        def _():
            self.hop(0, False).start()

        self.over_y(self.place, own=True).start()
        self.over_own().start()

    def z_event(self, step):
        for up in (True, False):

            @pl.when(self.has(step, up))
            def _(up=up):
                source = self.source_of(step, up)
                self.hop_in(step, up).wait_recv()
                if step < 2:

                    @pl.when(self.deep < 3 if up else self.deep > 0)
                    def _():
                        self.hop(step + 1, up).start()

                self.over_y(source).start()
                self.over_x(source).start()
                self.over_c(source).start()

    def each(self, step, work):
        if step is None:
            work(True)
            return
        for up in (True, False):

            @pl.when(self.has(step, up))
            def _(up=up):
                work(up)

    def y_event(self, step):
        def work(up):
            source = self.source_of(step, up, cross=True)
            self.over_y(source).wait_recv()
            self.over_x(source).start()
            self.over_c(source).start()

        self.each(step, work)

    def x_event(self, step, cross):
        def work(up):
            source = self.source_of(step, up, cross=cross)
            self.over_x(source, False).wait_recv()
            self.over_d(source).start()

        self.each(step, work)

    def finish(self):
        other = c_peer(self.place) % 2
        own = c_peer(self.place)
        for index in range(8):
            source = 2 * index + other

            @pl.when(source != own)
            def _(source=source):
                self.over_c(source).wait_recv()
                self.over_d(source).wait_recv()

            @pl.when(source == own)
            def _(source=source):
                remote(
                    self.own,
                    self.span(source, 0, self.rows),
                    self.c_s.at[index],
                    self.c_r.at[index],
                    (c_peer(self.place), self.side),
                ).wait_recv()

    def drain(self):
        for up in (True, False):
            for step in range(3):
                limit = self.deep < 3 if up else self.deep > 0
                if step > 0:
                    limit = jnp.logical_and(limit, self.has(step - 1, up))

                @pl.when(limit)
                def _(step=step, up=up):
                    self.hop(step, up).wait_send()

        for index in range(4):
            source = 4 * index + self.place % 4
            self.over_y(source).wait_send()
        mine = self.place % 2
        for index in range(8):
            source = 2 * index + mine

            @pl.when(source != self.place)
            def _(source=source):
                self.over_x(source).wait_send()
                self.over_c(source).wait_send()
                self.over_d(source).wait_send()

            @pl.when(source == self.place)
            def _():
                self.over_own().wait_send()


def row_of(vector):
    return vector[...].astype(jnp.float32).reshape(1, vector.shape[0])


def kept_of(widths, place, side, kind):
    return widths[(place * 2 + side) * MB // 32, kind]


def first_lanes(count, start, kept):
    lane = lax.broadcasted_iota(jnp.int32, (1, count), 1) + start
    return jnp.where(lane < kept, 1.0, 0.0)


def forward_kernel(
    tokens,
    joint_proj,
    query_bias,
    value_bias,
    out_proj,
    out_bias,
    first_gain,
    first_shift,
    inner_own,
    outer_own,
    bias_own,
    outer_bias,
    second_gain,
    second_shift,
    seg_over,
    widths,
    cls_at,
    out_grad,
    output,
    cls_out,
    inner_out,
    outer_out,
    probs_out,
    joint_out,
    context_out,
    normed_out,
    scale_out,
    act_out,
    slope_out,
    sum_grad_out,
    small_out,
    inner_all,
    outer_all,
    probs,
    joint,
    context,
    mask_bias,
    act,
    slope,
    first_low,
    wide,
    bias_all,
    inner_bias,
    joint_bias,
    save_sem,
    bias_send,
    bias_recv,
    *sems,
):
    place, side = lax.axis_index("ffn"), lax.axis_index("tok")
    out_bias, outer_bias = row_of(out_bias), row_of(outer_bias)
    first_gain, first_shift = row_of(first_gain), row_of(first_shift)
    second_gain, second_shift = row_of(second_gain), row_of(second_shift)
    rows_total = tokens.shape[0]
    units = inner_all.shape[0]
    share = inner_own.shape[0]
    width = tokens.shape[1]
    half = rows_total // 2
    kept_units = kept_of(widths, place, side, 0)
    own_bias = pltpu.make_async_copy(bias_own, bias_all.at[place], save_sem.at[12])
    own_bias.start()
    joint_bias[:, 0:width] = row_of(query_bias)
    joint_bias[:, width : 2 * width] = jnp.zeros((1, width), jnp.float32)
    joint_bias[:, 2 * width :] = row_of(value_bias)
    own_bias.wait()

    def bias_hop(step):
        peer = (c_peer(place), y_peer(place), z_peer(place, 1), z_peer(place, 2))[step]
        count = 1 << step
        piece = bias_all.at[pl.ds(place // count * count, count)]
        return remote(piece, piece, bias_send.at[step], bias_recv.at[step], (peer, side))

    def bias_event(step):
        bias_hop(step - 1).wait_recv()
        if step < 4:
            bias_hop(step).start()

    greet(place, side)
    inner = Spread(inner_own, inner_all, place, side, share, sems[:12])
    outer = Spread(outer_own, outer_all, place, side, share, sems[12:])
    inner.start()
    outer.start()
    bias_hop(0).start()
    own_rows = pl.ds(pl.multiple_of(place * share, 16), share)
    inner_all[own_rows, :] = inner_own[...]
    outer_all[own_rows, :] = outer_own[...]
    saves = []

    def save(source, target, index):
        pltpu.make_async_copy(source, target, save_sem.at[index]).start()
        saves.append((source, target, index))

    kind = lax.broadcasted_iota(jnp.int32, (128, rows_total), 0)
    kinds = jnp.where(kind == seg_over[...], 1.0, 0.0).astype(jnp.bfloat16)
    for b in range(2):
        lanes = slice(b * half, (b + 1) * half)
        mask_bias[:, lanes] = jnp.where(tn_dot(kinds, kinds[:, lanes]) > 0.5, 0.0, -1e30)

    joint_slots = {}

    def at_slot(index, table):
        for slot, todo in table.items():

            @pl.when(index == slot)
            def _(todo=todo):
                for event in todo:
                    event()

    def joint_step(j, carry):
        cols = pl.ds(pl.multiple_of(j * 256, 256), 256)
        joint[:, cols] = (nn_dot(tokens[...], joint_proj[:, cols]) + joint_bias[:, cols]).astype(
            jnp.bfloat16
        )
        at_slot(j, joint_slots)
        return carry

    lax.fori_loop(0, 3 * width // 256, joint_step, 0)
    save(joint, joint_out, 0)
    bias_event(1)
    slots = (
        {2: [lambda: inner.x_event(0, False), lambda: outer.z_event(0), lambda: outer.y_event(None)], 3: [lambda: inner.z_event(1), lambda: inner.y_event(0)], 4: [lambda: outer.x_event(None, True), lambda: outer.z_event(1), lambda: outer.y_event(0)], 5: [lambda: inner.x_event(0, True)]},
        {0: [lambda: inner.z_event(0), lambda: inner.y_event(None)], 2: [lambda: inner.x_event(None, True)], 3: [lambda: outer.x_event(0, False)], 4: [lambda: inner.x_event(1, False)], 5: [lambda: inner.z_event(2), lambda: inner.y_event(1), lambda: outer.x_event(1, False)]},
    )
    for p, step in ((0, 2), (2, 3), (4, 4)):
        slots[1].setdefault(p, []).append(lambda step=step: bias_event(step))
    first_half = (lax.broadcasted_iota(jnp.int32, (1, 128), 1) < DH).astype(jnp.bfloat16)
    halves = (first_half, 1 - first_half)
    factor = 1.4426950408889634 / math.sqrt(DH)
    pairs = HEADS // 2

    def pair_step(p, carry):
        cols = [pl.ds(pl.multiple_of(s * width + p * 128, 128), 128) for s in range(3)]
        out_cols = pl.ds(pl.multiple_of(p * 128, 128), 128)
        keys, values = joint[:, cols[1]], joint[:, cols[2]]
        for b in range(2):
            lanes = slice(b * half, (b + 1) * half)
            queries = joint[lanes, cols[0]]
            total = None
            for a in range(2):
                scores = nt_dot(keys * halves[a], queries) * factor + mask_bias[:, lanes]
                weights = jnp.exp2(scores - jnp.max(scores, axis=0, keepdims=True))
                weights = weights * (1.0 / jnp.sum(weights, axis=0, keepdims=True))
                low = weights.astype(jnp.bfloat16)
                probs[2 * p + a, :, lanes] = low
                part = tn_dot(low, values * halves[a])
                total = part if total is None else total + part
            context[lanes, out_cols] = (
                total * first_lanes(128, p * 128, kept_of(widths, place, side, 1) * DH)
            ).astype(jnp.bfloat16)
            if b == 0:
                at_slot(p, slots[0])
        pltpu.make_async_copy(
            probs.at[pl.ds(2 * p, 2)], probs_out.at[pl.ds(2 * p, 2)], save_sem.at[6 + p]
        ).start()
        at_slot(p, slots[1])
        return carry

    lax.fori_loop(0, pairs, pair_step, 0)
    save(context, context_out, 1)
    for j in range(width // 256):
        cols = slice(j * 256, (j + 1) * 256)
        wide[:, cols] = nn_dot(context[...], out_proj[:, cols])

    def first_norm(i, carry):
        rows = pl.ds(pl.multiple_of(i * 128, 128), 128)
        total = tokens[rows, :].astype(jnp.float32) + (wide[rows, :] + out_bias)
        centred = total - jnp.mean(total, axis=-1, keepdims=True)
        scale = lax.rsqrt(jnp.mean(centred * centred, axis=-1, keepdims=True) + 1e-12)
        normed = centred * scale
        normed_out[rows, :] = normed
        scale_out[rows, :] = scale
        first_low[rows, :] = (normed * first_gain + first_shift).astype(jnp.bfloat16)
        return carry

    lax.fori_loop(0, rows_total // 128, first_norm, 0)
    outer.x_event(0, True)
    outer.z_event(2)
    outer.y_event(1)
    inner.x_event(2, False)
    inner.x_event(1, True)
    inner.y_event(2)
    outer.x_event(2, False)
    outer.x_event(1, True)
    outer.y_event(2)
    inner.x_event(2, True)
    for q in range(units // (2 * share)):
        inner_bias[:, q * 2 * share : (q + 1) * 2 * share] = (
            bias_all[2 * q, 0:1, :] + bias_all[2 * q + 1, 0:1, :]
        )
    inner.finish()
    save(inner_all, inner_out, 2)
    unit_slots = {1: [lambda: outer.x_event(2, True)]}

    def unit_step(j, carry):
        cols = pl.ds(pl.multiple_of(j * 256, 256), 256)
        for b in range(2):
            rows = slice(b * half, (b + 1) * half)
            pre = nt_dot(first_low[rows, :], inner_all[cols, :]) + inner_bias[:, cols]
            gate = 0.5 + 0.5 * lax.erf(pre * 0.7071067811865476)
            on = first_lanes(256, j * 256, kept_units)
            act[rows, cols] = (pre * gate * on).astype(jnp.bfloat16)
            slope[rows, cols] = (
                (gate + pre * jnp.exp(-0.5 * pre * pre) * 0.3989422804014327) * on
            ).astype(jnp.bfloat16)
        for slot, todo in unit_slots.items():

            @pl.when(j == slot)
            def _(todo=todo):
                for event in todo:
                    event()

        return carry

    lax.fori_loop(0, units // 256, unit_step, 0)
    save(act, act_out, 3)
    save(slope, slope_out, 4)
    outer.finish()
    save(outer_all, outer_out, 5)
    for j in range(width // 256):
        cols = slice(j * 256, (j + 1) * 256)
        wide[:, cols] = nn_dot(act[...], outer_all[:, cols])
    small_out[...] = jnp.zeros_like(small_out)

    def second_norm(i, carry):
        rows = pl.ds(pl.multiple_of(i * 128, 128), 128)
        first = normed_out[rows, :] * first_gain + first_shift
        total = first + (wide[rows, :] + outer_bias)
        centred = total - jnp.mean(total, axis=-1, keepdims=True)
        scale = lax.rsqrt(jnp.mean(centred * centred, axis=-1, keepdims=True) + 1e-12)
        normed = centred * scale
        second = normed * second_gain + second_shift
        wide[rows, :] = second
        output[rows, :] = second.astype(jnp.bfloat16)
        grad = out_grad[rows, :].astype(jnp.float32)
        scaled = grad * second_gain
        back = scale * (
            scaled
            - jnp.mean(scaled, axis=-1, keepdims=True)
            - normed * jnp.mean(scaled * normed, axis=-1, keepdims=True)
        )
        sum_grad_out[rows, :] = back
        low = back.astype(jnp.bfloat16).astype(jnp.float32)
        small_out[0:1, :] += jnp.sum(grad * normed, axis=0, keepdims=True)
        small_out[1:2, :] += jnp.sum(grad, axis=0, keepdims=True)
        small_out[2:3, :] += jnp.sum(low, axis=0, keepdims=True)
        return carry

    lax.fori_loop(0, rows_total // 128, second_norm, 0)
    for j in range(SEGS):
        cls_out[j : j + 1, :] = wide[pl.ds(cls_at[0, j], 1), :]
    inner.drain()
    outer.drain()
    for step in range(4):
        bias_hop(step).wait_send()
    for source, target, index in saves:
        pltpu.make_async_copy(source, target, save_sem.at[index]).wait()
    for p in range(pairs):
        pltpu.make_async_copy(
            probs.at[pl.ds(2 * p, 2)], probs_out.at[pl.ds(2 * p, 2)], save_sem.at[6 + p]
        ).wait()


def run_forward(args, share, units, rows_total, width):
    sems = []
    for unused in range(2):
        for count in (3, 3, 3, 3, 4, 4, 8, 8, 8, 8, 8, 8):
            sems.append(pltpu.SemaphoreType.DMA((count,)))
    bf, fp = jnp.bfloat16, jnp.float32
    shape = jax.ShapeDtypeStruct
    vmem = pl.BlockSpec(memory_space=pltpu.VMEM)
    anywhere = pl.BlockSpec(memory_space=pl.ANY)
    smem = pl.BlockSpec(memory_space=pltpu.SMEM)
    in_specs = [vmem] * 15 + [smem, smem, vmem]
    return pl.pallas_call(
        forward_kernel,
        out_shape=(
            shape((rows_total, width), bf),
            shape((SEGS, width), fp),
            shape((units, width), bf),
            shape((units, width), bf),
            shape((HEADS, rows_total, rows_total), bf),
            shape((rows_total, 3 * width), bf),
            shape((rows_total, width), bf),
            shape((rows_total, width), fp),
            shape((rows_total, 1), fp),
            shape((rows_total, units), bf),
            shape((rows_total, units), bf),
            shape((rows_total, width), fp),
            shape((16, width), fp),
        ),
        in_specs=in_specs,
        out_specs=(
            vmem, vmem, anywhere, anywhere, anywhere, anywhere, anywhere, vmem, vmem, anywhere, anywhere, vmem, vmem,
        ),
        scratch_shapes=[
            pltpu.VMEM((units, width), bf),
            pltpu.VMEM((units, width), bf),
            pltpu.VMEM((HEADS, rows_total, rows_total), bf),
            pltpu.VMEM((rows_total, 3 * width), bf),
            pltpu.VMEM((rows_total, width), bf),
            pltpu.VMEM((rows_total, rows_total), fp),
            pltpu.VMEM((rows_total, units), bf),
            pltpu.VMEM((rows_total, units), bf),
            pltpu.VMEM((rows_total, width), bf),
            pltpu.VMEM((rows_total, width), fp),
            pltpu.VMEM((units // share, 8, 2 * share), fp),
            pltpu.VMEM((1, units), fp),
            pltpu.VMEM((1, 3 * width), fp),
            pltpu.SemaphoreType.DMA((7 + HEADS // 2,)),
            pltpu.SemaphoreType.DMA((4,)),
            pltpu.SemaphoreType.DMA((4,)),
        ]
        + sems,
        compiler_params=pltpu.CompilerParams(
            collective_id=0, has_side_effects=True, vmem_limit_bytes=64 * 1024 * 1024 - 65536
        ),
        name="forward",
    )(*args)


def backward_kernel(
    act_in,
    slope_in,
    sum_grad_in,
    outer_in,
    inner_in,
    normed_in,
    joint_in,
    context_in,
    probs_in,
    tokens_in,
    joint_proj_in,
    out_proj_in,
    scale,
    small_in,
    first_gain,
    first_shift,
    widths,
    input_grad,
    out_sum,
    joint_sum,
    outer_grad,
    inner_grad,
    small_out,
    act,
    slope,
    weight,
    probs,
    joint,
    context,
    normed,
    grad,
    tokens,
    tokens_over,
    out_proj,
    low,
    first_low,
    sums,
    far_c,
    far_x,
    far_y,
    far_z,
    far_v,
    far_w,
    own,
    far_u,
    parts,
    part_c,
    part_a,
    part_b,
    part_z,
    joint_grad,
    context_grad,
    small,
    small_far,
    load_sem,
    probs_sem,
    keep_sem,
    *sems,
):
    place, side = lax.axis_index("ffn"), lax.axis_index("tok")
    core, flank, deep = place % 2, (place // 2) % 2, place // 4
    first_gain, first_shift = row_of(first_gain), row_of(first_shift)
    kept_lanes = kept_of(widths, place, side, 1) * DH
    rows_total, units = act.shape
    width = grad.shape[1]
    half = rows_total // 2
    share = own.shape[1]
    bf, fp = jnp.bfloat16, jnp.float32
    sem_names = (
        "c", "x", "y", "z", "v", "w", "f", "u", "ac", "aa", "ab", "az", "gz", "gb", "ga", "gc", "bt"
    )
    send = dict(zip(sem_names, sems[: len(sem_names)]))
    recv = dict(zip(sem_names, sems[len(sem_names) :]))
    made = {}

    def define(name, index, source, target, device):
        made[(name,) + index] = lambda: remote(
            source(), target(), send[name].at[index], recv[name].at[index], device
        )

    def go(name, *index):
        made[(name,) + index]().start()

    def got(name, *index):
        made[(name,) + index]().wait_recv()

    peer_x, peer_y, peer_c = (place, 1 - side), (y_peer(place), side), (c_peer(place), side)
    peer_z = [None] + [(z_peer(place, turn), side) for turn in (1, 2, 3)]
    deep_of = [z_peer(place, turn) // 4 if turn else deep for turn in range(4)]
    third = share // 2

    def shard(turn, y, c, offset=0, count=None):
        start = ((deep_of[turn] * 2 + y) * 2 + c) * share + offset
        return pl.ds(pl.multiple_of(start, 16), share if count is None else count)

    left, right = slice(0, width // 2), slice(width // 2, width)
    own_part = pl.ds(pl.multiple_of(side * third, 16), third)

    def half_shard(t, y, offset):
        return shard(t, y, core, offset * third, third)

    for m in range(2):
        for t in range(4):
            for y in range(2):
                define(
                    "c", (m, t, y), lambda m=m, t=t, y=y: sums.at[m, shard(t, y, 1 - core)], lambda m=m, t=t, y=y: far_c.at[m, t, y], peer_c
                )
                define(
                    "x", (m, t, y), lambda m=m, t=t, y=y: sums.at[m, half_shard(t, y, 1 - side), left], lambda m=m, t=t, y=y: far_x.at[m, t, y], peer_x
                )
            define(
                "y", (m, t), lambda m=m, t=t: sums.at[m, half_shard(t, 1 - flank, side), left], lambda m=m, t=t: far_y.at[m, t], peer_y
            )
            define(
                "v", (m, t), lambda m=m, t=t: sums.at[m, shard(t, 1 - flank, core), right], lambda m=m, t=t: far_v.at[m, t], peer_y
            )
            if t:
                define(
                    "z", (m, t - 1), lambda m=m, t=t: sums.at[m, half_shard(t, flank, side), left], lambda m=m, t=t: far_z.at[m, t - 1], peer_z[t]
                )
                define(
                    "w", (m, t - 1), lambda m=m, t=t: sums.at[m, shard(t, flank, core), right], lambda m=m, t=t: far_w.at[m, t - 1], peer_z[t]
                )
        define("f", (m,), lambda m=m: own.at[m, own_part, left], lambda m=m: own.at[m, own_part, left], peer_x)
        define("u", (m,), lambda m=m: own.at[m, :, right], lambda m=m: far_u.at[m], peer_x)
    grads = (outer_grad, inner_grad)

    def add(target, source):
        target[...] = (target[...].astype(fp) + source[...].astype(fp)).astype(bf)

    def to_xy(m, t):
        for y in range(2):
            got("c", m, t, y)
            add(sums.at[m, shard(t, y, core)], far_c.at[m, t, y])
            go("x", m, t, y)
        go("v", m, t)

    def x_to_y(m, t):
        for y in range(2):
            got("x", m, t, y)
            add(sums.at[m, half_shard(t, y, side), left], far_x.at[m, t, y])
        go("y", m, t)

    def y_to_z(m, t):
        got("y", m, t)
        add(sums.at[m, half_shard(t, flank, side), left], far_y.at[m, t])
        if t:
            go("z", m, t - 1)

    def v_to_w(m, t):
        got("v", m, t)
        add(sums.at[m, shard(t, flank, core), right], far_v.at[m, t])
        if t:
            go("w", m, t - 1)

    def z_end(m):
        total = sums[m, half_shard(0, flank, side), left].astype(fp)
        for t in range(3):
            got("z", m, t)
            total = total + far_z[m, t].astype(fp)
        own[m, own_part, left] = total.astype(bf)
        go("f", m)

    def w_end(m):
        total = sums[m, shard(0, flank, core), right].astype(fp)
        for t in range(3):
            got("w", m, t)
            total = total + far_w[m, t].astype(fp)
        own[m, :, right] = total.astype(bf)
        go("u", m)

    def f_last(m):
        got("f", m)
        grads[m][:, left] = own[m, :, left].astype(fp)

    def u_last(m):
        got("u", m)
        grads[m][:, right] = own[m, :, right].astype(fp) + far_u[m].astype(fp)

    quarter = width // 2

    wide_piece = 2 * quarter // 3
    pieces = []
    for j in range(4):
        pieces.append((j, 0, wide_piece, j % 2))
        pieces.append((j, wide_piece, quarter - wide_piece, 1 - j % 2))

    def cols_of(q, c):
        start = c * quarter + pieces[q][1]
        return pl.ds(pl.multiple_of(start, 128), pieces[q][2])

    def span(q):
        return slice(pieces[q][1], pieces[q][1] + pieces[q][2])

    def rows_of(q, depth, flips=(0, 0), z=None):
        first, second = (flank, side) if pieces[q][3] else (side, flank)
        if flips[0]:
            first = 1 - first
        if flips[1]:
            second = 1 - second
        if depth == 0:
            return pl.ds(0, width)
        start, count = first * (width // 2), width // 2
        if depth > 1:
            start, count = start + second * (width // 4), width // 4
        if depth > 2:
            start, count = start + (deep if z is None else z) * (width // 16), width // 16
        return pl.ds(pl.multiple_of(start, 16), count)

    def region(q, depth, flips=(0, 0), z=None, c=None):
        return (pieces[q][0], rows_of(q, depth, flips, z), cols_of(q, core if c is None else c))

    def landing(q, depth, flips=(0, 0), z=None, c=None):
        j, offset, count, kind = pieces[q]
        c = core if c is None else c
        if j == 0:
            return out_sum.at[rows_of(q, depth, flips, z), cols_of(q, c)]
        start = (j - 1) * 256 + (width + c * 128 if offset else c * 2 * width)
        return joint_sum.at[rows_of(q, depth, flips, z), pl.ds(pl.multiple_of(start, 128), count)]

    for q, piece in enumerate(pieces):
        j = piece[0]
        near, far = (peer_y, peer_x) if piece[3] else (peer_x, peer_y)
        define("ac", (q,), lambda q=q: parts.at[region(q, 0, c=1 - core)], lambda q=q, j=j: part_c.at[j, :, span(q)], peer_c)
        define("aa", (q,), lambda q=q: parts.at[region(q, 1, (1, 0))], lambda q=q, j=j: part_a.at[j, :, span(q)], near)
        define("ab", (q,), lambda q=q: parts.at[region(q, 2, (0, 1))], lambda q=q, j=j: part_b.at[j, :, span(q)], far)
        for t in (1, 2, 3):
            define(
                "az",
                (q, t - 1),
                lambda q=q, t=t: parts.at[region(q, 3, z=deep_of[t])],
                lambda q=q, j=j, t=t: part_z.at[j, t - 1, :, span(q)],
                peer_z[t],
            )
            define(
                "gz",
                (q, t - 1),
                lambda q=q: parts.at[region(q, 3)],
                lambda q=q: landing(q, 3),
                peer_z[t],
            )

        def place_of(depth, q=q):
            return lambda: landing(q, depth)

        define("gb", (q,), place_of(2), place_of(2), far)
        define("ga", (q,), place_of(1), place_of(1), near)
        define("gc", (q,), place_of(0), place_of(0), peer_c)

    def keep(q):
        return pltpu.make_async_copy(parts.at[region(q, 3)], landing(q, 3), keep_sem.at[q])

    def sum_1(q):
        got("ac", q)
        add(parts.at[region(q, 0)], part_c.at[pieces[q][0], :, span(q)])
        go("aa", q)

    def sum_2(q):
        got("aa", q)
        add(parts.at[region(q, 1)], part_a.at[pieces[q][0], :, span(q)])
        go("ab", q)

    def sum_3(q):
        got("ab", q)
        add(parts.at[region(q, 2)], part_b.at[pieces[q][0], :, span(q)])
        for t in range(3):
            go("az", q, t)

    def sum_4(q):
        total = parts[region(q, 3)].astype(fp)
        for t in range(3):
            got("az", q, t)
            total = total + part_z[pieces[q][0], t, :, span(q)].astype(fp)
        parts[region(q, 3)] = total.astype(bf)
        for t in range(3):
            go("gz", q, t)
        keep(q).start()

    def sum_5(q):
        keep(q).wait()
        for t in range(3):
            landed = landing(q, 3, z=deep_of[t + 1])
            remote(landed, landed, send["gz"].at[q, t], recv["gz"].at[q, t], peer_z[t + 1]).wait_recv()
        go("gb", q)

    def arrive(name, q, depth, flips, c=None):
        piece = landing(q, depth, flips, c=c)
        remote(piece, piece, send[name].at[q], recv[name].at[q], peer_x).wait_recv()

    def sum_6(q):
        arrive("gb", q, 2, (0, 1))
        go("ga", q)

    def sum_7(q):
        arrive("ga", q, 1, (1, 0))
        go("gc", q)

    def sum_8(q):
        arrive("gc", q, 0, (0, 0), 1 - core)

    ring = (peer_c, peer_x, peer_y, peer_z[1], peer_z[2])
    for i, peer in enumerate(ring):
        define("bt", (i,), lambda i=i: small.at[i], lambda i=i: small_far.at[i], peer)

    def small_step(i):
        got("bt", i)
        if i < 4:
            small[i + 1] = small[i] + small_far[i]
            go("bt", i + 1)
        else:
            small_out[...] = small[i] + small_far[i]

    loads = [
        (sum_grad_in, grad),
        (act_in, act),
        (outer_in, weight),
        (slope_in, slope),
        (normed_in, normed),
        (context_in, context),
        (out_proj_in, out_proj),
        (tokens_in, tokens),
        (joint_in, joint),
        (inner_in, weight),
    ]
    for s in range(3):
        block = slice(s * width, (s + 1) * width)
        loads.append((joint_proj_in.at[:, block], weight.at[block]))

    def load(i):
        return pltpu.make_async_copy(loads[i][0], loads[i][1], load_sem.at[i])

    def fetch(p):
        return pltpu.make_async_copy(
            probs_in.at[pl.ds(2 * p, 2)], probs.at[p % 2], probs_sem.at[p % 2]
        )

    for i in range(9):
        load(i).start()
    fetch(0).start()
    greet(place, side)
    small[0] = small_in[...]
    load(0).wait()
    low[...] = grad[...].astype(bf)
    load(1).wait()

    def at_slot(index, table):
        for slot, todo in table.items():

            @pl.when(index == slot)
            def _(todo=todo):
                for event in todo:
                    event()

    def outer_group(t, table):
        base = deep_of[t] * (4 * share)

        def body(i, carry):
            here = pl.ds(pl.multiple_of(base + i * 256, 256), 256)
            sums[0, here, :] = tn_dot(act[:, here], low[...]).astype(bf)
            at_slot(i, table)
            return carry

        lax.fori_loop(0, 4 * share // 256, body, 0)
        for y in range(2):
            go("c", 0, t, y)

    def inner_group(t):
        base = deep_of[t] * (4 * share)

        def body(i, carry):
            here = pl.ds(pl.multiple_of(base + i * 256, 256), 256)
            sums[1, here, :] = tn_dot(act[:, here], first_low[...]).astype(bf)
            return carry

        lax.fori_loop(0, 4 * share // 256, body, 0)
        for y in range(2):
            go("c", 1, t, y)

    outer_group(3, {})
    outer_group(2, {})
    outer_group(1, {})
    outer_group(0, {})
    to_xy(0, 3)
    load(2).wait()
    load(3).wait()
    pre_slots = {0: [lambda: to_xy(0, 2)], 2: [lambda: to_xy(0, 1)], 3: [lambda: to_xy(0, 0)], 4: [lambda: x_to_y(0, 3), lambda: v_to_w(0, 3)], 8: [lambda: x_to_y(0, 2), lambda: v_to_w(0, 2)]}

    def pre_step(j, carry):
        cols = pl.ds(pl.multiple_of(j * 256, 256), 256)
        for b in range(2):
            rows = slice(b * half, (b + 1) * half)
            back = nt_dot(low[rows, :], weight[cols, :])
            act[rows, cols] = (back * slope[rows, cols].astype(fp)).astype(bf)
        bias_cols = pl.ds(pl.multiple_of((j % 3) * 256, 256), 256)
        small[0, pl.ds(8 + j // 3, 1), bias_cols] = jnp.sum(
            act[:, cols].astype(fp), axis=0, keepdims=True
        )
        at_slot(j, pre_slots)
        return carry

    lax.fori_loop(0, units // 256, pre_step, 0)
    load(9).start()
    load(4).wait()

    def first_step(i, carry):
        rows = pl.ds(pl.multiple_of(i * 128, 128), 128)
        first_low[rows, :] = (normed[rows, :] * first_gain + first_shift).astype(bf)
        return carry

    lax.fori_loop(0, rows_total // 128, first_step, 0)
    x_to_y(0, 1)
    v_to_w(0, 1)
    inner_group(3)
    load(9).wait()
    back_slots = {0: [lambda: x_to_y(0, 0), lambda: v_to_w(0, 0)], 1: [lambda: y_to_z(0, 3), lambda: to_xy(1, 3)], 2: [lambda: y_to_z(0, 2)]}
    for j in range(width // 256):
        cols = slice(j * 256, (j + 1) * 256)
        grad[:, cols] += nn_dot(act[...], weight[:, cols])
        for event in back_slots.get(j, []):
            event()

    for i in range(10, 13):
        load(i).start()

    def norm_step(i, carry):
        rows = pl.ds(pl.multiple_of(i * 128, 128), 128)
        incoming, unit = grad[rows, :], normed[rows, :]
        small[0, 3:4, :] += jnp.sum(incoming * unit, axis=0, keepdims=True)
        small[0, 4:5, :] += jnp.sum(incoming, axis=0, keepdims=True)
        scaled = incoming * first_gain
        back = scale[rows, :] * (
            scaled
            - jnp.mean(scaled, axis=-1, keepdims=True)
            - unit * jnp.mean(scaled * unit, axis=-1, keepdims=True)
        )
        grad[rows, :] = back
        back_low = back.astype(bf)
        low[rows, :] = back_low
        small[0, 5:6, :] += jnp.sum(back_low.astype(fp), axis=0, keepdims=True)
        return carry

    lax.fori_loop(0, rows_total // 128, norm_step, 0)
    y_to_z(0, 1)
    w_end(0)
    inner_group(2)
    y_to_z(0, 0)
    load(5).wait()
    out_slots = {0: [lambda: x_to_y(1, 3)], 2: [lambda: go("ac", 0), lambda: go("ac", 1)]}
    for j in range(width // 256):
        cols = slice(j * 256, (j + 1) * 256)
        parts[0, cols, :] = tn_dot(context[:, cols], low[...]).astype(bf)
        for event in out_slots.get(j, []):
            event()
    load(6).wait()
    context_slots = {0: [lambda: v_to_w(1, 3)], 1: [lambda: to_xy(1, 2), lambda: u_last(0), lambda: y_to_z(1, 3)], 2: [lambda: z_end(0), lambda: sum_1(0), lambda: sum_1(1)]}
    for j in range(width // 256):
        cols = slice(j * 256, (j + 1) * 256)
        context_grad[:, cols] = (
            nt_dot(low[...], out_proj[cols, :]) * first_lanes(256, j * 256, kept_lanes)
        ).astype(bf)
        for event in context_slots.get(j, []):
            event()
    load(7).wait()
    for j in range(width // 128):
        cols = slice(j * 128, (j + 1) * 128)
        tokens_over[cols, :] = tokens[:, cols].T

    load(8).wait()
    first_half = (lax.broadcasted_iota(jnp.int32, (1, 128), 1) < DH).astype(bf)
    halves = (first_half, 1 - first_half)
    factor = 1.0 / math.sqrt(DH)
    pairs = HEADS // 2
    pair_slots = (
        {1: [lambda: sum_2(1)], 2: [lambda: sum_3(1)], 4: [lambda: sum_1(4), lambda: sum_1(5)], 5: [lambda: sum_3(3)]},
        {0: [lambda: x_to_y(1, 2), lambda: v_to_w(1, 2), lambda: inner_group(1), lambda: f_last(0)], 1: [lambda: go("ac", 2), lambda: go("ac", 3), lambda: y_to_z(1, 2), lambda: to_xy(1, 1), lambda: sum_2(0)], 2: [lambda: sum_1(2), lambda: sum_1(3)], 3: [lambda: go("ac", 4), lambda: go("ac", 5), lambda: x_to_y(1, 1), lambda: v_to_w(1, 1), lambda: inner_group(0), lambda: sum_3(0), lambda: sum_2(3)], 4: [lambda: to_xy(1, 0), lambda: sum_4(1), lambda: sum_2(2), lambda: y_to_z(1, 1)], 5: [lambda: go("ac", 6), lambda: go("ac", 7), lambda: sum_4(0), lambda: sum_2(5), lambda: sum_2(4)]},
    )

    def pair_step(p, carry):
        @pl.when(p + 1 < pairs)
        def _():
            fetch(p + 1).start()

        fetch(p).wait()
        slot = p % 2
        cols = [pl.ds(pl.multiple_of(s * width + p * 128, 128), 128) for s in range(3)]
        out_cols = pl.ds(pl.multiple_of(p * 128, 128), 128)
        keys, values = joint[:, cols[1]], joint[:, cols[2]]
        value_part, key_part = None, None
        for b in range(2):
            lanes = slice(b * half, (b + 1) * half)
            queries, incoming = joint[lanes, cols[0]], context_grad[lanes, out_cols]
            query_part = None
            for a in range(2):
                weights_low = probs[slot, a, :, lanes]
                weights = weights_low.astype(fp)
                product = nt_dot(values * halves[a], incoming) * weights
                score_grad = (
                    product - weights * jnp.sum(product, axis=0, keepdims=True)
                ).astype(bf)
                part = nn_dot(weights_low, incoming * halves[a])
                value_part = part if value_part is None else value_part + part
                part = nn_dot(score_grad, queries * halves[a])
                key_part = part if key_part is None else key_part + part
                part = tn_dot(score_grad, keys * halves[a])
                query_part = part if query_part is None else query_part + part
            joint_grad[lanes, cols[0]] = (query_part * factor).astype(bf)
        joint_grad[:, cols[1]] = (key_part * factor).astype(bf)
        joint_grad[:, cols[2]] = value_part.astype(bf)
        small[0, 6:7, out_cols] = jnp.sum(
            joint_grad[:, cols[0]].astype(fp), axis=0, keepdims=True
        )
        small[0, 7:8, out_cols] = jnp.sum(
            joint_grad[:, cols[2]].astype(fp), axis=0, keepdims=True
        )
        at_slot(p, pair_slots[0])

        @pl.when(p % 2 == 1)
        def _():
            index = (p + 1) // 2
            for s in range(3):
                source = pl.ds(pl.multiple_of(s * width + (index - 1) * 256, 256), 256)
                block = nn_dot(tokens_over[...], joint_grad[:, source]).astype(bf)
                if s == 1:
                    parts[index, :, 256:384] = block[:, :128]
                    parts[index, :, 640:768] = block[:, 128:]
                else:
                    parts[index, :, s * 192 : s * 192 + 256] = block

        at_slot(p, pair_slots[1])
        return carry

    lax.fori_loop(0, pairs, pair_step, 0)
    for i in range(10, 13):
        load(i).wait()
    last_slots = {0: [lambda: go("bt", 0), lambda: sum_5(1)], 2: [lambda: v_to_w(1, 0), lambda: w_end(1), lambda: x_to_y(1, 0), lambda: sum_1(6), lambda: small_step(0), lambda: sum_1(7), lambda: sum_4(3), lambda: sum_3(4), lambda: sum_3(2)]}
    for j in range(width // 256):
        cols = slice(j * 256, (j + 1) * 256)
        total = grad[:, cols]
        for s in range(3):
            block = slice(s * width, (s + 1) * width)
            rows = slice(s * width + j * 256, s * width + (j + 1) * 256)
            total = total + nt_dot(joint_grad[:, block], weight[rows, :])
        grad[:, cols] = total
        if j == 2:
            pltpu.make_async_copy(grad, input_grad, keep_sem.at[8]).start()
        for event in last_slots.get(j, []):
            event()
    sum_3(5)
    y_to_z(1, 0)
    z_end(1)
    sum_6(1)
    sum_5(0)
    sum_5(3)
    u_last(1)
    small_step(1)
    sum_2(6)
    sum_2(7)
    sum_7(1)
    sum_4(4)
    f_last(1)
    sum_6(0)
    sum_8(1)
    sum_6(3)
    sum_3(6)
    small_step(2)
    sum_4(2)
    sum_3(7)
    sum_4(5)
    sum_7(0)
    sum_7(3)
    sum_8(0)
    sum_5(4)
    sum_8(3)
    sum_6(4)
    sum_4(6)
    small_step(3)
    sum_5(2)
    sum_7(4)
    sum_4(7)
    sum_8(4)
    sum_6(2)
    sum_5(5)
    sum_6(5)
    sum_5(6)
    small_step(4)
    sum_7(2)
    sum_5(7)
    sum_7(5)
    sum_6(6)
    sum_8(2)
    sum_8(5)
    sum_6(7)
    sum_7(7)
    sum_7(6)
    sum_8(7)
    sum_8(6)
    result = pltpu.make_async_copy(grad, input_grad, keep_sem.at[8])
    result.wait()
    for build in made.values():
        build().wait_send()


def run_backward(args, share, units, rows_total, width):
    bf, fp = jnp.bfloat16, jnp.float32
    shape = jax.ShapeDtypeStruct
    vmem = pl.BlockSpec(memory_space=pltpu.VMEM)
    anywhere = pl.BlockSpec(memory_space=pl.ANY)
    third = share // 2
    counts = [
        (2, 4, 2), (2, 4, 2), (2, 4), (2, 3), (2, 4), (2, 3), (2,), (2,),
        (8,), (8,), (8,), (8, 3), (8, 3), (8,), (8,), (8,), (5,),
    ]
    sems = [pltpu.SemaphoreType.DMA(count) for unused in range(2) for count in counts]
    quarter = width // 2
    return pl.pallas_call(
        backward_kernel,
        out_shape=(
            shape((rows_total, width), fp),
            shape((width, width), bf),
            shape((width, 3 * width), bf),
            shape((share, width), fp),
            shape((share, width), fp),
            shape((16, width), fp),
        ),
        in_specs=[anywhere] * 12 + [vmem] * 4 + [pl.BlockSpec(memory_space=pltpu.SMEM)],
        out_specs=(anywhere, anywhere, anywhere, vmem, vmem, vmem),
        scratch_shapes=[
            pltpu.VMEM((rows_total, units), bf),
            pltpu.VMEM((rows_total, units), bf),
            pltpu.VMEM((units, width), bf),
            pltpu.VMEM((2, 2, rows_total, rows_total), bf),
            pltpu.VMEM((rows_total, 3 * width), bf),
            pltpu.VMEM((rows_total, width), bf),
            pltpu.VMEM((rows_total, width), fp),
            pltpu.VMEM((rows_total, width), fp),
            pltpu.VMEM((rows_total, width), bf),
            pltpu.VMEM((width, rows_total), bf),
            pltpu.VMEM((width, width), bf),
            pltpu.VMEM((rows_total, width), bf),
            pltpu.VMEM((rows_total, width), bf),
            pltpu.VMEM((2, units, width), bf),
            pltpu.VMEM((2, 4, 2, share, width), bf),
            pltpu.VMEM((2, 4, 2, third, quarter), bf),
            pltpu.VMEM((2, 4, third, quarter), bf),
            pltpu.VMEM((2, 3, third, quarter), bf),
            pltpu.VMEM((2, 4, share, quarter), bf),
            pltpu.VMEM((2, 3, share, quarter), bf),
            pltpu.VMEM((2, share, width), bf),
            pltpu.VMEM((2, share, quarter), bf),
            pltpu.VMEM((4, width, width), bf),
            pltpu.VMEM((4, width, quarter), bf),
            pltpu.VMEM((4, width // 2, quarter), bf),
            pltpu.VMEM((4, width // 4, quarter), bf),
            pltpu.VMEM((4, 3, width // 16, quarter), bf),
            pltpu.VMEM((rows_total, 3 * width), bf),
            pltpu.VMEM((rows_total, width), bf),
            pltpu.VMEM((5, 16, width), fp),
            pltpu.VMEM((5, 16, width), fp),
            pltpu.SemaphoreType.DMA((13,)),
            pltpu.SemaphoreType.DMA((2,)),
            pltpu.SemaphoreType.DMA((9,)),
        ]
        + sems,
        compiler_params=pltpu.CompilerParams(
            collective_id=1, has_side_effects=True, vmem_limit_bytes=64 * 1024 * 1024 - 65536
        ),
        name="backward",
    )(*args)


def on_device_fast(
    tokens,
    joint_proj,
    query_bias,
    value_bias,
    out_proj,
    out_bias,
    first_gain,
    first_shift,
    inner_proj,
    inner_bias,
    outer_proj,
    outer_bias,
    second_gain,
    second_shift,
    segment_ids,
    cls_positions,
    widths,
    out_grad,
):
    tok_rows, model_width = tokens.shape
    unit_share = inner_proj.shape[1]
    ffn_count = lax.axis_size("ffn")
    ffn_place = lax.axis_index("ffn")
    unit_total = unit_share * ffn_count
    shifted = jnp.arange(2 * unit_share, dtype=jnp.int32) // unit_share == ffn_place % 2
    bias_block = jnp.where(shifted, jnp.tile(inner_bias, 2).astype(jnp.float32), 0.0)
    bias_block = jnp.broadcast_to(bias_block, (8, 2 * unit_share))
    (
        output, cls_states, inner_rows, outer_rows, probs_again, joint_flat, context_low,
        first_normed, first_scale, act_low, slope_low, sum_grad, small_a,
    ) = run_forward(
        (
            tokens, joint_proj, query_bias, value_bias, out_proj, out_bias, first_gain, first_shift,
            inner_proj.T, outer_proj, bias_block, outer_bias, second_gain, second_shift,
            segment_ids[None], widths, cls_positions, out_grad,
        ),
        unit_share, unit_total, tok_rows, model_width,
    )
    input_grad, out_summed, joint_summed, outer_part, inner_part, small = run_backward(
        (
            act_low, slope_low, sum_grad, outer_rows, inner_rows, first_normed, joint_flat,
            context_low, probs_again, tokens, joint_proj, out_proj, first_scale, small_a,
            first_gain, first_shift, widths,
        ),
        unit_share, unit_total, tok_rows, model_width,
    )
    cls_states = cls_states[None]
    outer_proj_grad = outer_part
    inner_proj_grad = inner_part.T
    out_proj_grad = out_summed.astype(jnp.float32)
    joint_proj_grad = joint_summed.astype(jnp.float32)
    second_gain_grad, second_shift_grad, outer_bias_grad = small[0], small[1], small[2]
    first_gain_grad, first_shift_grad, out_bias_grad = small[3], small[4], small[5]
    query_bias_grad, value_bias_grad = small[6], small[7]
    inner_bias_grad = lax.dynamic_slice(
        small[8:12].reshape(-1), (ffn_place * unit_share,), (unit_share,)
    )
    return (
        output,
        cls_states,
        input_grad,
        joint_proj_grad,
        query_bias_grad,
        value_bias_grad,
        out_proj_grad,
        out_bias_grad,
        first_gain_grad,
        first_shift_grad,
        inner_proj_grad,
        inner_bias_grad,
        outer_proj_grad,
        outer_bias_grad,
        second_gain_grad,
        second_shift_grad,
    )


def solution(mesh):
    return jax.shard_map(
        on_device_fast if mesh.shape["ffn"] == 16 and mesh.shape["tok"] == 2 else on_device,
        mesh=mesh,
        in_specs=(
            P(("ffn", "tok"), None),
            P(),
            P(),
            P(),
            P(),
            P(),
            P(),
            P(),
            P(None, "ffn"),
            P("ffn"),
            P("ffn", None),
            P(),
            P(),
            P(),
            P(("ffn", "tok")),
            P(("ffn", "tok"), None),
            P(),
            P(("ffn", "tok"), None),
        ),
        out_specs=(
            P(("ffn", "tok"), None),
            P(("ffn", "tok"), None, None),
            P(("ffn", "tok"), None),
            P(),
            P(),
            P(),
            P(),
            P(),
            P(),
            P(),
            P(None, "ffn"),
            P("ffn"),
            P("ffn", None),
            P(),
            P(),
            P(),
        ),
        check_vma=False,
    )
```
